32 devices in a mesh: seq: 8 (over z, y), batch: 4 (over x, core).
Axes of the slice: x: 2, y: 2, z: 4, core: 2. Of those that a mesh axis runs over, the one named last changes fastest.
Arguments:
- inputs: bfloat16 [56, 1024, 768], P('batch', 'seq'), may hold values from -6 to 6
- lengths: int32 [4, 14], P('batch'), may hold values from 1 to 1024, 8960 in all within a row
- pre_attention_gain: bfloat16 [768], replicated, may hold values from 0.5 to 1.5
- pre_attention_bias: bfloat16 [768], replicated, may hold values from -1 to 1
- pre_forward_gain: bfloat16 [768], replicated, may hold values from 0.5 to 1.5
- pre_forward_bias: bfloat16 [768], replicated, may hold values from -1 to 1
- query_weight: bfloat16 [768, 768], replicated, may hold values from -0.4375 to 0.4375
- query_bias: bfloat16 [768], replicated, may hold values from -1.5 to 1.5
- keyvalue_weight: bfloat16 [768, 128], replicated, may hold values from -0.21875 to 0.21875
- keyvalue_bias: bfloat16 [128], replicated, may hold values from -1.5 to 1.5
- output_weight: bfloat16 [768, 768], replicated, may hold values from -0.875 to 0.875
- output_bias: bfloat16 [768], replicated, may hold values from -1 to 1
- up_weight: bfloat16 [768, 3072], replicated, may hold values from -0.21875 to 0.21875
- up_bias: bfloat16 [3072], replicated, may hold values from -1.5 to 1.5
- down_weight: bfloat16 [3072, 768], replicated, may hold values from -0.15625 to 0.15625
- down_bias: bfloat16 [768], replicated, may hold values from -1 to 1
- out_grad: bfloat16 [56, 1024, 768], P('batch', 'seq'), may hold values from -6 to 6
- later_kv_grad: float32 [56, 1024, 128], P('batch', 'seq'), may hold values from -6 to 6
Outputs:
- layer_out: bfloat16 [56, 1024, 768], P('batch', 'seq')
- keyvalue_out: bfloat16 [56, 1024, 128], P('batch', 'seq')
- input_grad: float32 [56, 1024, 768], P('batch', 'seq')
- grad_pre_attention_gain: float32 [768], replicated
- grad_pre_attention_bias: float32 [768], replicated
- grad_pre_forward_gain: float32 [768], replicated
- grad_pre_forward_bias: float32 [768], replicated
- grad_query_weight: float32 [768, 768], P(('seq', 'batch'))
- grad_query_bias: float32 [768], replicated
- grad_keyvalue_weight: float32 [768, 128], P(('seq', 'batch'))
- grad_keyvalue_bias: float32 [128], replicated
- grad_output_weight: float32 [768, 768], P(('seq', 'batch'))
- grad_output_bias: float32 [768], replicated
- grad_up_weight: float32 [768, 3072], P(('seq', 'batch'))
- grad_up_bias: float32 [3072], replicated
- grad_down_weight: float32 [3072, 768], P(('seq', 'batch'))
- grad_down_bias: float32 [768], replicated
The draws below stay inside these ranges and needn't reach their ends.
Inputs may be any that keep to these rules, and one draw needn't show every extreme that they name: In each row the 14 live lengths sum to 8960, and some sequence of each row is 1024 long; positions from a sequence's live length on are never attended to.
All inputs are finite; a program needn't handle non-finite values.
Results may differ from the reference program's by a relative error of at most 0.013.
The reference program's roundings to bfloat16 on the way count: a program that leaves them out, or rounds other values in their place, can miss the bound.
Values may be sent and summed in bfloat16 or wider, within the bound.
No kernel may reach another device: no remote copies, remote signals or barrier semaphores. Data moves between devices by JAX's collectives and lax.ppermute only.
A program may use at most 256 MiB of HBM per device.

```python
import math
import jax
import jax.numpy as jnp
import numpy as np
from jax import lax

D = 768
HEADS = 12
HEAD_DIM = 64
FF = 3072
ROT = 16
SEQ_DEV = 14
LEN = 1024
NSEQ = 56
LIVE = 8960
N_BATCH = 4


def block_levels(own_key, extent, cuts, low, top_value):
    loudness = 1.0
    for axis_at, blocks in cuts:
        heights = jax.random.uniform(jax.random.fold_in(jax.random.fold_in(own_key, 6), axis_at), (blocks,), jnp.float32, low / len(cuts), top_value / len(cuts))
        loudness = loudness * jnp.repeat(jnp.exp(heights), extent[axis_at] // blocks).reshape((-1,) + (1,) * (len(extent) - 1 - axis_at))
    return loudness


def length_profile(amount, total, limit, skew):
    weights = [(1 << 20) // math.isqrt(grade ** skew) + 1 for grade in range(2, amount + 1)]
    surplus, given = total - limit - (amount - 1), [1] * (amount - 1)
    while surplus > 0:
        candidates = [i for i in range(amount - 1) if given[i] < limit]
        mass, remaining = sum([weights[i] for i in candidates]), surplus
        for i in candidates:
            extra = min(limit - given[i], max(1, remaining * weights[i] // mass), surplus)
            given[i] = given[i] + extra
            surplus = surplus - extra
    return np.array([limit] + given)


def ragged(stream_key, number_of, total, limit, slope):
    if number_of == 2:
        one = jax.random.randint(stream_key, (), max(1, total - limit), min(limit, total - 1) + 1)
        return jnp.stack([one, total - one])
    sizes = jnp.asarray(length_profile(number_of, total, limit, slope), jnp.int32)
    twos = (number_of - 1) // 2
    giver, receiver = sizes[1:1 + 2 * twos:2], sizes[2:2 + 2 * twos:2]
    slack = jnp.minimum(giver - 1, limit - receiver)
    shifted = jax.random.randint(jax.random.fold_in(stream_key, 1), (twos,), 0, 1 << 20) % (slack + 1)
    sizes = sizes.at[1:1 + 2 * twos:2].set(giver - shifted).at[2:2 + 2 * twos:2].set(receiver + shifted)
    return sizes[jax.random.permutation(jax.random.fold_in(stream_key, 2), number_of)]


def noise(rng, shape, spread, limit, cuts=(), kind=jnp.bfloat16):
    entries = jax.random.normal(rng, shape, jnp.float32) * spread
    if len(cuts) > 0:
        entries = block_levels(rng, shape, cuts, -0.22, 0.18) * entries
    return jnp.clip(entries, min=-limit, max=limit).astype(kind)


def setup_inputs(seed: int = 0) -> dict:
    arg_keys = jax.random.split(jax.random.key(seed), 19)
    return {
        "inputs": noise(arg_keys[0], (NSEQ, LEN, D), 1.0, 6.0, ((0, 4), (1, 8))),
        "lengths": jax.vmap(lambda own: ragged(own, SEQ_DEV, LIVE, LEN, 1))(jax.random.split(arg_keys[1], N_BATCH)).reshape((N_BATCH, SEQ_DEV)).astype(jnp.int32),
        "pre_attention_gain": jnp.clip(1.0 + 0.1 * jax.random.normal(arg_keys[2], (D,), jnp.float32), 0.5, 1.5).astype(jnp.bfloat16),
        "pre_attention_bias": noise(arg_keys[3], (D,), 0.2, 1.0),
        "pre_forward_gain": jnp.clip(1.0 + 0.1 * jax.random.normal(arg_keys[4], (D,), jnp.float32), 0.5, 1.5).astype(jnp.bfloat16),
        "pre_forward_bias": noise(arg_keys[5], (D,), 0.2, 1.0),
        "query_weight": noise(arg_keys[6], (D, D), (D // 4) ** -0.5, 0.4375),
        "query_bias": noise(arg_keys[7], (D,), 0.3, 1.5),
        "keyvalue_weight": noise(arg_keys[8], (D, 2 * HEAD_DIM), D ** -0.5, 0.21875),
        "keyvalue_bias": noise(arg_keys[9], (2 * HEAD_DIM,), 0.3, 1.5),
        "output_weight": noise(arg_keys[10], (D, D), (D // 16) ** -0.5, 0.875),
        "output_bias": noise(arg_keys[11], (D,), 0.2, 1.0),
        "up_weight": noise(arg_keys[12], (D, FF), D ** -0.5, 0.21875),
        "up_bias": noise(arg_keys[13], (FF,), 0.3, 1.5),
        "down_weight": noise(arg_keys[14], (FF, D), (FF // 2) ** -0.5, 0.15625),
        "down_bias": noise(arg_keys[15], (D,), 0.2, 1.0),
        "out_grad": noise(arg_keys[16], (NSEQ, LEN, D), 1.0, 6.0, ((0, 4), (1, 8))),
        "later_kv_grad": noise(arg_keys[17], (NSEQ, LEN, 2 * HEAD_DIM), 1.0, 6.0, ((0, 4), (1, 8)), jnp.float32),
    }


@jax.custom_vjp
def low(v):
    return lax.optimization_barrier(v.astype(jnp.bfloat16)).astype(jnp.float32)

@jax.custom_vjp
def low_back(v):
    return v

def low_keep(v):
    return (low(v), None)

def low_pass(kept, grad):
    return (grad,)

def back_keep(v):
    return (v, None)

def back_low(kept, grad):
    return (low(grad),)
low.defvjp(low_keep, low_pass)
low_back.defvjp(back_keep, back_low)
norm_eps = 1e-05
masked_score = -1000000000.0
highest = lax.Precision.HIGHEST

def rope_tables(positions):
    half_rot = ROT // 2
    frequency = jnp.exp(jnp.arange(half_rot, dtype=jnp.float32) * (-2.0 * math.log(10000.0) / ROT))
    angles = positions.astype(jnp.float32)[:, None] * frequency[None, :]
    return (jnp.cos(angles), jnp.sin(angles))

def rotate(vector_in, cos_table, sin_table, direction):
    half_rot = ROT // 2
    front_part = vector_in[..., :half_rot]
    back_part = vector_in[..., half_rot:ROT]
    new_front = front_part * cos_table - direction * back_part * sin_table
    new_back = back_part * cos_table + direction * front_part * sin_table
    return jnp.concatenate([new_front, new_back, vector_in[..., ROT:]], axis=-1)

def layer_norm(x_float, gain_vec, bias_vec):
    mean_val = lax.optimization_barrier(jnp.mean(x_float, axis=-1, keepdims=True))
    centered = x_float - mean_val
    variance = lax.optimization_barrier(jnp.mean(centered * centered, axis=-1, keepdims=True))
    return centered * lax.rsqrt(variance + norm_eps) * gain_vec + bias_vec

def project(left_in, right_in):
    return jnp.einsum('gld,df->glf', left_in, right_in, precision=highest)

def forward(x_float, seq_lengths, params):
    attention_norm_gain, attn_shift, feedforward_norm_gain, ffwd_shift, query_weight, query_bias, keyvalue_weight, keyvalue_bias, output_weight, output_bias, up_weight, up_bias, down_weight, down_bias = params
    group_size, seq_len, model_width = x_float.shape
    positions = jnp.arange(seq_len, dtype=jnp.int32)
    cos_table, sin_table = rope_tables(positions)
    h_attn = low(layer_norm(x_float, attention_norm_gain, attn_shift))
    h_ffwd = low(layer_norm(x_float, feedforward_norm_gain, ffwd_shift))
    pair_pre = low_back(project(h_attn, keyvalue_weight) + keyvalue_bias)
    keys_turned = rotate(pair_pre[..., :HEAD_DIM], cos_table, sin_table, 1.0)
    pair_out = low(jnp.concatenate([keys_turned, pair_pre[..., HEAD_DIM:]], axis=-1))
    query_pre = low_back(project(h_attn, query_weight) + query_bias)
    query_turned = rotate(query_pre.reshape(group_size, seq_len, HEADS, HEAD_DIM), cos_table[:, None, :], sin_table[:, None, :], 1.0)
    query_low = low(query_turned)
    raw_scores = jnp.einsum('glhd,gmd->ghlm', query_low, pair_out[..., :HEAD_DIM], precision=highest) * HEAD_DIM ** (-0.5)
    raw_scores = low_back(raw_scores)
    causal = positions[None, :] <= positions[:, None]
    live_keys = positions[None, :] < seq_lengths[:, None]
    allowed = causal[None, None, :, :] & live_keys[:, None, None, :]
    probs = low(jax.nn.softmax(jnp.where(allowed, raw_scores, masked_score), axis=-1))
    mixed = jnp.einsum('ghlm,gmd->glhd', probs, pair_out[..., HEAD_DIM:], precision=highest)
    mixed = low(low_back(mixed)).reshape(group_size, seq_len, model_width)
    attn_branch = project(mixed, output_weight) + output_bias
    up_pre = low_back(project(h_ffwd, up_weight) + up_bias)
    activ = low(jax.nn.gelu(up_pre, approximate=False))
    ffwd_branch = project(activ, down_weight) + down_bias
    return (x_float + attn_branch + ffwd_branch, pair_out)

def reference(inputs, lengths, pre_attention_gain, pre_attention_bias, pre_forward_gain, pre_forward_bias, query_weight, query_bias, keyvalue_weight, keyvalue_bias, output_weight, output_bias, up_weight, up_bias, down_weight, down_bias, out_grad, later_kv_grad):
    params = (pre_attention_gain.astype(jnp.float32), pre_attention_bias.astype(jnp.float32), pre_forward_gain.astype(jnp.float32), pre_forward_bias.astype(jnp.float32), query_weight.astype(jnp.float32), query_bias.astype(jnp.float32), keyvalue_weight.astype(jnp.float32), keyvalue_bias.astype(jnp.float32), output_weight.astype(jnp.float32), output_bias.astype(jnp.float32), up_weight.astype(jnp.float32), up_bias.astype(jnp.float32), down_weight.astype(jnp.float32), down_bias.astype(jnp.float32))
    group_size = math.gcd(NSEQ, max(1, 4096 // LEN))
    group_count = NSEQ // group_size

    def regroup(whole):
        return whole.reshape((group_count, group_size) + whole.shape[1:])

    def step(totals, inputs_now):
        x_group, len_group, grad_group, later_group = inputs_now

        def run(x_in, params_in):
            return forward(x_in, len_group, params_in)
        (out_group, pair_group), pullback = jax.vjp(run, x_group.astype(jnp.float32), params)
        grad_x, grad_params = pullback((grad_group.astype(jnp.float32), later_group))
        totals = jax.tree.map(jnp.add, totals, grad_params)
        return (totals, (out_group.astype(jnp.bfloat16), pair_group.astype(jnp.bfloat16), grad_x))
    start = jax.tree.map(jnp.zeros_like, params)
    grad_sums, (outs_all, pairs_all, grads_all) = lax.scan(step, start, (regroup(inputs), regroup(lengths.reshape(-1)), regroup(out_grad), regroup(later_kv_grad)))
    layer_out = outs_all.reshape(NSEQ, LEN, D)
    keyvalue_out = pairs_all.reshape(NSEQ, LEN, 2 * HEAD_DIM)
    input_grad = grads_all.reshape(NSEQ, LEN, D)
    return (layer_out, keyvalue_out, input_grad, grad_sums[0], grad_sums[1], grad_sums[2], grad_sums[3], grad_sums[4], grad_sums[5], grad_sums[6], grad_sums[7], grad_sums[8], grad_sums[9], grad_sums[10], grad_sums[11], grad_sums[12], grad_sums[13])
```

```python
import functools
import math

import jax
import jax.numpy as jnp
from jax import lax
from jax.experimental import pallas as pl
from jax.experimental.pallas import tpu as pltpu
from jax.sharding import PartitionSpec as P

ROT = 16
EPS = 1e-05
LOG2E = 1.4426950408889634
f32 = jnp.float32
bf16 = jnp.bfloat16
VMEM_LIMIT = 58 << 20


def dot(left, right, left_dim, right_dim):
    return lax.dot_general(
        left, right, (((left_dim,), (right_dim,)), ((), ())), preferred_element_type=f32
    )


def params():
    return pltpu.CompilerParams(
        dimension_semantics=("arbitrary",), vmem_limit_bytes=VMEM_LIMIT
    )


def rope_tables(first, count):
    half = ROT // 2
    frequency = jnp.exp(jnp.arange(half, dtype=f32) * (-2.0 * math.log(10000.0) / ROT))
    angles = (first + jnp.arange(count, dtype=jnp.int32)).astype(f32)[:, None] * frequency[None, :]
    cos, sin = jnp.cos(angles), jnp.sin(angles)
    one = jnp.ones((count, 64 - ROT), f32)
    nil = jnp.zeros((count, half), f32)
    rest = jnp.zeros((count, 64 - ROT), f32)
    main = jnp.concatenate([cos, cos, one], axis=1)
    front = jnp.concatenate([-sin, nil, rest], axis=1)
    back = jnp.concatenate([nil, sin, rest], axis=1)
    return jnp.stack([jnp.concatenate([t, t], axis=1) for t in (main, front, back)])


def rope(x, main, front, back):
    return x * main + pltpu.roll(x, 120, 1) * front + pltpu.roll(x, 8, 1) * back


def stacked(table, times):
    return jnp.concatenate([table] * times, axis=0)


def standardize(x):
    mean = jnp.mean(x, axis=1, keepdims=True)
    centered = x - mean
    inv = lax.rsqrt(jnp.mean(centered * centered, axis=1, keepdims=True) + EPS)
    return centered * inv, inv


def full(shape):
    return pl.BlockSpec(shape, lambda *_: (0,) * len(shape))


def rows_of(rows, width):
    return pl.BlockSpec((rows, width), lambda i, *_: (i, 0))


def norm_kv(x, vecs, kv_w, kv_b, tables, rows, times):
    total, width = x.shape

    def body(x_ref, vec_ref, w_ref, b_ref, t_ref, ha_ref, hf_ref, kv_ref):
        xhat, _ = standardize(x_ref[...].astype(f32))
        ha = (xhat * vec_ref[0:1, :] + vec_ref[1:2, :]).astype(bf16)
        hf_ref[...] = (xhat * vec_ref[2:3, :] + vec_ref[3:4, :]).astype(bf16)
        ha_ref[...] = ha
        kv = dot(ha, w_ref[...], 1, 0) + b_ref[...]
        lane = lax.broadcasted_iota(jnp.int32, (1, 128), 1)
        turned = rope(kv, *[stacked(t_ref[i], times) for i in range(3)])
        kv_ref[...] = jnp.where(lane < 64, turned, kv).astype(bf16)

    return pl.pallas_call(
        body,
        grid=(total // rows,),
        in_specs=[rows_of(rows, width), full(vecs.shape), full(kv_w.shape), full(kv_b.shape), full(tables.shape)],
        out_specs=[rows_of(rows, width), rows_of(rows, width), rows_of(rows, 128)],
        out_shape=[
            jax.ShapeDtypeStruct((total, width), bf16),
            jax.ShapeDtypeStruct((total, width), bf16),
            jax.ShapeDtypeStruct((total, 128), bf16),
        ],
        compiler_params=params(),
        name="norm_kv",
    )(x, vecs, kv_w, kv_b, tables)


def query_grad_o(ha, g, q_w, q_b, o_w, tables, rows, times):
    total, width = ha.shape

    def body(ha_ref, g_ref, wq_ref, bq_ref, wo_ref, t_ref, q_ref, go_ref):
        q = dot(ha_ref[...], wq_ref[...], 1, 0) + bq_ref[...]
        turn = [stacked(t_ref[i], times) for i in range(3)]
        for c in range(0, width, 128):
            q_ref[:, c : c + 128] = rope(q[:, c : c + 128], *turn).astype(bf16)
        go_ref[...] = dot(g_ref[...], wo_ref[...], 1, 1).astype(bf16)

    return pl.pallas_call(
        body,
        grid=(total // rows,),
        in_specs=[
            rows_of(rows, width), rows_of(rows, width), full(q_w.shape), full(q_b.shape),
            full(o_w.shape), full(tables.shape),
        ],
        out_specs=[rows_of(rows, width), rows_of(rows, width)],
        out_shape=[jax.ShapeDtypeStruct((total, width), bf16)] * 2,
        compiler_params=params(),
        name="query_grad_o",
    )(ha, g, q_w, q_b, o_w, tables)


def gelu_and_slope(u):
    cdf = 0.5 + 0.5 * lax.erf(u * 0.7071067811865476)
    pdf = jnp.exp(u * u * -0.5) * 0.3989422804014327
    return u * cdf, cdf + u * pdf


def feed_forward(h, g, up_w, up_b, down_w, chunk, rows):
    total, width = h.shape
    hidden = up_w.shape[1]

    def body(h_ref, g_ref, wu_ref, bu_ref, wd_ref, out_ref, gh_ref, dwu_ref, dwd_ref, dbu_ref, act_s, gup_s):
        @pl.when(pl.program_id(0) == 0)
        def _():
            out_ref[...] = jnp.zeros_like(out_ref)
            gh_ref[...] = jnp.zeros_like(gh_ref)

        wu = wu_ref[...]
        wd = wd_ref[...]
        bu = bu_ref[...]

        def block(i, acc):
            sl = pl.ds(pl.multiple_of(i * rows, rows), rows)
            hb = h_ref[sl, :]
            gb = g_ref[sl, :]
            act, slope = gelu_and_slope(dot(hb, wu, 1, 0) + bu)
            act = act.astype(bf16)
            gup = (dot(gb, wd, 1, 1) * slope).astype(bf16)
            act_s[sl, :] = act
            gup_s[sl, :] = gup
            out_ref[sl, :] += dot(act, wd, 1, 0)
            gh_ref[sl, :] += dot(gup, wu, 1, 1)
            return acc + jnp.sum(gup.astype(f32), axis=0, keepdims=True)

        dbu_ref[...] = lax.fori_loop(0, total // rows, block, jnp.zeros((1, chunk), f32))
        dwu_ref[...] = dot(h_ref[...], gup_s[...], 0, 0).astype(bf16)
        dwd_ref[...] = dot(act_s[...], g_ref[...], 0, 0).astype(bf16)

    whole = full((total, width))
    cols = pl.BlockSpec((width, chunk), lambda c: (0, c))
    vec = pl.BlockSpec((1, chunk), lambda c: (0, c))
    tall = pl.BlockSpec((chunk, width), lambda c: (c, 0))
    return pl.pallas_call(
        body,
        grid=(hidden // chunk,),
        in_specs=[whole, whole, cols, vec, tall],
        out_specs=[whole, whole, cols, tall, vec],
        out_shape=[
            jax.ShapeDtypeStruct((total, width), f32),
            jax.ShapeDtypeStruct((total, width), f32),
            jax.ShapeDtypeStruct((width, hidden), bf16),
            jax.ShapeDtypeStruct((hidden, width), bf16),
            jax.ShapeDtypeStruct((1, hidden), f32),
        ],
        scratch_shapes=[pltpu.VMEM((total, chunk), bf16), pltpu.VMEM((total, chunk), bf16)],
        compiler_params=params(),
        name="feed_forward",
    )(h, g, up_w, up_b, down_w)


def attention(lengths, place, q, go, kv, tables, first, count, keep, key_block):
    seqs, block, width = q.shape
    span = kv.shape[1]
    pairs = width // 128

    def body(len_ref, place_ref, q_ref, go_ref, kv_ref, t_ref, *refs):
        o_ref, dq_ref, dkv_ref, dk_acc, dv_acc = refs[-5:]
        live = len_ref[pl.program_id(0) + first]
        start = place_ref[0] * block
        limit = jnp.minimum(live, start + block)
        blocks = (limit + key_block - 1) // key_block
        lane = lax.broadcasted_iota(jnp.int32, (1, 128), 1)
        low = lane < 64
        scale = 0.125

        def branch(number):
            keys = number * key_block
            pair = kv_ref[0, :keys, :].astype(f32)
            swapped = pltpu.roll(pair, 64, 1)
            key_pos = (keys - key_block) + lax.broadcasted_iota(jnp.int32, (block, key_block), 1)
            own_pos = start + lax.broadcasted_iota(jnp.int32, (block, key_block), 0)
            bias = jnp.where((key_pos <= own_pos) & (key_pos < live), 0.0, -1e9).astype(f32)
            bias = stacked(bias, pairs)
            qs = jnp.concatenate([q_ref[0, :, 128 * p : 128 * (p + 1)] for p in range(pairs)], axis=0)
            gs = jnp.concatenate([go_ref[0, :, 128 * p : 128 * (p + 1)] for p in range(pairs)], axis=0)
            gf = gs.astype(f32)

            def half(k_side, v_side):
                s = dot(qs, k_side, 1, 1)
                last = s[:, keys - key_block :] + bias
                s = jnp.concatenate([s[:, : keys - key_block], last], axis=1) if number > 1 else last
                top = jnp.max(s, axis=1, keepdims=True)
                expo = jnp.exp2((s - top) * (scale * LOG2E))
                prob = expo * (1.0 / jnp.sum(expo, axis=1, keepdims=True))
                prob_low = prob.astype(bf16)
                o = dot(prob_low, v_side, 1, 0)
                dp = dot(gs, v_side, 1, 1)
                delta = jnp.sum(o * gf, axis=1, keepdims=True)
                ds = (prob * (dp - delta)).astype(bf16)
                return o, dot(ds, k_side, 1, 0), dot(ds, qs, 0, 0), dot(prob_low, gs, 0, 0)

            o0, dq0, dk0, dv0 = half(
                jnp.where(low, pair, 0.0).astype(bf16), jnp.where(low, swapped, 0.0).astype(bf16)
            )
            dk_acc[:keys, :] = dk0
            dv_acc[:keys, :] = dv0
            o1, dq1, dk1, dv1 = half(
                jnp.where(low, 0.0, swapped).astype(bf16), jnp.where(low, 0.0, pair).astype(bf16)
            )
            o = (o0 + o1).astype(bf16)
            dq = (dq0 + dq1) * scale
            turn = [t_ref[0], -t_ref[1], -t_ref[2]]
            for p in range(pairs):
                o_ref[0, :, 128 * p : 128 * (p + 1)] = o[p * block : (p + 1) * block]
                dq_ref[0, :, 128 * p : 128 * (p + 1)] = rope(dq[p * block : (p + 1) * block], *turn).astype(bf16)
            dk = (dk_acc[:keys, :] + pltpu.roll(dk1, 64, 1)) * scale
            dv = dv1 + pltpu.roll(dv_acc[:keys, :], 64, 1)
            dkv_ref[0, :keys, :] = jnp.where(low, dk, dv).astype(bf16)
            if keys < span:
                dkv_ref[0, keys:, :] = jnp.zeros((span - keys, 128), bf16)

        for number in range(1, span // key_block + 1):
            pl.when(blocks == number)(functools.partial(branch, number))

    row = pl.BlockSpec((1, block, width), lambda s, *_: (s + first, 0, 0))
    kv_in = pl.BlockSpec((1, span, 128), lambda s, *_: (s + first, 0, 0))
    kv_out = pl.BlockSpec((1, span, 128), lambda s, *_: (s, 0, 0))
    anywhere = pl.BlockSpec(memory_space=pl.ANY)
    return pl.pallas_call(
        body,
        grid_spec=pltpu.PrefetchScalarGridSpec(
            num_scalar_prefetch=2,
            grid=(count,),
            in_specs=[row, row, kv_in, full(tables.shape)] + [anywhere] * len(keep),
            out_specs=[row, row, kv_out],
            scratch_shapes=[pltpu.VMEM((span, 128), f32), pltpu.VMEM((span, 128), f32)],
        ),
        out_shape=[
            jax.ShapeDtypeStruct((seqs, block, width), bf16),
            jax.ShapeDtypeStruct((seqs, block, width), bf16),
            jax.ShapeDtypeStruct((count, span, 128), bf16),
        ],
        input_output_aliases={6: 0, 7: 1} if keep else {},
        compiler_params=params(),
        name="attention",
    )(lengths, place, q, go, kv, tables, *keep)


def projections(o, g, x, ffn, ha, dq, o_w, q_w, bias, rows):
    total, width = o.shape

    def body(o_ref, g_ref, x_ref, f_ref, ha_ref, dq_ref, wo_ref, wq_ref, b_ref, out_ref, gh_ref, dwo_ref, dwq_ref, sum_ref, acc_o, acc_q):
        step = pl.program_id(0)
        ob = o_ref[...]
        gb = g_ref[...]
        dqb = dq_ref[...]
        out = x_ref[...].astype(f32) + dot(ob, wo_ref[...], 1, 0) + f_ref[...] + b_ref[...]
        out_ref[...] = out.astype(bf16)
        gh_ref[...] = dot(dqb, wq_ref[...], 1, 1)
        dwo = dot(ob, gb, 0, 0)
        dwq = dot(ha_ref[...], dqb, 0, 0)
        sums = jnp.concatenate(
            [jnp.sum(gb.astype(f32), axis=0, keepdims=True), jnp.sum(dqb.astype(f32), axis=0, keepdims=True)], axis=0
        )

        @pl.when(step == 0)
        def _():
            acc_o[...] = dwo
            acc_q[...] = dwq
            sum_ref[...] = sums

        @pl.when(step > 0)
        def _():
            acc_o[...] += dwo
            acc_q[...] += dwq
            sum_ref[...] += sums

        dwo_ref[...] = acc_o[...].astype(bf16)
        dwq_ref[...] = acc_q[...].astype(bf16)

    r = rows_of(rows, width)
    square = full((width, width))
    return pl.pallas_call(
        body,
        grid=(total // rows,),
        in_specs=[r, r, r, r, r, r, square, square, full((1, width))],
        out_specs=[r, r, square, square, full((2, width))],
        out_shape=[
            jax.ShapeDtypeStruct((total, width), bf16),
            jax.ShapeDtypeStruct((total, width), f32),
            jax.ShapeDtypeStruct((width, width), bf16),
            jax.ShapeDtypeStruct((width, width), bf16),
            jax.ShapeDtypeStruct((2, width), f32),
        ],
        scratch_shapes=[pltpu.VMEM((width, width), f32), pltpu.VMEM((width, width), f32)],
        compiler_params=params(),
        name="projections",
    )(o, g, x, ffn, ha, dq, o_w, q_w, bias)


def input_gradient(x, g, ghq, ghf, gkv, later, ha, kv_w, vecs, tables, rows, times):
    total, width = x.shape

    def body(x_ref, g_ref, ghq_ref, ghf_ref, gkv_ref, later_ref, ha_ref, w_ref, vec_ref, t_ref, dx_ref, dw_ref, sum_ref, sumkv_ref):
        step = pl.program_id(0)
        lane = lax.broadcasted_iota(jnp.int32, (1, 128), 1)
        pair = gkv_ref[...] + later_ref[...]
        turn = [stacked(t_ref[i], times) for i in range(3)]
        pair = jnp.where(lane < 64, rope(pair, turn[0], -turn[1], -turn[2]), pair).astype(bf16)
        gha = ghq_ref[...] + dot(pair, w_ref[...], 1, 1)
        ghf = ghf_ref[...]
        xhat, inv = standardize(x_ref[...].astype(f32))
        gn = gha * vec_ref[0:1, :] + ghf * vec_ref[2:3, :]
        first = jnp.mean(gn, axis=1, keepdims=True)
        second = jnp.mean(gn * xhat, axis=1, keepdims=True)
        dx_ref[...] = g_ref[...].astype(f32) + inv * (gn - first - xhat * second)
        dw = dot(ha_ref[...], pair, 0, 0)
        sums = jnp.concatenate(
            [jnp.sum(v, axis=0, keepdims=True) for v in (gha * xhat, gha, ghf * xhat, ghf)], axis=0
        )
        sumkv = jnp.sum(pair.astype(f32), axis=0, keepdims=True)

        @pl.when(step == 0)
        def _():
            dw_ref[...] = dw
            sum_ref[...] = sums
            sumkv_ref[...] = sumkv

        @pl.when(step > 0)
        def _():
            dw_ref[...] += dw
            sum_ref[...] += sums
            sumkv_ref[...] += sumkv

    r = rows_of(rows, width)
    n = rows_of(rows, 128)
    return pl.pallas_call(
        body,
        grid=(total // rows,),
        in_specs=[r, r, r, r, n, n, r, full(kv_w.shape), full(vecs.shape), full(tables.shape)],
        out_specs=[r, full((width, 128)), full((4, width)), full((1, 128))],
        out_shape=[
            jax.ShapeDtypeStruct((total, width), f32),
            jax.ShapeDtypeStruct((width, 128), f32),
            jax.ShapeDtypeStruct((4, width), f32),
            jax.ShapeDtypeStruct((1, 128), f32),
        ],
        compiler_params=params(),
        name="input_gradient",
    )(x, g, ghq, ghf, gkv, later, ha, kv_w, vecs, tables)


def flip(axis, size, bit):
    return [(i, i ^ (1 << bit)) for i in range(size)]


def bit_of(axis, bit):
    return (lax.axis_index(axis) >> bit) & 1


def halve(parts, axis, size, bit, dims, last):
    mine = bit_of(axis, bit)
    out = []
    for part in parts:
        own = lax.dynamic_index_in_dim(part, mine, dims, keepdims=False)
        other = lax.dynamic_index_in_dim(part, 1 - mine, dims, keepdims=False)
        got = lax.ppermute(other, axis, flip(axis, size, bit))
        total = own.astype(f32) + got.astype(f32)
        out.append(total if last else total.astype(bf16))
    return out


def bits(size):
    return size.bit_length() - 1


def scatter_weights(parts, seq, batch, start=0, stop=None):
    names = [("seq", b) for b in reversed(range(bits(seq)))] + [("batch", b) for b in reversed(range(bits(batch)))]
    parts = [p.reshape((2,) * len(names) + (p.shape[0] // (seq * batch),) + p.shape[1:]) for p in parts]
    order = [("batch", b) for b in range(bits(batch))] + [("seq", b) for b in range(bits(seq))]
    for number, item in enumerate(order):
        size = seq if item[0] == "seq" else batch
        parts = halve(parts, item[0], size, item[1], names.index(item), number == len(order) - 1)
        names.remove(item)
    return parts


def scatter_seq(part, seq):
    count, span, width = part.shape
    part = part.reshape((count,) + (2,) * bits(seq) + (span // seq, width))
    for b in range(bits(seq)):
        part = halve([part], "seq", seq, b, bits(seq) - b, b == bits(seq) - 1)[0]
    return part


def all_sum(x, seq, batch):
    for axis, size in (("batch", batch), ("seq", seq)):
        for b in range(bits(size)):
            x = x + lax.ppermute(x, axis, flip(axis, size, b))
    return x


def make(mesh):
    seq = mesh.shape["seq"]
    batch = mesh.shape["batch"]

    def shards(
        inputs, lengths, ga, ba, gf, bf, q_w, q_b, kv_w, kv_b, o_w, o_b, up_w, up_b, down_w, down_b, out_grad, later
    ):
        seqs, block, width = inputs.shape
        total = seqs * block
        span = block * seq
        hidden = up_w.shape[1]
        place = lax.axis_index("seq").astype(jnp.int32).reshape(1)
        tables = rope_tables(place[0] * block, block)
        x = inputs.reshape(total, width)
        g = out_grad.reshape(total, width)
        vecs = jnp.stack([ga, ba, gf, bf]).astype(f32)
        rows = 2 * block
        ha, hf, kv = norm_kv(x, vecs, kv_w, kv_b.astype(f32)[None], tables, rows, 2)
        kv = kv.reshape(seqs, block, 128)
        kv_all = lax.all_gather(kv, "seq", axis=1, tiled=True)
        q, go = query_grad_o(ha, g, q_w, q_b.astype(f32)[None], o_w, tables, rows, 2)
        ffn, ghf, dwu, dwd, dbu = feed_forward(hf, g, up_w, up_b.astype(f32)[None], down_w, 768, total // 2)
        q = q.reshape(seqs, block, width)
        go = go.reshape(seqs, block, width)
        live = lengths[0]
        groups = [5, 5, 4]
        keep = ()
        first = 0
        sums = []
        for count in groups:
            o, dq, dkv = attention(live, place, q, go, kv_all, tables, first, count, keep, 256)
            keep = (o, dq)
            first += count
            sums.append(scatter_seq(dkv, seq))
        sum_up, sum_down = scatter_weights([dwu, dwd], seq, batch)
        gkv = jnp.concatenate(sums, axis=0).reshape(total, 128)
        bias = (o_b.astype(f32) + down_b.astype(f32))[None]
        out, ghq, dwo, dwq, early = projections(
            o.reshape(total, width), g, x, ffn, ha, dq.reshape(total, width), o_w, q_w, bias, total // 2
        )
        sum_o, sum_q = scatter_weights([dwo, dwq], seq, batch)
        dx, dwkv, late, sumkv = input_gradient(
            x, g, ghq, ghf, gkv, later.reshape(total, 128), ha, kv_w, vecs, tables, rows, 2
        )
        (sum_kv,) = scatter_weights([dwkv.astype(bf16)], seq, batch)
        vec = jnp.concatenate([early.reshape(-1), late.reshape(-1), dbu.reshape(-1), sumkv.reshape(-1)])
        vec = all_sum(jnp.pad(vec, (0, -vec.shape[0] % 1024)).reshape(-1, 128), seq, batch).reshape(-1)
        sg, sq = vec[:width], vec[width : 2 * width]
        sv = [vec[(2 + i) * width : (3 + i) * width] for i in range(4)]
        su = vec[6 * width : 6 * width + hidden]
        sk = vec[6 * width + hidden : 6 * width + hidden + 128]
        return (
            out.reshape(seqs, block, width), kv, dx.reshape(seqs, block, width), sv[0], sv[1], sv[2], sv[3],
            sum_q, sq, sum_kv, sk, sum_o, sg, sum_up, su, sum_down, sg,
        )

    return shards


def solution(mesh):
    rows = P("batch", "seq", None)
    split = P(("seq", "batch"), None)
    return jax.shard_map(
        make(mesh),
        mesh=mesh,
        in_specs=(rows, P("batch", None)) + (P(),) * 14 + (rows, rows),
        out_specs=(rows, rows, rows, P(), P(), P(), P(), split, P(), split, P(), split, P(), split, P(), split, P()),
        check_vma=False,
    )
```

```python
import functools
import math

import jax
import jax.numpy as jnp
from jax import lax
from jax.experimental import pallas as pl
from jax.experimental.pallas import tpu as pltpu
from jax.sharding import PartitionSpec as P

ROT = 16
EPS = 1e-05
LOG2E = 1.4426950408889634
f32 = jnp.float32
bf16 = jnp.bfloat16
VMEM_LIMIT = 58 << 20


def dot(left, right, left_dim, right_dim):
    return lax.dot_general(
        left, right, (((left_dim,), (right_dim,)), ((), ())), preferred_element_type=f32
    )


def params():
    return pltpu.CompilerParams(
        dimension_semantics=("arbitrary",), vmem_limit_bytes=VMEM_LIMIT
    )


def rope_tables(first, count):
    half = ROT // 2
    lane = jnp.arange(128, dtype=jnp.int32)[None, :] % 64
    frequency = jnp.exp((lane % half).astype(f32) * (-2.0 * math.log(10000.0) / ROT))
    angles = (first + jnp.arange(count, dtype=jnp.int32)).astype(f32)[:, None] * frequency
    main = jnp.where(lane < ROT, jnp.cos(angles), 1.0)
    sin = jnp.sin(angles)
    front = jnp.where(lane < half, -sin, 0.0)
    back = jnp.where((lane >= half) & (lane < ROT), sin, 0.0)
    return jnp.stack([main, front, back])


def rope(x, main, front, back):
    return x * main + pltpu.roll(x, 120, 1) * front + pltpu.roll(x, 8, 1) * back


def stacked(table, times):
    return jnp.concatenate([table] * times, axis=0)


def standardize(x):
    mean = jnp.mean(x, axis=1, keepdims=True)
    centered = x - mean
    inv = lax.rsqrt(jnp.mean(centered * centered, axis=1, keepdims=True) + EPS)
    return centered * inv, inv


def full(shape):
    return pl.BlockSpec(shape, lambda *_: (0,) * len(shape))


def rows_of(rows, width):
    return pl.BlockSpec((rows, width), lambda i, *_: (i, 0))


def norm_kv(x, vecs, kv_w, kv_b, tables, rows, times):
    total, width = x.shape

    def body(x_ref, vec_ref, w_ref, b_ref, t_ref, ha_ref, hf_ref, kv_ref):
        xhat, _ = standardize(x_ref[...].astype(f32))
        ha = (xhat * vec_ref[0:1, :] + vec_ref[1:2, :]).astype(bf16)
        hf_ref[...] = (xhat * vec_ref[2:3, :] + vec_ref[3:4, :]).astype(bf16)
        ha_ref[...] = ha
        kv = dot(ha, w_ref[...], 1, 0) + b_ref[...]
        lane = lax.broadcasted_iota(jnp.int32, (1, 128), 1)
        turned = rope(kv, *[stacked(t_ref[i], times) for i in range(3)])
        kv_ref[...] = jnp.where(lane < 64, turned, kv).astype(bf16)

    return pl.pallas_call(
        body,
        grid=(total // rows,),
        in_specs=[rows_of(rows, width), full(vecs.shape), full(kv_w.shape), full(kv_b.shape), full(tables.shape)],
        out_specs=[rows_of(rows, width), rows_of(rows, width), rows_of(rows, 128)],
        out_shape=[
            jax.ShapeDtypeStruct((total, width), bf16),
            jax.ShapeDtypeStruct((total, width), bf16),
            jax.ShapeDtypeStruct((total, 128), bf16),
        ],
        compiler_params=params(),
        name="norm_kv",
    )(x, vecs, kv_w, kv_b, tables)


def query_grad_o(ha, g, q_w, q_b, o_w, tables, rows, times):
    total, width = ha.shape

    def body(ha_ref, g_ref, wq_ref, bq_ref, wo_ref, t_ref, q_ref, go_ref):
        q = dot(ha_ref[...], wq_ref[...], 1, 0) + bq_ref[...]
        turn = [stacked(t_ref[i], times) for i in range(3)]
        for c in range(0, width, 128):
            q_ref[:, c : c + 128] = rope(q[:, c : c + 128], *turn).astype(bf16)
        go_ref[...] = dot(g_ref[...], wo_ref[...], 1, 1).astype(bf16)

    return pl.pallas_call(
        body,
        grid=(total // rows,),
        in_specs=[
            rows_of(rows, width), rows_of(rows, width), full(q_w.shape), full(q_b.shape),
            full(o_w.shape), full(tables.shape),
        ],
        out_specs=[rows_of(rows, width), rows_of(rows, width)],
        out_shape=[jax.ShapeDtypeStruct((total, width), bf16)] * 2,
        compiler_params=params(),
        name="query_grad_o",
    )(ha, g, q_w, q_b, o_w, tables)


def gelu_and_slope(u):
    cdf = 0.5 + 0.5 * lax.erf(u * 0.7071067811865476)
    pdf = jnp.exp(u * u * -0.5) * 0.3989422804014327
    return u * cdf, cdf + u * pdf


def feed_forward(h, g, up_w, up_b, down_w, chunk, rows):
    total, width = h.shape
    hidden = up_w.shape[1]

    def body(h_ref, g_ref, wu_ref, bu_ref, wd_ref, act_ref, gh_ref, dwu_ref, dwd_ref, dbu_ref, gup_s):
        @pl.when(pl.program_id(0) == 0)
        def _():
            gh_ref[...] = jnp.zeros_like(gh_ref)

        wu = wu_ref[...]
        wd = wd_ref[...]
        bu = bu_ref[...]

        def block(i, acc):
            sl = pl.ds(pl.multiple_of(i * rows, rows), rows)
            hb = h_ref[sl, :]
            gb = g_ref[sl, :]
            act, slope = gelu_and_slope(dot(hb, wu, 1, 0) + bu)
            act = act.astype(bf16)
            gup = (dot(gb, wd, 1, 1) * slope).astype(bf16)
            act_ref[sl, :] = act
            gup_s[sl, :] = gup
            gh_ref[sl, :] += dot(gup, wu, 1, 1)
            return acc + jnp.sum(gup.astype(f32), axis=0, keepdims=True)

        dbu_ref[...] = lax.fori_loop(0, total // rows, block, jnp.zeros((1, chunk), f32))
        dwu_ref[...] = dot(h_ref[...], gup_s[...], 0, 0).astype(bf16)
        dwd_ref[...] = dot(act_ref[...], g_ref[...], 0, 0).astype(bf16)

    whole = full((total, width))
    cols = pl.BlockSpec((width, chunk), lambda c: (0, c))
    vec = pl.BlockSpec((1, chunk), lambda c: (0, c))
    tall = pl.BlockSpec((chunk, width), lambda c: (c, 0))
    return pl.pallas_call(
        body,
        grid=(hidden // chunk,),
        in_specs=[whole, whole, cols, vec, tall],
        out_specs=[pl.BlockSpec((total, chunk), lambda c: (0, c)), whole, cols, tall, vec],
        out_shape=[
            jax.ShapeDtypeStruct((total, hidden), bf16),
            jax.ShapeDtypeStruct((total, width), f32),
            jax.ShapeDtypeStruct((width, hidden), bf16),
            jax.ShapeDtypeStruct((hidden, width), bf16),
            jax.ShapeDtypeStruct((1, hidden), f32),
        ],
        scratch_shapes=[pltpu.VMEM((total, chunk), bf16)],
        compiler_params=params(),
        name="feed_forward",
    )(h, g, up_w, up_b, down_w)


def attention(lengths, place, q, go, kv, tables, first, count, keep, key_block):
    seqs, block, width = q.shape
    span = kv.shape[1]
    pairs = width // 128

    def body(len_ref, place_ref, q_ref, go_ref, kv_ref, t_ref, *refs):
        o_ref, dq_ref, dkv_ref, dk_acc, dv_acc = refs[-5:]
        live = len_ref[pl.program_id(0) + first]
        start = place_ref[0] * block
        limit = jnp.minimum(live, start + block)
        blocks = (limit + key_block - 1) // key_block
        lane = lax.broadcasted_iota(jnp.int32, (1, 128), 1)
        low = lane < 64
        scale = 0.125

        def branch(number):
            keys = number * key_block
            pair = kv_ref[0, :keys, :].astype(f32)
            swapped = pltpu.roll(pair, 64, 1)
            key_pos = (keys - key_block) + lax.broadcasted_iota(jnp.int32, (block, key_block), 1)
            own_pos = start + lax.broadcasted_iota(jnp.int32, (block, key_block), 0)
            bias = jnp.where((key_pos <= own_pos) & (key_pos < live), 0.0, -1e9).astype(f32)
            bias = stacked(bias, pairs)
            qs = jnp.concatenate([q_ref[0, :, 128 * p : 128 * (p + 1)] for p in range(pairs)], axis=0)
            gs = jnp.concatenate([go_ref[0, :, 128 * p : 128 * (p + 1)] for p in range(pairs)], axis=0)
            gf = gs.astype(f32)

            def half(k_side, v_side):
                s = dot(qs, k_side, 1, 1)
                last = s[:, keys - key_block :] + bias
                s = jnp.concatenate([s[:, : keys - key_block], last], axis=1) if number > 1 else last
                top = jnp.max(s, axis=1, keepdims=True)
                expo = jnp.exp2((s - top) * (scale * LOG2E))
                prob = expo * (1.0 / jnp.sum(expo, axis=1, keepdims=True))
                prob_low = prob.astype(bf16)
                o = dot(prob_low, v_side, 1, 0)
                dp = dot(gs, v_side, 1, 1)
                delta = jnp.sum(o * gf, axis=1, keepdims=True)
                ds = (prob * (dp - delta)).astype(bf16)
                return o, dot(ds, k_side, 1, 0), dot(ds, qs, 0, 0), dot(prob_low, gs, 0, 0)

            o0, dq0, dk0, dv0 = half(
                jnp.where(low, pair, 0.0).astype(bf16), jnp.where(low, swapped, 0.0).astype(bf16)
            )
            dk_acc[:keys, :] = dk0
            dv_acc[:keys, :] = dv0
            o1, dq1, dk1, dv1 = half(
                jnp.where(low, 0.0, swapped).astype(bf16), jnp.where(low, 0.0, pair).astype(bf16)
            )
            o = (o0 + o1).astype(bf16)
            dq = (dq0 + dq1) * scale
            turn = [t_ref[0], -t_ref[1], -t_ref[2]]
            for p in range(pairs):
                o_ref[0, :, 128 * p : 128 * (p + 1)] = o[p * block : (p + 1) * block]
                dq_ref[0, :, 128 * p : 128 * (p + 1)] = rope(dq[p * block : (p + 1) * block], *turn).astype(bf16)
            dk = (dk_acc[:keys, :] + pltpu.roll(dk1, 64, 1)) * scale
            dv = dv1 + pltpu.roll(dv_acc[:keys, :], 64, 1)
            dkv_ref[: keys // block, 0] = jnp.where(low, dk, dv).astype(bf16).reshape(keys // block, block, 128)
            if keys < span:
                dkv_ref[keys // block :, 0] = jnp.zeros(((span - keys) // block, block, 128), bf16)

        for number in range(1, span // key_block + 1):
            pl.when(blocks == number)(functools.partial(branch, number))

    row = pl.BlockSpec((1, block, width), lambda s, *_: (s + first, 0, 0))
    kv_in = pl.BlockSpec((1, span, 128), lambda s, *_: (s + first, 0, 0))
    kv_out = pl.BlockSpec((span // block, 1, block, 128), lambda s, *_: (0, s, 0, 0))
    anywhere = pl.BlockSpec(memory_space=pl.ANY)
    return pl.pallas_call(
        body,
        grid_spec=pltpu.PrefetchScalarGridSpec(
            num_scalar_prefetch=2,
            grid=(count,),
            in_specs=[row, row, kv_in, full(tables.shape)] + [anywhere] * len(keep),
            out_specs=[row, row, kv_out],
            scratch_shapes=[pltpu.VMEM((span, 128), f32), pltpu.VMEM((span, 128), f32)],
        ),
        out_shape=[
            jax.ShapeDtypeStruct((seqs, block, width), bf16),
            jax.ShapeDtypeStruct((seqs, block, width), bf16),
            jax.ShapeDtypeStruct((span // block, count, block, 128), bf16),
        ],
        input_output_aliases={6: 0, 7: 1} if keep else {},
        compiler_params=params(),
        name="attention",
    )(lengths, place, q, go, kv, tables, *keep)


def weight_grads(o, g, ha, dq, q_w, rows):
    total, width = o.shape

    def body(o_ref, g_ref, ha_ref, dq_ref, wq_ref, gh_ref, dwo_ref, dwq_ref, sum_ref, acc_o, acc_q):
        step = pl.program_id(0)
        gb = g_ref[...]
        dqb = dq_ref[...]
        gh_ref[...] = dot(dqb, wq_ref[...], 1, 1)
        dwo = dot(o_ref[...], gb, 0, 0)
        dwq = dot(ha_ref[...], dqb, 0, 0)
        sums = jnp.concatenate(
            [jnp.sum(gb.astype(f32), axis=0, keepdims=True), jnp.sum(dqb.astype(f32), axis=0, keepdims=True)], axis=0
        )

        @pl.when(step == 0)
        def _():
            acc_o[...] = dwo
            acc_q[...] = dwq
            sum_ref[...] = sums

        @pl.when(step > 0)
        def _():
            acc_o[...] += dwo
            acc_q[...] += dwq
            sum_ref[...] += sums

        dwo_ref[...] = acc_o[...].astype(bf16)
        dwq_ref[...] = acc_q[...].astype(bf16)

    r = rows_of(rows, width)
    square = full((width, width))
    return pl.pallas_call(
        body,
        grid=(total // rows,),
        in_specs=[r, r, r, r, square],
        out_specs=[r, square, square, full((2, width))],
        out_shape=[
            jax.ShapeDtypeStruct((total, width), f32),
            jax.ShapeDtypeStruct((width, width), bf16),
            jax.ShapeDtypeStruct((width, width), bf16),
            jax.ShapeDtypeStruct((2, width), f32),
        ],
        scratch_shapes=[pltpu.VMEM((width, width), f32), pltpu.VMEM((width, width), f32)],
        compiler_params=params(),
        name="weight_grads",
    )(o, g, ha, dq, q_w)


def layer_output(o, act, x, o_w, down_w, bias, rows, first, count, keep):
    total, width = o.shape
    hidden = act.shape[1]

    def body(o_ref, a_ref, x_ref, wo_ref, wd_ref, b_ref, *refs):
        out = x_ref[...].astype(f32) + dot(o_ref[...], wo_ref[...], 1, 0) + b_ref[...]
        refs[-1][...] = (out + dot(a_ref[...], wd_ref[...], 1, 0)).astype(bf16)

    def part(cols):
        return pl.BlockSpec((rows, cols), lambda i: (i + first, 0))

    return pl.pallas_call(
        body,
        grid=(count,),
        in_specs=[part(width), part(hidden), part(width), full((width, width)), full((hidden, width)), full((1, width))]
        + [pl.BlockSpec(memory_space=pl.ANY)] * len(keep),
        out_specs=part(width),
        out_shape=jax.ShapeDtypeStruct((total, width), bf16),
        input_output_aliases={6: 0} if keep else {},
        compiler_params=params(),
        name="layer_output",
    )(o, act, x, o_w, down_w, bias, *keep)


def input_gradient(x, g, ghq, ghf, gkv, later, ha, kv_w, vecs, tables, rows, times):
    total, width = x.shape

    def body(x_ref, g_ref, ghq_ref, ghf_ref, gkv_ref, later_ref, ha_ref, w_ref, vec_ref, t_ref, dx_ref, dw_ref, sum_ref, sumkv_ref):
        step = pl.program_id(0)
        lane = lax.broadcasted_iota(jnp.int32, (1, 128), 1)
        pair = gkv_ref[...] + later_ref[...]
        turn = [stacked(t_ref[i], times) for i in range(3)]
        pair = jnp.where(lane < 64, rope(pair, turn[0], -turn[1], -turn[2]), pair).astype(bf16)
        gha = ghq_ref[...] + dot(pair, w_ref[...], 1, 1)
        ghf = ghf_ref[...]
        xhat, inv = standardize(x_ref[...].astype(f32))
        gn = gha * vec_ref[0:1, :] + ghf * vec_ref[2:3, :]
        first = jnp.mean(gn, axis=1, keepdims=True)
        second = jnp.mean(gn * xhat, axis=1, keepdims=True)
        dx_ref[...] = g_ref[...].astype(f32) + inv * (gn - first - xhat * second)
        dw = dot(ha_ref[...], pair, 0, 0)
        sums = jnp.concatenate(
            [jnp.sum(v, axis=0, keepdims=True) for v in (gha * xhat, gha, ghf * xhat, ghf)], axis=0
        )
        sumkv = jnp.sum(pair.astype(f32), axis=0, keepdims=True)

        @pl.when(step == 0)
        def _():
            dw_ref[...] = dw
            sum_ref[...] = sums
            sumkv_ref[...] = sumkv

        @pl.when(step > 0)
        def _():
            dw_ref[...] += dw
            sum_ref[...] += sums
            sumkv_ref[...] += sumkv

    r = rows_of(rows, width)
    n = rows_of(rows, 128)
    return pl.pallas_call(
        body,
        grid=(total // rows,),
        in_specs=[r, r, r, r, n, n, r, full(kv_w.shape), full(vecs.shape), full(tables.shape)],
        out_specs=[r, full((width, 128)), full((4, width)), full((1, 128))],
        out_shape=[
            jax.ShapeDtypeStruct((total, width), f32),
            jax.ShapeDtypeStruct((width, 128), f32),
            jax.ShapeDtypeStruct((4, width), f32),
            jax.ShapeDtypeStruct((1, 128), f32),
        ],
        compiler_params=params(),
        name="input_gradient",
    )(x, g, ghq, ghf, gkv, later, ha, kv_w, vecs, tables)


def bits(size):
    return size.bit_length() - 1


class Reduction:
    def __init__(self, parts, dims, stages, sizes, whole=None):
        self.parts = list(parts)
        self.dims = [list(d) for d in dims]
        self.stages = [list(s) for s in stages]
        self.sizes = sizes
        self.whole = whole
        self.inbox = None

    def left(self):
        return max(len(s) for s in self.stages)

    def launch(self):
        self.inbox = []
        for part, dims, stages in zip(self.parts, self.dims, self.stages):
            axis, which = stages[0]
            size = self.sizes[axis]
            index = lax.axis_index(axis)
            pieces = []
            for code in range(1 << len(which)):
                mask = sum(1 << b for n, b in enumerate(which) if code >> n & 1)
                piece = part
                for place, b in sorted(((dims.index((axis, b)), b) for b in which), reverse=True):
                    bit = ((index ^ mask) >> b) & 1
                    piece = lax.dynamic_index_in_dim(piece, bit, place, keepdims=False)
                if self.whole is not None:
                    self.shape = piece.shape
                    piece = jnp.concatenate([piece.reshape(-1, 128), self.whole], axis=0)
                if mask:
                    piece = lax.ppermute(piece, axis, [(i, i ^ mask) for i in range(size)])
                pieces.append(piece)
            self.inbox.append(pieces)

    def collect(self):
        out = []
        for n, pieces in enumerate(self.inbox):
            axis, which = self.stages[n].pop(0)
            total = sum(p.astype(f32) for p in pieces[1:]) + pieces[0].astype(f32)
            for b in which:
                self.dims[n].remove((axis, b))
            if self.whole is not None:
                count = total.shape[0] - self.whole.shape[0]
                self.whole = total[count:]
                total = total[:count].reshape(self.shape)
                out.append(total)
            else:
                out.append(total.astype(bf16) if self.stages[n] else total)
        self.parts = out
        self.inbox = None

    def run(self):
        while self.left():
            self.launch()
            self.collect()
        return self.parts


def make(mesh):
    seq = mesh.shape["seq"]
    batch = mesh.shape["batch"]

    def shards(
        inputs, lengths, ga, ba, gf, bf, q_w, q_b, kv_w, kv_b, o_w, o_b, up_w, up_b, down_w, down_b, out_grad, later
    ):
        seqs, block, width = inputs.shape
        total = seqs * block
        span = block * seq
        hidden = up_w.shape[1]
        place = lax.axis_index("seq").astype(jnp.int32).reshape(1)
        tables = rope_tables(place[0] * block, block)
        x = inputs.reshape(total, width)
        g = out_grad.reshape(total, width)
        vecs = jnp.stack([ga, ba, gf, bf]).astype(f32)
        rows = 2 * block
        sizes = {"seq": seq, "batch": batch}
        seq_dims = [("seq", b) for b in reversed(range(bits(seq)))]
        all_dims = seq_dims + [("batch", b) for b in reversed(range(bits(batch)))]
        b_bits = [("batch", [b]) for b in range(bits(batch))]
        s_bits = [("seq", [b]) for b in range(bits(seq))]
        order_a = b_bits + s_bits
        order_b = b_bits[:1] + s_bits[:1] + b_bits[1:] + s_bits[1:]
        s_rest = [("seq", list(range(b, min(b + 2, bits(seq))))) for b in range(1, bits(seq), 2)]
        direct = [("batch", list(range(bits(batch))))] + s_bits[:1] + s_rest

        def split_rows(p):
            return p.reshape((2,) * len(all_dims) + (p.shape[0] // (seq * batch),) + p.shape[1:])

        def weights(parts, orders):
            return Reduction([split_rows(p) for p in parts], [all_dims] * len(parts), orders, sizes)

        def fence(first, work):
            flat = [p for r in work for p in r.parts]
            first, flat = lax.optimization_barrier((first, flat))
            for r in work:
                r.parts, flat = flat[: len(r.parts)], flat[len(r.parts) :]
            return first

        def settle(value, work):
            flat = [p for r in work for pieces in r.inbox for p in pieces]
            value, flat = lax.optimization_barrier((value, flat))
            flat = iter(flat)
            for r in work:
                r.inbox = [[next(flat) for _ in pieces] for pieces in r.inbox]
                r.collect()
            return value

        def active(work):
            return [r for r in work if r.left()]

        ha, hf, kv = norm_kv(x, vecs, kv_w, kv_b.astype(f32)[None], tables, rows, 2)
        kv = kv.reshape(seqs, block, 128)
        kv_all = lax.all_gather(kv, "seq", axis=1, tiled=True)
        q, go = query_grad_o(ha, g, q_w, q_b.astype(f32)[None], o_w, tables, rows, 2)
        hf, q, go = lax.optimization_barrier((hf, q, go))
        act, ghf, dwu, dwd, dbu = feed_forward(hf, g, up_w, up_b.astype(f32)[None], down_w, 768, total // 2)
        dwu, dwd, kv_all = lax.optimization_barrier((dwu, dwd, kv_all))
        q = q.reshape(seqs, block, width)
        go = go.reshape(seqs, block, width)
        ffn_sum = weights([dwu, dwd], [order_a, order_b])
        ffn_sum.launch()
        ffn_sum.collect()
        live = fence(lengths[0], [ffn_sum])
        groups = [4, 4, 4, seqs - 12]
        keep = ()
        first = 0
        kv_sums = []
        for count in groups:
            work = active([ffn_sum] + kv_sums)
            for r in work:
                r.launch()
            o, dq, dkv = attention(live, place, q, go, kv_all, tables, first, count, keep, 256)
            o = settle(o, work)
            live = fence(live, work)
            keep = (o, dq)
            first += count
            dkv = dkv.reshape((2,) * bits(seq) + (count, block, 128))
            kv_sums.append(Reduction([dkv], [seq_dims], [s_bits if count > 2 else s_bits[:1] + s_rest], sizes))
        o = o.reshape(total, width)
        dq = dq.reshape(total, width)
        work = active(kv_sums)
        for r in work:
            r.launch()
        ghq, dwo, dwq, early = weight_grads(o, g, ha, dq, q_w, total // 2)
        ghq = settle(ghq, work)
        proj_sum = weights([dwo, dwq], [order_a, order_b])
        proj_sum.launch()
        gkv = jnp.concatenate([r.run()[0] for r in kv_sums], axis=0).reshape(total, 128)
        proj_sum.collect()
        gkv = fence(gkv, [proj_sum])
        proj_sum.launch()
        dx, dwkv, late, sumkv = input_gradient(
            x, g, ghq, ghf, gkv, later.reshape(total, 128), ha, kv_w, vecs, tables, rows, 2
        )
        late = settle(late, [proj_sum])
        vec = jnp.concatenate([early.reshape(-1), dbu.reshape(-1), late.reshape(-1), sumkv.reshape(-1)])
        vec = jnp.pad(vec, (0, -vec.shape[0] % 1024)).reshape(-1, 128)
        kvw_sum = Reduction([split_rows(dwkv)], [all_dims], [direct], sizes, whole=vec)
        bias = (o_b.astype(f32) + down_b.astype(f32))[None]
        bias = fence(bias, [proj_sum, kvw_sum])
        out_rows = total // 7
        out = ()
        for begin, count in ((0, 3), (3, 2), (5, 2)):
            work = active([proj_sum, kvw_sum])
            for r in work:
                r.launch()
            out = (layer_output(o, act, x, o_w, down_w, bias, out_rows, begin, count, out),)
            out = (settle(out[0], work),)
            bias = fence(bias, work)
        (out,) = out
        sum_up, sum_down = ffn_sum.run()
        sum_o, sum_q = proj_sum.run()
        (sum_kv,) = kvw_sum.run()
        vec = kvw_sum.whole.reshape(-1)
        ends = [width, 2 * width, 2 * width + hidden]
        ends += [ends[-1] + width * (i + 1) for i in range(4)]
        sg, sq, su, s0, s1, s2, s3 = [vec[i:j] for i, j in zip([0] + ends[:-1], ends)]
        sk = vec[ends[-1] : ends[-1] + 128]
        return (
            out.reshape(seqs, block, width), kv, dx.reshape(seqs, block, width), s0, s1, s2, s3,
            sum_q, sq, sum_kv, sk, sum_o, sg, sum_up, su, sum_down, sg,
        )

    return shards


def solution(mesh):
    rows = P("batch", "seq", None)
    split = P(("seq", "batch"), None)
    return jax.shard_map(
        make(mesh),
        mesh=mesh,
        in_specs=(rows, P("batch", None)) + (P(),) * 14 + (rows, rows),
        out_specs=(rows, rows, rows, P(), P(), P(), P(), split, P(), split, P(), split, P(), split, P(), split, P()),
        check_vma=False,
    )
```

```python
import functools
import math

import jax
import jax.numpy as jnp
from jax import lax
from jax.experimental import pallas as pl
from jax.experimental.pallas import tpu as pltpu
from jax.sharding import PartitionSpec as P

ROT = 16
EPS = 1e-05
LOG2E = 1.4426950408889634
f32 = jnp.float32
bf16 = jnp.bfloat16
VMEM_LIMIT = 58 << 20


def dot(left, right, left_dim, right_dim):
    return lax.dot_general(
        left, right, (((left_dim,), (right_dim,)), ((), ())), preferred_element_type=f32
    )


def params():
    return pltpu.CompilerParams(
        dimension_semantics=("arbitrary",), vmem_limit_bytes=VMEM_LIMIT
    )


def rope_tables(first, count):
    half = ROT // 2
    lane = jnp.arange(128, dtype=jnp.int32)[None, :] % 64
    frequency = jnp.exp((lane % half).astype(f32) * (-2.0 * math.log(10000.0) / ROT))
    angles = (first + jnp.arange(count, dtype=jnp.int32)).astype(f32)[:, None] * frequency
    main = jnp.where(lane < ROT, jnp.cos(angles), 1.0)
    sin = jnp.sin(angles)
    front = jnp.where(lane < half, -sin, 0.0)
    back = jnp.where((lane >= half) & (lane < ROT), sin, 0.0)
    return jnp.stack([main, front, back])


def rope(x, main, front, back):
    return x * main + pltpu.roll(x, 120, 1) * front + pltpu.roll(x, 8, 1) * back


def stacked(table, times):
    return jnp.concatenate([table] * times, axis=0)


def standardize(x):
    mean = jnp.mean(x, axis=1, keepdims=True)
    centered = x - mean
    inv = lax.rsqrt(jnp.mean(centered * centered, axis=1, keepdims=True) + EPS)
    return centered * inv, inv


def full(shape):
    return pl.BlockSpec(shape, lambda *_: (0,) * len(shape))


def rows_of(rows, width):
    return pl.BlockSpec((rows, width), lambda i, *_: (i, 0))


def norm_kv(x, ga, ba, gf, bf, kv_w, kv_b, tables, rows, times):
    total, width = x.shape

    def body(x_ref, ga_ref, ba_ref, gf_ref, bf_ref, w_ref, b_ref, t_ref, ha_ref, hf_ref, kv_ref):
        xhat, _ = standardize(x_ref[...].astype(f32))
        ha = (xhat * ga_ref[...].astype(f32) + ba_ref[...].astype(f32)).astype(bf16)
        hf_ref[...] = (xhat * gf_ref[...].astype(f32) + bf_ref[...].astype(f32)).astype(bf16)
        ha_ref[...] = ha
        kv = dot(ha, w_ref[...], 1, 0) + b_ref[...].astype(f32)
        lane = lax.broadcasted_iota(jnp.int32, (1, 128), 1)
        turned = rope(kv, *[stacked(t_ref[i], times) for i in range(3)])
        kv_ref[...] = jnp.where(lane < 64, turned, kv).astype(bf16)

    return pl.pallas_call(
        body,
        grid=(total // rows,),
        in_specs=[rows_of(rows, width)] + [full((1, width))] * 4 + [full(kv_w.shape), full(kv_b.shape), full(tables.shape)],
        out_specs=[rows_of(rows, width), rows_of(rows, width), rows_of(rows, 128)],
        out_shape=[
            jax.ShapeDtypeStruct((total, width), bf16),
            jax.ShapeDtypeStruct((total, width), bf16),
            jax.ShapeDtypeStruct((total, 128), bf16),
        ],
        compiler_params=params(),
        name="norm_kv",
    )(x, ga, ba, gf, bf, kv_w, kv_b, tables)


def query_grad_o(ha, g, q_w, q_b, o_w, tables, rows, times):
    total, width = ha.shape

    def body(ha_ref, g_ref, wq_ref, bq_ref, wo_ref, t_ref, q_ref, go_ref):
        q = dot(ha_ref[...], wq_ref[...], 1, 0) + bq_ref[...].astype(f32)
        turn = [stacked(t_ref[i], times) for i in range(3)]
        for c in range(0, width, 128):
            q_ref[:, c : c + 128] = rope(q[:, c : c + 128], *turn).astype(bf16)
        go_ref[...] = dot(g_ref[...], wo_ref[...], 1, 1).astype(bf16)

    return pl.pallas_call(
        body,
        grid=(total // rows,),
        in_specs=[
            rows_of(rows, width), rows_of(rows, width), full(q_w.shape), full(q_b.shape),
            full(o_w.shape), full(tables.shape),
        ],
        out_specs=[rows_of(rows, width), rows_of(rows, width)],
        out_shape=[jax.ShapeDtypeStruct((total, width), bf16)] * 2,
        compiler_params=params(),
        name="query_grad_o",
    )(ha, g, q_w, q_b, o_w, tables)


def gelu_and_slope(u):
    cdf = 0.5 + 0.5 * lax.erf(u * 0.7071067811865476)
    pdf = jnp.exp(u * u * -0.5) * 0.3989422804014327
    return u * cdf, cdf + u * pdf


def feed_forward(h, g, up_w, up_b, down_w, chunk, rows):
    total, width = h.shape
    hidden = up_w.shape[1]

    def body(h_ref, g_ref, wu_ref, bu_ref, wd_ref, act_ref, gh_ref, dwu_ref, dwd_ref, dbu_ref, gup_s):
        @pl.when(pl.program_id(0) == 0)
        def _():
            gh_ref[...] = jnp.zeros_like(gh_ref)

        wu = wu_ref[...]
        wd = wd_ref[...]
        bu = bu_ref[...].astype(f32)

        def block(i, acc):
            sl = pl.ds(pl.multiple_of(i * rows, rows), rows)
            hb = h_ref[sl, :]
            gb = g_ref[sl, :]
            act, slope = gelu_and_slope(dot(hb, wu, 1, 0) + bu)
            act = act.astype(bf16)
            gup = (dot(gb, wd, 1, 1) * slope).astype(bf16)
            act_ref[sl, :] = act
            gup_s[sl, :] = gup
            gh_ref[sl, :] += dot(gup, wu, 1, 1)
            return acc + jnp.sum(gup.astype(f32), axis=0, keepdims=True)

        dbu_ref[...] = lax.fori_loop(0, total // rows, block, jnp.zeros((1, chunk), f32))
        dwu_ref[...] = dot(h_ref[...], gup_s[...], 0, 0).astype(bf16)
        dwd_ref[...] = dot(act_ref[...], g_ref[...], 0, 0).astype(bf16)

    whole = full((total, width))
    cols = pl.BlockSpec((width, chunk), lambda c: (0, c))
    vec = pl.BlockSpec((1, chunk), lambda c: (0, c))
    tall = pl.BlockSpec((chunk, width), lambda c: (c, 0))
    return pl.pallas_call(
        body,
        grid=(hidden // chunk,),
        in_specs=[whole, whole, cols, vec, tall],
        out_specs=[pl.BlockSpec((total, chunk), lambda c: (0, c)), whole, cols, tall, vec],
        out_shape=[
            jax.ShapeDtypeStruct((total, hidden), bf16),
            jax.ShapeDtypeStruct((total, width), f32),
            jax.ShapeDtypeStruct((width, hidden), bf16),
            jax.ShapeDtypeStruct((hidden, width), bf16),
            jax.ShapeDtypeStruct((1, hidden), f32),
        ],
        scratch_shapes=[pltpu.VMEM((total, chunk), bf16)],
        compiler_params=params(),
        name="feed_forward",
    )(h, g, up_w, up_b, down_w)


def attention(lengths, place, q, go, kv, tables, first, count, keep, key_block):
    seqs, block, width = q.shape
    span = kv.shape[1]
    pairs = width // 128

    def body(len_ref, place_ref, q_ref, go_ref, kv_ref, t_ref, *refs):
        o_ref, dq_ref, dkv_ref, dk_acc, dv_acc = refs[-5:]
        live = len_ref[pl.program_id(0) + first]
        start = place_ref[0] * block
        limit = jnp.minimum(live, start + block)
        blocks = (limit + key_block - 1) // key_block
        lane = lax.broadcasted_iota(jnp.int32, (1, 128), 1)
        low = lane < 64
        scale = 0.125

        def branch(number):
            keys = number * key_block
            pair = kv_ref[0, :keys, :].astype(f32)
            swapped = pltpu.roll(pair, 64, 1)
            key_pos = (keys - key_block) + lax.broadcasted_iota(jnp.int32, (block, key_block), 1)
            own_pos = start + lax.broadcasted_iota(jnp.int32, (block, key_block), 0)
            bias = jnp.where((key_pos <= own_pos) & (key_pos < live), 0.0, -1e9).astype(f32)
            bias = stacked(bias, pairs)
            qs = jnp.concatenate([q_ref[0, :, 128 * p : 128 * (p + 1)] for p in range(pairs)], axis=0)
            gs = jnp.concatenate([go_ref[0, :, 128 * p : 128 * (p + 1)] for p in range(pairs)], axis=0)
            gf = gs.astype(f32)

            ke = jnp.where(low, pair, 0.0).astype(bf16)
            ve = jnp.where(low, swapped, 0.0).astype(bf16)
            ko = jnp.where(low, 0.0, swapped).astype(bf16)
            vo = jnp.where(low, 0.0, pair).astype(bf16)

            def scores(k_side):
                s = dot(qs, k_side, 1, 1)
                last = s[:, keys - key_block :] + bias
                return jnp.concatenate([s[:, : keys - key_block], last], axis=1) if number > 1 else last

            def softmax(s):
                top = jnp.max(s, axis=1, keepdims=True)
                expo = jnp.exp2((s - top) * (scale * LOG2E))
                prob = expo * (1.0 / jnp.sum(expo, axis=1, keepdims=True))
                return prob, prob.astype(bf16)

            def slope(prob, o, dp):
                delta = jnp.sum(o * gf, axis=1, keepdims=True)
                return (prob * (dp - delta)).astype(bf16)

            s0, s1 = scores(ke), scores(ko)
            p0, l0 = softmax(s0)
            o0 = dot(l0, ve, 1, 0)
            dp0 = dot(gs, ve, 1, 1)
            p1, l1 = softmax(s1)
            o1 = dot(l1, vo, 1, 0)
            dp1 = dot(gs, vo, 1, 1)
            ds0 = slope(p0, o0, dp0)
            dv_acc[:keys, :] = dot(l0, gs, 0, 0)
            dq0 = dot(ds0, ke, 1, 0)
            dk_acc[:keys, :] = dot(ds0, qs, 0, 0)
            ds1 = slope(p1, o1, dp1)
            dv1 = dot(l1, gs, 0, 0)
            dq1 = dot(ds1, ko, 1, 0)
            dk1 = dot(ds1, qs, 0, 0)
            o = (o0 + o1).astype(bf16)
            dq = (dq0 + dq1) * scale
            turn = [t_ref[0], -t_ref[1], -t_ref[2]]
            for p in range(pairs):
                o_ref[0, :, 128 * p : 128 * (p + 1)] = o[p * block : (p + 1) * block]
                dq_ref[0, :, 128 * p : 128 * (p + 1)] = rope(dq[p * block : (p + 1) * block], *turn).astype(bf16)
            dk = (dk_acc[:keys, :] + pltpu.roll(dk1, 64, 1)) * scale
            dv = dv1 + pltpu.roll(dv_acc[:keys, :], 64, 1)
            dkv_ref[: keys // block, 0] = jnp.where(low, dk, dv).astype(bf16).reshape(keys // block, block, 128)
            if keys < span:
                dkv_ref[keys // block :, 0] = jnp.zeros(((span - keys) // block, block, 128), bf16)

        for number in range(1, span // key_block + 1):
            pl.when(blocks == number)(functools.partial(branch, number))

    row = pl.BlockSpec((1, block, width), lambda s, *_: (s + first, 0, 0))
    kv_in = pl.BlockSpec((1, span, 128), lambda s, *_: (s + first, 0, 0))
    kv_out = pl.BlockSpec((span // block, 1, block, 128), lambda s, *_: (0, s, 0, 0))
    anywhere = pl.BlockSpec(memory_space=pl.ANY)
    return pl.pallas_call(
        body,
        grid_spec=pltpu.PrefetchScalarGridSpec(
            num_scalar_prefetch=2,
            grid=(count,),
            in_specs=[row, row, kv_in, full(tables.shape)] + [anywhere] * len(keep),
            out_specs=[row, row, kv_out],
            scratch_shapes=[pltpu.VMEM((span, 128), f32), pltpu.VMEM((span, 128), f32)],
        ),
        out_shape=[
            jax.ShapeDtypeStruct((seqs, block, width), bf16),
            jax.ShapeDtypeStruct((seqs, block, width), bf16),
            jax.ShapeDtypeStruct((span // block, count, block, 128), bf16),
        ],
        input_output_aliases={6: 0, 7: 1} if keep else {},
        compiler_params=params(),
        name="attention",
    )(lengths, place, q, go, kv, tables, *keep)


def weight_grads(o, g, ha, dq, rows):
    total, width = o.shape

    def body(o_ref, g_ref, ha_ref, dq_ref, dwo_ref, dwq_ref, sum_ref, acc_o, acc_q):
        step = pl.program_id(0)
        gb = g_ref[...]
        dqb = dq_ref[...]
        dwo = dot(o_ref[...], gb, 0, 0)
        dwq = dot(ha_ref[...], dqb, 0, 0)
        sums = jnp.concatenate(
            [jnp.sum(gb.astype(f32), axis=0, keepdims=True), jnp.sum(dqb.astype(f32), axis=0, keepdims=True)], axis=0
        )

        @pl.when(step == 0)
        def _():
            acc_o[...] = dwo
            acc_q[...] = dwq
            sum_ref[...] = sums

        @pl.when(step > 0)
        def _():
            acc_o[...] += dwo
            acc_q[...] += dwq
            sum_ref[...] += sums

        @pl.when(step == total // rows - 1)
        def _():
            dwo_ref[...] = acc_o[...].astype(bf16)
            dwq_ref[...] = acc_q[...].astype(bf16)

    r = rows_of(rows, width)
    square = full((width, width))
    return pl.pallas_call(
        body,
        grid=(total // rows,),
        in_specs=[r, r, r, r],
        out_specs=[square, square, full((2, width))],
        out_shape=[
            jax.ShapeDtypeStruct((width, width), bf16),
            jax.ShapeDtypeStruct((width, width), bf16),
            jax.ShapeDtypeStruct((2, width), f32),
        ],
        scratch_shapes=[pltpu.VMEM((width, width), f32), pltpu.VMEM((width, width), f32)],
        compiler_params=params(),
        name="weight_grads",
    )(o, g, ha, dq)


def layer_output(o, act, x, o_w, down_w, o_b, down_b, rows, first, chunk, keep):
    total, width = o.shape
    hidden = act.shape[1]

    def body(o_ref, a_ref, x_ref, wo_ref, wd_ref, bo_ref, bd_ref, *refs):
        out_ref, acc = refs[-2:]
        step = pl.program_id(0)

        @pl.when(step == 0)
        def _():
            bias = bo_ref[...].astype(f32) + bd_ref[...].astype(f32)
            acc[...] = x_ref[...].astype(f32) + dot(o_ref[...], wo_ref[...], 1, 0) + bias

        acc[...] += dot(a_ref[...], wd_ref[...], 1, 0)

        @pl.when(step == hidden // chunk - 1)
        def _():
            out_ref[...] = acc[...].astype(bf16)

    part = pl.BlockSpec((rows, width), lambda k: (first, 0))
    return pl.pallas_call(
        body,
        grid=(hidden // chunk,),
        in_specs=[
            part,
            pl.BlockSpec((rows, chunk), lambda k: (first, k)),
            part,
            full((width, width)),
            pl.BlockSpec((chunk, width), lambda k: (k, 0)),
            full((1, width)),
            full((1, width)),
        ]
        + [pl.BlockSpec(memory_space=pl.ANY)] * len(keep),
        out_specs=part,
        out_shape=jax.ShapeDtypeStruct((total, width), bf16),
        scratch_shapes=[pltpu.VMEM((rows, width), f32)],
        input_output_aliases={7: 0} if keep else {},
        compiler_params=params(),
        name="layer_output",
    )(o, act, x, o_w, down_w, o_b, down_b, *keep)


def input_gradient(x, g, dq, q_w, ghf, gkv, later, ha, kv_w, ga, gf, tables, rows, times, first, keep):
    total, width = x.shape

    def body(*refs):
        x_ref, g_ref, dq_ref, wq_ref, ghf_ref, gkv_ref, later_ref, ha_ref, w_ref, ga_ref, gf_ref, t_ref = refs[:12]
        dx_ref, dw_ref, sum_ref, sumkv_ref = refs[-4:]
        step = pl.program_id(0)
        lane = lax.broadcasted_iota(jnp.int32, (1, 128), 1)
        pair = gkv_ref[...] + later_ref[...]
        turn = [stacked(t_ref[i], times) for i in range(3)]
        pair = jnp.where(lane < 64, rope(pair, turn[0], -turn[1], -turn[2]), pair).astype(bf16)
        gha = dot(dq_ref[...], wq_ref[...], 1, 1) + dot(pair, w_ref[...], 1, 1)
        ghf = ghf_ref[...]
        xhat, inv = standardize(x_ref[...].astype(f32))
        gn = gha * ga_ref[...].astype(f32) + ghf * gf_ref[...].astype(f32)
        mean = jnp.mean(gn, axis=1, keepdims=True)
        second = jnp.mean(gn * xhat, axis=1, keepdims=True)
        dx_ref[...] = g_ref[...].astype(f32) + inv * (gn - mean - xhat * second)
        dw = dot(ha_ref[...], pair, 0, 0)
        sums = jnp.concatenate(
            [jnp.sum(v, axis=0, keepdims=True) for v in (gha * xhat, gha, ghf * xhat, ghf)], axis=0
        )
        sumkv = jnp.sum(pair.astype(f32), axis=0, keepdims=True)

        @pl.when(step == 0)
        def _():
            if keep:
                dw_ref[...] = dw + refs[13][...]
                sum_ref[...] = sums + refs[14][...]
                sumkv_ref[...] = sumkv + refs[15][...]
            else:
                dw_ref[...] = dw
                sum_ref[...] = sums
                sumkv_ref[...] = sumkv

        @pl.when(step > 0)
        def _():
            dw_ref[...] += dw
            sum_ref[...] += sums
            sumkv_ref[...] += sumkv

    r = pl.BlockSpec((rows, width), lambda i: (i + first, 0))
    n = pl.BlockSpec((rows, 128), lambda i: (i + first, 0))
    own = pl.BlockSpec((rows, 128), lambda i: (i, 0))
    vec = full((1, width))
    small = [full((width, 128)), full((4, width)), full((1, 128))]
    return pl.pallas_call(
        body,
        grid=(gkv.shape[0] // rows,),
        in_specs=[r, r, r, full((width, width)), r, own, n, r, full(kv_w.shape), vec, vec, full(tables.shape)]
        + ([pl.BlockSpec(memory_space=pl.ANY)] + small if keep else []),
        out_specs=[r] + small,
        out_shape=[
            jax.ShapeDtypeStruct((total, width), f32),
            jax.ShapeDtypeStruct((width, 128), f32),
            jax.ShapeDtypeStruct((4, width), f32),
            jax.ShapeDtypeStruct((1, 128), f32),
        ],
        input_output_aliases={12: 0} if keep else {},
        compiler_params=params(),
        name="input_gradient",
    )(x, g, dq, q_w, ghf, gkv, later, ha, kv_w, ga, gf, tables, *keep)


def bits(size):
    return size.bit_length() - 1


class Reduction:
    def __init__(self, parts, dims, stages, sizes, whole=None):
        self.parts = list(parts)
        self.dims = [list(d) for d in dims]
        self.stages = [list(s) for s in stages]
        self.sizes = sizes
        self.whole = whole
        self.inbox = None

    def left(self):
        return max(len(s) for s in self.stages)

    def launch(self):
        self.inbox = []
        for part, dims, stages in zip(self.parts, self.dims, self.stages):
            axis, which = stages[0]
            size = self.sizes[axis]
            index = lax.axis_index(axis)
            pieces = []
            for code in range(1 << len(which)):
                mask = sum(1 << b for n, b in enumerate(which) if code >> n & 1)
                piece = part
                for place, b in sorted(((dims.index((axis, b)), b) for b in which), reverse=True):
                    bit = ((index ^ mask) >> b) & 1
                    piece = lax.dynamic_index_in_dim(piece, bit, place, keepdims=False)
                if self.whole is not None:
                    self.shape = piece.shape
                    piece = jnp.concatenate([piece.reshape(-1, 128), self.whole], axis=0)
                if mask:
                    piece = lax.ppermute(piece, axis, [(i, i ^ mask) for i in range(size)])
                pieces.append(piece)
            self.inbox.append(pieces)

    def collect(self):
        out = []
        for n, pieces in enumerate(self.inbox):
            axis, which = self.stages[n].pop(0)
            total = sum(p.astype(f32) for p in pieces[1:]) + pieces[0].astype(f32)
            for b in which:
                self.dims[n].remove((axis, b))
            if self.whole is not None:
                count = total.shape[0] - self.whole.shape[0]
                self.whole = total[count:]
                total = total[:count].reshape(self.shape)
                out.append(total)
            else:
                out.append(total.astype(bf16) if self.stages[n] else total)
        self.parts = out
        self.inbox = None

    def run(self):
        if self.inbox:
            self.collect()
        while self.left():
            self.launch()
            self.collect()
        return self.parts


def make(mesh):
    seq = mesh.shape["seq"]
    batch = mesh.shape["batch"]

    def shards(
        inputs, lengths, ga, ba, gf, bf, q_w, q_b, kv_w, kv_b, o_w, o_b, up_w, up_b, down_w, down_b, out_grad, later
    ):
        seqs, block, width = inputs.shape
        total = seqs * block
        span = block * seq
        hidden = up_w.shape[1]
        place = lax.axis_index("seq").astype(jnp.int32).reshape(1)
        tables = rope_tables(place[0] * block, block)
        x = inputs.reshape(total, width)
        g = out_grad.reshape(total, width)
        ga, ba, gf, bf, q_b, kv_b, o_b, up_b, down_b = [
            v.reshape(1, -1) for v in (ga, ba, gf, bf, q_b, kv_b, o_b, up_b, down_b)
        ]
        rows = 2 * block
        sizes = {"seq": seq, "batch": batch}
        seq_dims = [("seq", b) for b in reversed(range(bits(seq)))]
        all_dims = seq_dims + [("batch", b) for b in reversed(range(bits(batch)))]
        b_bits = [("batch", [b]) for b in range(bits(batch))]
        s_bits = [("seq", [b]) for b in range(bits(seq))]
        order_a = b_bits + s_bits
        order_b = b_bits[:1] + s_bits[:1] + b_bits[1:] + s_bits[1:]
        s_rest = [("seq", list(range(b, min(b + 2, bits(seq))))) for b in range(1, bits(seq), 2)]
        direct = [("batch", list(range(bits(batch))))] + s_bits[:1] + s_rest

        def split_rows(p):
            return p.reshape((2,) * len(all_dims) + (p.shape[0] // (seq * batch),) + p.shape[1:])

        def weights(parts, orders):
            return Reduction([split_rows(p) for p in parts], [all_dims] * len(parts), orders, sizes)

        def fence(first, work):
            flat = [p for r in work for p in r.parts]
            first, flat = lax.optimization_barrier((first, flat))
            for r in work:
                r.parts, flat = flat[: len(r.parts)], flat[len(r.parts) :]
            return first

        def settle(value, work):
            work = [r for r in work if r.inbox]
            flat = [p for r in work for pieces in r.inbox for p in pieces]
            value, flat = lax.optimization_barrier((value, flat))
            flat = iter(flat)
            for r in work:
                r.inbox = [[next(flat) for _ in pieces] for pieces in r.inbox]
                r.collect()
            return value

        def active(work):
            return [r for r in work if r.left()]

        ha, hf, kv = norm_kv(x, ga, ba, gf, bf, kv_w, kv_b, tables, rows, 2)
        kv = kv.reshape(seqs, block, 128)
        kv_all = lax.all_gather(kv, "seq", axis=1, tiled=True)
        q, go = query_grad_o(ha, g, q_w, q_b, o_w, tables, rows, 2)
        hf, q, go = lax.optimization_barrier((hf, q, go))
        act, ghf, dwu, dwd, dbu = feed_forward(hf, g, up_w, up_b, down_w, 768, total // 2)
        dwu, dwd, kv_all = lax.optimization_barrier((dwu, dwd, kv_all))
        q = q.reshape(seqs, block, width)
        go = go.reshape(seqs, block, width)
        ffn_sum = weights([dwu, dwd], [order_a, order_b])
        ffn_sum.launch()
        ffn_sum.collect()
        live = fence(lengths[0], [ffn_sum])
        groups = [4, 4, 4, seqs - 12]
        keep = ()
        first = 0
        kv_sums = []
        for count in groups:
            work = active([ffn_sum] + kv_sums)
            for r in work:
                r.launch()
            o, dq, dkv = attention(live, place, q, go, kv_all, tables, first, count, keep, 256)
            o = settle(o, work)
            live = fence(live, work)
            keep = (o, dq)
            first += count
            dkv = dkv.reshape((2,) * bits(seq) + (count, block, 128))
            kv_sums.append(Reduction([dkv], [seq_dims], [s_bits if first <= 8 else s_bits[:1] + s_rest], sizes))
        o = o.reshape(total, width)
        dq = dq.reshape(total, width)
        work = active(kv_sums)
        for r in work:
            r.launch()
        dwo, dwq, early = weight_grads(o, g, ha, dq, total // 2)
        proj_sum = weights([dwo, dwq], [order_a, order_b])
        proj_sum.launch()
        later = later.reshape(total, 128)

        def gradient_of(part, begin, keep):
            part = jnp.concatenate([p.run()[0] for p in part], axis=0).reshape(-1, 128)
            return input_gradient(
                x, g, dq, q_w, ghf, part, later, ha, kv_w, ga, gf, tables, rows, 2, begin * block // rows, keep
            )

        grads = gradient_of(kv_sums[:1], 0, ())
        grads = settle(grads, work + [proj_sum])
        work = active(kv_sums) + [proj_sum]
        for r in work:
            r.launch()
        grads = gradient_of(kv_sums[1:3], groups[0], tuple(grads))
        grads = settle(grads, work)
        proj_sum.launch()
        dx, dwkv, late, sumkv = gradient_of(kv_sums[3:], seqs - groups[3], tuple(grads))
        vec = jnp.concatenate([early.reshape(-1), dbu.reshape(-1), late.reshape(-1), sumkv.reshape(-1)])
        vec = jnp.pad(vec, (0, -vec.shape[0] % 1024)).reshape(-1, 128)
        kvw_sum = Reduction([split_rows(dwkv)], [all_dims], [direct], sizes, whole=vec)
        bias = fence(o_b, [kvw_sum])
        out = ()
        for part, begin in ((2, 0), (4, 2), (4, 3)):
            work = active([proj_sum, kvw_sum])
            for r in work:
                if not r.inbox:
                    r.launch()
            out = (layer_output(o, act, x, o_w, down_w, bias, down_b, total // part, begin, width, out),)
            out = (settle(out[0], work),)
            bias = fence(bias, work)
        (out,) = out
        sum_up, sum_down = ffn_sum.run()
        sum_o, sum_q = proj_sum.run()
        (sum_kv,) = kvw_sum.run()
        vec = kvw_sum.whole.reshape(-1)
        ends = [width, 2 * width, 2 * width + hidden]
        ends += [ends[-1] + width * (i + 1) for i in range(4)]
        sg, sq, su, s0, s1, s2, s3 = [vec[i:j] for i, j in zip([0] + ends[:-1], ends)]
        sk = vec[ends[-1] : ends[-1] + 128]
        return (
            out.reshape(seqs, block, width), kv, dx.reshape(seqs, block, width), s0, s1, s2, s3,
            sum_q, sq, sum_kv, sk, sum_o, sg, sum_up, su, sum_down, sg,
        )

    return shards


def solution(mesh):
    rows = P("batch", "seq", None)
    split = P(("seq", "batch"), None)
    return jax.shard_map(
        make(mesh),
        mesh=mesh,
        in_specs=(rows, P("batch", None)) + (P(),) * 14 + (rows, rows),
        out_specs=(rows, rows, rows, P(), P(), P(), P(), split, P(), split, P(), split, P(), split, P(), split, P()),
        check_vma=False,
    )
```

```python
import functools
import math

import jax
import jax.numpy as jnp
from jax import lax
from jax.experimental import pallas as pl
from jax.experimental.pallas import tpu as pltpu
from jax.sharding import PartitionSpec as P

ROT = 16
EPS = 1e-05
LOG2E = 1.4426950408889634
f32 = jnp.float32
bf16 = jnp.bfloat16
VMEM_LIMIT = 58 << 20


def dot(left, right, left_dim, right_dim):
    return lax.dot_general(
        left, right, (((left_dim,), (right_dim,)), ((), ())), preferred_element_type=f32
    )


def params():
    return pltpu.CompilerParams(
        dimension_semantics=("arbitrary",), vmem_limit_bytes=VMEM_LIMIT
    )


def rope_tables(first, count):
    half = ROT // 2
    lane = jnp.arange(128, dtype=jnp.int32)[None, :] % 64
    frequency = jnp.exp((lane % half).astype(f32) * (-2.0 * math.log(10000.0) / ROT))
    angles = (first + jnp.arange(count, dtype=jnp.int32)).astype(f32)[:, None] * frequency
    main = jnp.where(lane < ROT, jnp.cos(angles), 1.0)
    sin = jnp.sin(angles)
    front = jnp.where(lane < half, -sin, 0.0)
    back = jnp.where((lane >= half) & (lane < ROT), sin, 0.0)
    return jnp.stack([main, front, back])


def rope(x, main, front, back):
    return x * main + pltpu.roll(x, 120, 1) * front + pltpu.roll(x, 8, 1) * back


def stacked(table, times):
    return jnp.concatenate([table] * times, axis=0)


def standardize(x):
    mean = jnp.mean(x, axis=1, keepdims=True)
    centered = x - mean
    inv = lax.rsqrt(jnp.mean(centered * centered, axis=1, keepdims=True) + EPS)
    return centered * inv, inv


def full(shape):
    return pl.BlockSpec(shape, lambda *_: (0,) * len(shape))


def rows_of(rows, width):
    return pl.BlockSpec((rows, width), lambda i, *_: (i, 0))


def norm_kv(x, ga, ba, gf, bf, kv_w, kv_b, tables, rows, times):
    total, width = x.shape

    def body(x_ref, ga_ref, ba_ref, gf_ref, bf_ref, w_ref, b_ref, t_ref, ha_ref, hf_ref, kv_ref):
        xhat, _ = standardize(x_ref[...].astype(f32))
        ha = (xhat * ga_ref[...].astype(f32) + ba_ref[...].astype(f32)).astype(bf16)
        hf_ref[...] = (xhat * gf_ref[...].astype(f32) + bf_ref[...].astype(f32)).astype(bf16)
        ha_ref[...] = ha
        kv = dot(ha, w_ref[...], 1, 0) + b_ref[...].astype(f32)
        lane = lax.broadcasted_iota(jnp.int32, (1, 128), 1)
        turned = rope(kv, *[stacked(t_ref[i], times) for i in range(3)])
        kv_ref[...] = jnp.where(lane < 64, turned, kv).astype(bf16)

    return pl.pallas_call(
        body,
        grid=(total // rows,),
        in_specs=[rows_of(rows, width)] + [full((1, width))] * 4 + [full(kv_w.shape), full(kv_b.shape), full(tables.shape)],
        out_specs=[rows_of(rows, width), rows_of(rows, width), rows_of(rows, 128)],
        out_shape=[
            jax.ShapeDtypeStruct((total, width), bf16),
            jax.ShapeDtypeStruct((total, width), bf16),
            jax.ShapeDtypeStruct((total, 128), bf16),
        ],
        compiler_params=params(),
        name="norm_kv",
    )(x, ga, ba, gf, bf, kv_w, kv_b, tables)


def query_grad_o(ha, g, q_w, q_b, o_w, tables, rows, times):
    total, width = ha.shape

    def body(ha_ref, g_ref, wq_ref, bq_ref, wo_ref, t_ref, q_ref, go_ref):
        q = dot(ha_ref[...], wq_ref[...], 1, 0) + bq_ref[...].astype(f32)
        turn = [stacked(t_ref[i], times) for i in range(3)]
        for c in range(0, width, 128):
            q_ref[:, c : c + 128] = rope(q[:, c : c + 128], *turn).astype(bf16)
        go_ref[...] = dot(g_ref[...], wo_ref[...], 1, 1).astype(bf16)

    return pl.pallas_call(
        body,
        grid=(total // rows,),
        in_specs=[
            rows_of(rows, width), rows_of(rows, width), full(q_w.shape), full(q_b.shape),
            full(o_w.shape), full(tables.shape),
        ],
        out_specs=[rows_of(rows, width), rows_of(rows, width)],
        out_shape=[jax.ShapeDtypeStruct((total, width), bf16)] * 2,
        compiler_params=params(),
        name="query_grad_o",
    )(ha, g, q_w, q_b, o_w, tables)


def gelu_and_slope(u):
    cdf = 0.5 + 0.5 * lax.erf(u * 0.7071067811865476)
    pdf = jnp.exp(u * u * -0.5) * 0.3989422804014327
    return u * cdf, cdf + u * pdf


def feed_forward(h, g, up_w, up_b, down_w, chunk, rows, bit, owners):
    total, width = h.shape
    hidden = up_w.shape[1]

    up_rows, down_rows = width // owners, hidden // owners
    split = up_rows % 8 == 0 and chunk % (2 * down_rows) == 0
    down_owners = chunk // down_rows

    def body(bit_ref, h_ref, g_ref, wu_ref, bu_ref, wd_ref, act_ref, gh_ref, dbu_ref, *refs):
        gup_s = refs[-1]

        @pl.when(pl.program_id(0) == 0)
        def _():
            gh_ref[...] = jnp.zeros_like(gh_ref)

        wu = wu_ref[...]
        wd = wd_ref[...]
        bu = bu_ref[...].astype(f32)

        def block(i, acc):
            sl = pl.ds(pl.multiple_of(i * rows, rows), rows)
            hb = h_ref[sl, :]
            gb = g_ref[sl, :]
            act, slope = gelu_and_slope(dot(hb, wu, 1, 0) + bu)
            act = act.astype(bf16)
            gup = (dot(gb, wd, 1, 1) * slope).astype(bf16)
            act_ref[sl, :] = act
            gup_s[sl, :] = gup
            gh_ref[sl, :] += dot(gup, wu, 1, 1)
            return acc + jnp.sum(gup.astype(f32), axis=0, keepdims=True)

        dbu_ref[...] = lax.fori_loop(0, total // rows, block, jnp.zeros((1, chunk), f32))
        dwu = dot(h_ref[...], gup_s[...], 0, 0)
        if split:
            up_s, down_s = refs[4:6]
            up_s[...] = dwu.reshape(up_s.shape)
            down_s[...] = dot(act_ref[...], g_ref[...], 0, 0).reshape(down_s.shape)
            part_out(up_s, refs[0], refs[1], bit_ref[0])
            part_out(down_s, refs[2], refs[3], bit_ref[0])
        else:
            refs[0][...] = dwu.astype(bf16)
            refs[1][...] = dot(act_ref[...], g_ref[...], 0, 0).astype(bf16)

    whole = full((total, width))
    cols = pl.BlockSpec((width, chunk), lambda c, *_: (0, c))
    vec = pl.BlockSpec((1, chunk), lambda c, *_: (0, c))
    tall = pl.BlockSpec((chunk, width), lambda c, *_: (c, 0))
    if split:
        up_half = pl.BlockSpec((owners // 2, up_rows, chunk), lambda c, *_: (0, 0, c))
        down_half = pl.BlockSpec((down_owners // 2, down_rows, width), lambda c, *_: (c, 0, 0))
        weight_specs = [up_half, up_half, down_half, down_half]
        weight_shapes = [jax.ShapeDtypeStruct((owners // 2, up_rows, hidden), bf16)] * 2
        weight_shapes += [jax.ShapeDtypeStruct((owners // 2, down_rows, width), bf16)] * 2
        scratch = [
            pltpu.VMEM((owners // 2, 2, up_rows, chunk), f32),
            pltpu.VMEM((down_owners // 2, 2, down_rows, width), f32),
        ]
    else:
        weight_specs = [cols, tall]
        weight_shapes = [jax.ShapeDtypeStruct((width, hidden), bf16), jax.ShapeDtypeStruct((hidden, width), bf16)]
        scratch = []
    return pl.pallas_call(
        body,
        grid_spec=pltpu.PrefetchScalarGridSpec(
            num_scalar_prefetch=1,
            grid=(hidden // chunk,),
            in_specs=[whole, whole, cols, vec, tall],
            out_specs=[pl.BlockSpec((total, chunk), lambda c, *_: (0, c)), whole, vec] + weight_specs,
            scratch_shapes=scratch + [pltpu.VMEM((total, chunk), bf16)],
        ),
        out_shape=[
            jax.ShapeDtypeStruct((total, hidden), bf16),
            jax.ShapeDtypeStruct((total, width), f32),
            jax.ShapeDtypeStruct((1, hidden), f32),
        ]
        + weight_shapes,
        compiler_params=params(),
        name="feed_forward",
    )(bit, h, g, up_w, up_b, down_w)


def part_out(source, own, other, bit):
    def one(i, _):
        own[i] = source[i, bit].astype(bf16)
        other[i] = source[i, 1 - bit].astype(bf16)
        return 0

    lax.fori_loop(0, source.shape[0], one, 0)


def attention(lengths, place, q, go, kv, tables, first, count, keep, key_block):
    seqs, block, width = q.shape
    span = kv.shape[1]
    pairs = width // 128

    def body(len_ref, place_ref, q_ref, go_ref, kv_ref, t_ref, *refs):
        o_ref, dq_ref, dkv_ref, dk_acc, dv_acc = refs[-5:]
        live = len_ref[pl.program_id(0) + first]
        start = place_ref[0] * block
        limit = jnp.minimum(live, start + block)
        blocks = (limit + key_block - 1) // key_block
        lane = lax.broadcasted_iota(jnp.int32, (1, 128), 1)
        low = lane < 64
        scale = 0.125

        def branch(number):
            keys = number * key_block
            pair = kv_ref[0, :keys, :].astype(f32)
            swapped = pltpu.roll(pair, 64, 1)
            key_pos = (keys - key_block) + lax.broadcasted_iota(jnp.int32, (block, key_block), 1)
            own_pos = start + lax.broadcasted_iota(jnp.int32, (block, key_block), 0)
            bias = jnp.where((key_pos <= own_pos) & (key_pos < live), 0.0, -1e9).astype(f32)
            bias = stacked(bias, pairs)
            qs = jnp.concatenate([q_ref[0, :, 128 * p : 128 * (p + 1)] for p in range(pairs)], axis=0)
            gs = jnp.concatenate([go_ref[0, :, 128 * p : 128 * (p + 1)] for p in range(pairs)], axis=0)
            gf = gs.astype(f32)

            ke = jnp.where(low, pair, 0.0).astype(bf16)
            ve = jnp.where(low, swapped, 0.0).astype(bf16)
            ko = jnp.where(low, 0.0, swapped).astype(bf16)
            vo = jnp.where(low, 0.0, pair).astype(bf16)

            def scores(k_side):
                s = dot(qs, k_side, 1, 1)
                last = s[:, keys - key_block :] + bias
                return jnp.concatenate([s[:, : keys - key_block], last], axis=1) if number > 1 else last

            def softmax(s):
                top = jnp.max(s, axis=1, keepdims=True)
                expo = jnp.exp2((s - top) * (scale * LOG2E))
                prob = expo * (1.0 / jnp.sum(expo, axis=1, keepdims=True))
                return prob, prob.astype(bf16)

            def slope(prob, o, dp):
                delta = jnp.sum(o * gf, axis=1, keepdims=True)
                return (prob * (dp - delta)).astype(bf16)

            s0, s1 = scores(ke), scores(ko)
            p0, l0 = softmax(s0)
            o0 = dot(l0, ve, 1, 0)
            dp0 = dot(gs, ve, 1, 1)
            p1, l1 = softmax(s1)
            o1 = dot(l1, vo, 1, 0)
            dp1 = dot(gs, vo, 1, 1)
            ds0 = slope(p0, o0, dp0)
            dv_acc[:keys, :] = dot(l0, gs, 0, 0)
            dq0 = dot(ds0, ke, 1, 0)
            dk_acc[:keys, :] = dot(ds0, qs, 0, 0)
            ds1 = slope(p1, o1, dp1)
            dv1 = dot(l1, gs, 0, 0)
            dq1 = dot(ds1, ko, 1, 0)
            dk1 = dot(ds1, qs, 0, 0)
            o = (o0 + o1).astype(bf16)
            dq = (dq0 + dq1) * scale
            turn = [t_ref[0], -t_ref[1], -t_ref[2]]
            for p in range(pairs):
                o_ref[0, :, 128 * p : 128 * (p + 1)] = o[p * block : (p + 1) * block]
                dq_ref[0, :, 128 * p : 128 * (p + 1)] = rope(dq[p * block : (p + 1) * block], *turn).astype(bf16)
            dk = (dk_acc[:keys, :] + pltpu.roll(dk1, 64, 1)) * scale
            dv = dv1 + pltpu.roll(dv_acc[:keys, :], 64, 1)
            dkv_ref[: keys // block, 0] = jnp.where(low, dk, dv).astype(bf16).reshape(keys // block, block, 128)
            if keys < span:
                dkv_ref[keys // block :, 0] = jnp.zeros(((span - keys) // block, block, 128), bf16)

        for number in range(1, span // key_block + 1):
            pl.when(blocks == number)(functools.partial(branch, number))

    row = pl.BlockSpec((1, block, width), lambda s, *_: (s + first, 0, 0))
    kv_in = pl.BlockSpec((1, span, 128), lambda s, *_: (s + first, 0, 0))
    kv_out = pl.BlockSpec((span // block, 1, block, 128), lambda s, *_: (0, s, 0, 0))
    anywhere = pl.BlockSpec(memory_space=pl.ANY)
    return pl.pallas_call(
        body,
        grid_spec=pltpu.PrefetchScalarGridSpec(
            num_scalar_prefetch=2,
            grid=(count,),
            in_specs=[row, row, kv_in, full(tables.shape)] + [anywhere] * len(keep),
            out_specs=[row, row, kv_out],
            scratch_shapes=[pltpu.VMEM((span, 128), f32), pltpu.VMEM((span, 128), f32)],
        ),
        out_shape=[
            jax.ShapeDtypeStruct((seqs, block, width), bf16),
            jax.ShapeDtypeStruct((seqs, block, width), bf16),
            jax.ShapeDtypeStruct((span // block, count, block, 128), bf16),
        ],
        input_output_aliases={6: 0, 7: 1} if keep else {},
        compiler_params=params(),
        name="attention",
    )(lengths, place, q, go, kv, tables, *keep)


def weight_grads(o, g, ha, dq, rows, bit, owners):
    total, width = o.shape
    part = width // owners
    split = part % 8 == 0
    shape = (owners // 2, 2, part, width) if split else (width, width)

    def body(bit_ref, o_ref, g_ref, ha_ref, dq_ref, sum_ref, *refs):
        acc_o, acc_q = refs[-2:]
        step = pl.program_id(0)
        gb = g_ref[...]
        dqb = dq_ref[...]
        dwo = dot(o_ref[...], gb, 0, 0).reshape(shape)
        dwq = dot(ha_ref[...], dqb, 0, 0).reshape(shape)
        sums = jnp.concatenate(
            [jnp.sum(gb.astype(f32), axis=0, keepdims=True), jnp.sum(dqb.astype(f32), axis=0, keepdims=True)], axis=0
        )

        @pl.when(step == 0)
        def _():
            acc_o[...] = dwo
            acc_q[...] = dwq
            sum_ref[...] = sums

        @pl.when(step > 0)
        def _():
            acc_o[...] += dwo
            acc_q[...] += dwq
            sum_ref[...] += sums

        @pl.when(step == total // rows - 1)
        def _():
            if split:
                part_out(acc_o, refs[0], refs[1], bit_ref[0])
                part_out(acc_q, refs[2], refs[3], bit_ref[0])
            else:
                refs[0][...] = acc_o[...].astype(bf16)
                refs[1][...] = acc_q[...].astype(bf16)

    r = rows_of(rows, width)
    out = (owners // 2, part, width) if split else (width, width)
    number = 4 if split else 2
    return pl.pallas_call(
        body,
        grid_spec=pltpu.PrefetchScalarGridSpec(
            num_scalar_prefetch=1,
            grid=(total // rows,),
            in_specs=[r, r, r, r],
            out_specs=[full((2, width))] + [full(out)] * number,
            scratch_shapes=[pltpu.VMEM(shape, f32), pltpu.VMEM(shape, f32)],
        ),
        out_shape=[jax.ShapeDtypeStruct((2, width), f32)] + [jax.ShapeDtypeStruct(out, bf16)] * number,
        compiler_params=params(),
        name="weight_grads",
    )(bit, o, g, ha, dq)


def layer_output(o, act, x, o_w, down_w, o_b, down_b, rows, first, chunk, keep):
    total, width = o.shape
    hidden = act.shape[1]

    def body(o_ref, a_ref, x_ref, wo_ref, wd_ref, bo_ref, bd_ref, *refs):
        out_ref, acc = refs[-2:]
        step = pl.program_id(0)

        @pl.when(step == 0)
        def _():
            bias = bo_ref[...].astype(f32) + bd_ref[...].astype(f32)
            acc[...] = x_ref[...].astype(f32) + dot(o_ref[...], wo_ref[...], 1, 0) + bias

        acc[...] += dot(a_ref[...], wd_ref[...], 1, 0)

        @pl.when(step == hidden // chunk - 1)
        def _():
            out_ref[...] = acc[...].astype(bf16)

    part = pl.BlockSpec((rows, width), lambda k: (first, 0))
    return pl.pallas_call(
        body,
        grid=(hidden // chunk,),
        in_specs=[
            part,
            pl.BlockSpec((rows, chunk), lambda k: (first, k)),
            part,
            full((width, width)),
            pl.BlockSpec((chunk, width), lambda k: (k, 0)),
            full((1, width)),
            full((1, width)),
        ]
        + [pl.BlockSpec(memory_space=pl.ANY)] * len(keep),
        out_specs=part,
        out_shape=jax.ShapeDtypeStruct((total, width), bf16),
        scratch_shapes=[pltpu.VMEM((rows, width), f32)],
        input_output_aliases={7: 0} if keep else {},
        compiler_params=params(),
        name="layer_output",
    )(o, act, x, o_w, down_w, o_b, down_b, *keep)


def input_gradient(x, g, dq, q_w, ghf, gkv, later, ha, kv_w, ga, gf, tables, rows, times, first, keep):
    total, width = x.shape

    def body(*refs):
        x_ref, g_ref, dq_ref, wq_ref, ghf_ref, gkv_ref, later_ref, ha_ref, w_ref, ga_ref, gf_ref, t_ref = refs[:12]
        dx_ref, dw_ref, sum_ref, sumkv_ref = refs[-4:]
        step = pl.program_id(0)
        lane = lax.broadcasted_iota(jnp.int32, (1, 128), 1)
        pair = gkv_ref[...] + later_ref[...]
        turn = [stacked(t_ref[i], times) for i in range(3)]
        pair = jnp.where(lane < 64, rope(pair, turn[0], -turn[1], -turn[2]), pair).astype(bf16)
        gha = dot(dq_ref[...], wq_ref[...], 1, 1) + dot(pair, w_ref[...], 1, 1)
        ghf = ghf_ref[...]
        xhat, inv = standardize(x_ref[...].astype(f32))
        gn = gha * ga_ref[...].astype(f32) + ghf * gf_ref[...].astype(f32)
        mean = jnp.mean(gn, axis=1, keepdims=True)
        second = jnp.mean(gn * xhat, axis=1, keepdims=True)
        dx_ref[...] = g_ref[...].astype(f32) + inv * (gn - mean - xhat * second)
        dw = dot(ha_ref[...], pair, 0, 0)
        sums = jnp.concatenate(
            [jnp.sum(v, axis=0, keepdims=True) for v in (gha * xhat, gha, ghf * xhat, ghf)], axis=0
        )
        sumkv = jnp.sum(pair.astype(f32), axis=0, keepdims=True)

        @pl.when(step == 0)
        def _():
            if keep:
                dw_ref[...] = dw + refs[13][...]
                sum_ref[...] = sums + refs[14][...]
                sumkv_ref[...] = sumkv + refs[15][...]
            else:
                dw_ref[...] = dw
                sum_ref[...] = sums
                sumkv_ref[...] = sumkv

        @pl.when(step > 0)
        def _():
            dw_ref[...] += dw
            sum_ref[...] += sums
            sumkv_ref[...] += sumkv

    r = pl.BlockSpec((rows, width), lambda i: (i + first, 0))
    n = pl.BlockSpec((rows, 128), lambda i: (i + first, 0))
    own = pl.BlockSpec((rows, 128), lambda i: (i, 0))
    vec = full((1, width))
    small = [full((width, 128)), full((4, width)), full((1, 128))]
    return pl.pallas_call(
        body,
        grid=(gkv.shape[0] // rows,),
        in_specs=[r, r, r, full((width, width)), r, own, n, r, full(kv_w.shape), vec, vec, full(tables.shape)]
        + ([pl.BlockSpec(memory_space=pl.ANY)] + small if keep else []),
        out_specs=[r] + small,
        out_shape=[
            jax.ShapeDtypeStruct((total, width), f32),
            jax.ShapeDtypeStruct((width, 128), f32),
            jax.ShapeDtypeStruct((4, width), f32),
            jax.ShapeDtypeStruct((1, 128), f32),
        ],
        input_output_aliases={12: 0} if keep else {},
        compiler_params=params(),
        name="input_gradient",
    )(x, g, dq, q_w, ghf, gkv, later, ha, kv_w, ga, gf, tables, *keep)


def bits(size):
    return size.bit_length() - 1


def combine(items):
    digits = jnp.stack([jnp.zeros((), jnp.int32) if d is None else d.astype(jnp.int32) for _, d in items])
    flat = [p for ops, _ in items for p in ops]
    shapes, counts = [], []
    for ops, digit in items:
        shape = ops[0].shape
        if digit is None:
            shapes.append(jax.ShapeDtypeStruct(shape, f32))
            counts.append(1)
        else:
            counts.append(shape[1])
            shapes += [jax.ShapeDtypeStruct((shape[0], shape[2]) + shape[3:], bf16)] * shape[1]

    def body(digit_ref, *refs):
        ins, outs = list(refs[: len(flat)]), list(refs[len(flat) :])
        for n, (ops, digit) in enumerate(items):
            mine, ins = ins[: len(ops)], ins[len(ops) :]
            made, outs = outs[: counts[n]], outs[counts[n] :]
            shape = ops[0].shape

            def one(i, _, mine=mine, made=made, shape=shape, n=n, digit=digit):
                if digit is None:
                    made[0][i] = sum(r[i].astype(f32) for r in mine)
                else:
                    first, last = i // shape[2], i % shape[2]
                    for mask, out in enumerate(made):
                        place = digit_ref[n] ^ mask
                        if len(mine) == 1:
                            out[first, last] = mine[0][first, place, last]
                        else:
                            out[first, last] = sum(r[first, place, last].astype(f32) for r in mine).astype(bf16)
                return 0

            lax.fori_loop(0, shape[0] if digit is None else shape[0] * shape[2], one, 0)

    vmem = pl.BlockSpec(memory_space=pltpu.VMEM)
    out = pl.pallas_call(
        body,
        in_specs=[pl.BlockSpec(memory_space=pltpu.SMEM)] + [vmem] * len(flat),
        out_specs=[vmem] * len(shapes),
        out_shape=shapes,
        compiler_params=pltpu.CompilerParams(vmem_limit_bytes=VMEM_LIMIT),
        name="combine",
    )(digits, *flat)
    out = list(out)
    return [[out.pop(0) for _ in range(c)] for c in counts]


class Reduction:
    def __init__(self, parts, dims, stages, sizes, whole=None):
        self.parts = list(parts)
        self.dims = [list(d) for d in dims]
        self.stages = [list(s) for s in stages]
        self.sizes = sizes
        self.whole = whole
        self.inbox = None
        self.held = None

    def left(self):
        return max(len(s) for s in self.stages)

    def launch(self):
        self.inbox = []
        for part, dims, stages in zip(self.parts, self.dims, self.stages):
            axis, which = stages[0]
            size = self.sizes[axis]
            index = lax.axis_index(axis)
            pieces = []
            for code in range(1 << len(which)):
                mask = sum(1 << b for n, b in enumerate(which) if code >> n & 1)
                piece = part
                for place, b in sorted(((dims.index((axis, b)), b) for b in which), reverse=True):
                    bit = ((index ^ mask) >> b) & 1
                    piece = lax.dynamic_index_in_dim(piece, bit, place, keepdims=False)
                if self.whole is not None:
                    self.shape = piece.shape
                    piece = jnp.concatenate([piece.reshape(-1, 128), self.whole], axis=0)
                if mask:
                    piece = lax.ppermute(piece, axis, [(i, i ^ mask) for i in range(size)])
                pieces.append(piece)
            self.inbox.append(pieces)

    def collect(self):
        out = []
        for n, pieces in enumerate(self.inbox):
            axis, which = self.stages[n].pop(0)
            total = sum(p.astype(f32) for p in pieces[1:]) + pieces[0].astype(f32)
            for b in which:
                self.dims[n].remove((axis, b))
            if self.whole is not None:
                count = total.shape[0] - self.whole.shape[0]
                self.whole = total[count:]
                total = total[:count].reshape(self.shape)
                out.append(total)
            else:
                out.append(total.astype(bf16) if self.stages[n] else total)
        self.parts = out
        self.inbox = None

    def digit(self, n):
        axis, which = self.stages[n][0]
        return axis, which, (lax.axis_index(axis) >> which[0]) & ((1 << len(which)) - 1)

    def send(self, n, pieces):
        axis, which = self.stages[n][0]
        size = self.sizes[axis]
        masks = [m << which[0] for m in range(len(pieces))]
        return [lax.ppermute(p, axis, [(i, i ^ m) for i in range(size)]) if m else p for p, m in zip(pieces, masks)]

    def begin(self, halves):
        self.inbox = [self.send(n, list(p)) for n, p in enumerate(halves)]

    def take(self):
        held = []
        for n, pieces in enumerate(self.inbox):
            axis, which = self.stages[n].pop(0)
            for b in which:
                self.dims[n].remove((axis, b))
            held.append(pieces)
        self.held = held
        self.inbox = None

    def run(self):
        if self.inbox:
            self.collect()
        while self.left():
            self.launch()
            self.collect()
        return self.parts


def make(mesh):
    seq = mesh.shape["seq"]
    batch = mesh.shape["batch"]

    def shards(
        inputs, lengths, ga, ba, gf, bf, q_w, q_b, kv_w, kv_b, o_w, o_b, up_w, up_b, down_w, down_b, out_grad, later
    ):
        seqs, block, width = inputs.shape
        total = seqs * block
        span = block * seq
        hidden = up_w.shape[1]
        place = lax.axis_index("seq").astype(jnp.int32).reshape(1)
        tables = rope_tables(place[0] * block, block)
        x = inputs.reshape(total, width)
        g = out_grad.reshape(total, width)
        ga, ba, gf, bf, q_b, kv_b, o_b, up_b, down_b = [
            v.reshape(1, -1) for v in (ga, ba, gf, bf, q_b, kv_b, o_b, up_b, down_b)
        ]
        rows = 2 * block
        sizes = {"seq": seq, "batch": batch}
        seq_dims = [("seq", b) for b in reversed(range(bits(seq)))]
        all_dims = seq_dims + [("batch", b) for b in reversed(range(bits(batch)))]
        b_bits = [("batch", [b]) for b in range(bits(batch))]
        s_bits = [("seq", [b]) for b in range(bits(seq))]
        order_a = b_bits + s_bits
        order_b = b_bits[:1] + s_bits[:1] + b_bits[1:] + s_bits[1:]
        s_rest = [("seq", list(range(b, min(b + 2, bits(seq))))) for b in range(1, bits(seq), 2)]
        direct = [("batch", list(range(bits(batch))))] + s_bits[:1] + s_rest

        def split_rows(p):
            return p.reshape((2,) * len(all_dims) + (p.shape[0] // (seq * batch),) + p.shape[1:])

        def weights(parts, orders):
            return Reduction([split_rows(p) for p in parts], [all_dims] * len(parts), orders, sizes)

        owners = seq * batch
        fused = (width // owners) % 8 == 0 and (hidden // owners) % 8 == 0

        def fence(first, work):
            flat = [p for r in work for p in r.parts]
            first, flat = lax.optimization_barrier((first, flat))
            for r in work:
                r.parts, flat = flat[: len(r.parts)], flat[len(r.parts) :]
            return first

        def settle(value, work):
            work = [r for r in work if r.inbox]
            flat = [p for r in work for pieces in r.inbox for p in pieces]
            value, flat = lax.optimization_barrier((value, flat))
            flat = iter(flat)
            for r in work:
                r.inbox = [[next(flat) for _ in pieces] for pieces in r.inbox]
                if fused and r.whole is None:
                    r.take()
                else:
                    r.collect()
            return value

        def advance(first, work):
            work = [r for r in work if r.left() or r.held]
            plain = [r for r in work if not fused or r.whole is not None]
            work = [r for r in work if r not in plain]
            items, kinds = [], []
            for r in work:
                for n in range(len(r.parts)):
                    ops = r.held[n] if r.held else [r.parts[n]]
                    shape = ops[0].shape
                    tail = shape[-2:]
                    if r.stages[n]:
                        axis, which, digit = r.digit(n)
                        at = min(r.dims[n].index((axis, b)) for b in which)
                        lead = (2,) * len(r.dims[n])
                        rest = math.prod(shape[:-2]) // math.prod(lead)
                        before = math.prod(lead[:at])
                        middle = 1 << len(which)
                        after = math.prod(lead[at + len(which) :]) * rest
                        items.append(([p.reshape((before, middle, after) + tail) for p in ops], digit))
                    else:
                        items.append(([p.reshape((-1,) + tail) for p in ops], None))
            if items:
                made = combine(items)
                for r in work:
                    mine, made = made[: len(r.parts)], made[len(r.parts) :]
                    r.held = None
                    if r.left():
                        r.inbox = [r.send(n, p) for n, p in enumerate(mine)]
                    r.parts = [p[0] for p in mine]
            first = fence(first, work + plain)
            for r in plain:
                if r.left():
                    r.launch()
            return first

        def active(work):
            return [r for r in work if r.left() or r.held]

        ha, hf, kv = norm_kv(x, ga, ba, gf, bf, kv_w, kv_b, tables, rows, 2)
        kv = kv.reshape(seqs, block, 128)
        kv_all = lax.all_gather(kv, "seq", axis=1, tiled=True)
        q, go = query_grad_o(ha, g, q_w, q_b, o_w, tables, rows, 2)
        hf, q, go = lax.optimization_barrier((hf, q, go))
        bit = (lax.axis_index("batch") & 1).astype(jnp.int32).reshape(1)
        act, ghf, dbu, *dff = feed_forward(hf, g, up_w, up_b, down_w, hidden // 4, total // 2, bit, owners)
        dff, kv_all = lax.optimization_barrier((dff, kv_all))
        q = q.reshape(seqs, block, width)
        go = go.reshape(seqs, block, width)

        def from_kernel(made, orders):
            if len(made) == len(orders):
                r = weights(made, orders)
                r.launch()
            else:
                r = Reduction(made[::2], [all_dims] * len(orders), orders, sizes)
                r.begin(list(zip(made[::2], made[1::2])))
            return r

        ffn_sum = from_kernel(dff, [order_a, order_b])
        live = settle(lengths[0], [ffn_sum])
        groups = [4, 4, 4, seqs - 12]
        keep = ()
        first = 0
        kv_sums = []
        for count in groups:
            work = active([ffn_sum] + kv_sums)
            live = advance(live, work)
            o, dq, dkv = attention(live, place, q, go, kv_all, tables, first, count, keep, 256)
            o = settle(o, work)
            keep = (o, dq)
            first += count
            dkv = dkv.reshape((2,) * bits(seq) + (count, block, 128))
            kv_sums.append(Reduction([dkv], [seq_dims], [s_bits], sizes))
        o = o.reshape(total, width)
        dq = dq.reshape(total, width)
        later = later.reshape(total, 128)

        def gradient_of(part, begin, keep):
            part = jnp.concatenate([p.reshape(-1, 128) for p in part], axis=0)
            return input_gradient(
                x, g, dq, q_w, ghf, part, later, ha, kv_w, ga, gf, tables, rows, 2, begin * block // rows, keep
            )

        def sums_of(items):
            if fused:
                return [r.parts[0] for r in items]
            return [r.run()[0] for r in items]

        work = active([ffn_sum] + kv_sums)
        o = advance(o, work)
        early, *dproj = weight_grads(o, g, ha, dq, total // 2, bit, owners)
        early = settle(early, work)
        dproj = advance(dproj, active([ffn_sum] + kv_sums))
        proj_sum = from_kernel(dproj, [order_a, order_b])
        grads = gradient_of(sums_of(kv_sums[:1]), 0, ())
        grads = settle(grads, kv_sums + [proj_sum])
        work = active(kv_sums + [proj_sum])
        grads = advance(grads, work)
        grads = gradient_of(sums_of(kv_sums[1:3]), groups[0], tuple(grads))
        grads = settle(grads, work)
        grads = advance(grads, active(kv_sums + [proj_sum]))
        dx, dwkv, late, sumkv = gradient_of(sums_of(kv_sums[3:]), seqs - groups[3], tuple(grads))
        vec = jnp.concatenate([early.reshape(-1), dbu.reshape(-1), late.reshape(-1), sumkv.reshape(-1)])
        vec = jnp.pad(vec, (0, -vec.shape[0] % 1024)).reshape(-1, 128)
        kvw_sum = Reduction([split_rows(dwkv)], [all_dims], [direct], sizes, whole=vec)
        bias = advance(o_b, [kvw_sum])
        out = ()
        for part, begin in ((2, 0), (4, 2), (4, 3)):
            out = (layer_output(o, act, x, o_w, down_w, bias, down_b, total // part, begin, width, out),)
            work = active([proj_sum, kvw_sum])
            out = (settle(out[0], work),)
            bias = advance(bias, work)
        (out,) = out
        if not fused:
            ffn_sum.run()
            proj_sum.run()
            kvw_sum.run()
        sum_up, sum_down = [p.reshape(p.shape[-2:]) for p in ffn_sum.parts]
        sum_o, sum_q = [p.reshape(p.shape[-2:]) for p in proj_sum.parts]
        sum_kv = kvw_sum.parts[0].reshape(-1, 128)
        vec = kvw_sum.whole.reshape(-1)
        ends = [width, 2 * width, 2 * width + hidden]
        ends += [ends[-1] + width * (i + 1) for i in range(4)]
        sg, sq, su, s0, s1, s2, s3 = [vec[i:j] for i, j in zip([0] + ends[:-1], ends)]
        sk = vec[ends[-1] : ends[-1] + 128]
        return (
            out.reshape(seqs, block, width), kv, dx.reshape(seqs, block, width), s0, s1, s2, s3,
            sum_q, sq, sum_kv, sk, sum_o, sg, sum_up, su, sum_down, sg,
        )

    return shards


def solution(mesh):
    rows = P("batch", "seq", None)
    split = P(("seq", "batch"), None)
    return jax.shard_map(
        make(mesh),
        mesh=mesh,
        in_specs=(rows, P("batch", None)) + (P(),) * 14 + (rows, rows),
        out_specs=(rows, rows, rows, P(), P(), P(), P(), split, P(), split, P(), split, P(), split, P(), split, P()),
        check_vma=False,
    )
```

```python
import functools
import math

import jax
import jax.numpy as jnp
from jax import lax
from jax.experimental import pallas as pl
from jax.experimental.pallas import tpu as pltpu
from jax.sharding import PartitionSpec as P

ROT = 16
EPS = 1e-05
LOG2E = 1.4426950408889634
f32 = jnp.float32
bf16 = jnp.bfloat16
VMEM_LIMIT = 58 << 20


def dot(left, right, left_dim, right_dim):
    return lax.dot_general(
        left, right, (((left_dim,), (right_dim,)), ((), ())), preferred_element_type=f32
    )


def params():
    return pltpu.CompilerParams(
        dimension_semantics=("arbitrary",), vmem_limit_bytes=VMEM_LIMIT
    )


def rope_tables(first, count):
    half = ROT // 2
    lane = jnp.arange(128, dtype=jnp.int32)[None, :] % 64
    frequency = jnp.exp((lane % half).astype(f32) * (-2.0 * math.log(10000.0) / ROT))
    angles = (first + jnp.arange(count, dtype=jnp.int32)).astype(f32)[:, None] * frequency
    main = jnp.where(lane < ROT, jnp.cos(angles), 1.0)
    sin = jnp.sin(angles)
    front = jnp.where(lane < half, -sin, 0.0)
    back = jnp.where((lane >= half) & (lane < ROT), sin, 0.0)
    return jnp.stack([main, front, back])


def rope(x, main, front, back):
    return x * main + pltpu.roll(x, 120, 1) * front + pltpu.roll(x, 8, 1) * back


def stacked(table, times):
    return jnp.concatenate([table] * times, axis=0)


def standardize(x):
    mean = jnp.mean(x, axis=1, keepdims=True)
    centered = x - mean
    inv = lax.rsqrt(jnp.mean(centered * centered, axis=1, keepdims=True) + EPS)
    return centered * inv, inv


def full(shape):
    return pl.BlockSpec(shape, lambda *_: (0,) * len(shape))


def rows_of(rows, width):
    return pl.BlockSpec((rows, width), lambda i, *_: (i, 0))


def vector(start, width):
    return pl.BlockSpec((1, width), lambda *_: (0, start // width))


def norm_kv(x, vectors, at, kv_w, tables, rows, times):
    total, width = x.shape

    def body(x_ref, ga_ref, ba_ref, gf_ref, bf_ref, w_ref, b_ref, t_ref, ha_ref, hf_ref, kv_ref):
        xhat, _ = standardize(x_ref[...].astype(f32))
        ha = (xhat * ga_ref[...].astype(f32) + ba_ref[...].astype(f32)).astype(bf16)
        hf_ref[...] = (xhat * gf_ref[...].astype(f32) + bf_ref[...].astype(f32)).astype(bf16)
        ha_ref[...] = ha
        kv = dot(ha, w_ref[...], 1, 0) + b_ref[...].astype(f32)
        lane = lax.broadcasted_iota(jnp.int32, (1, 128), 1)
        turned = rope(kv, *[stacked(t_ref[i], times) for i in range(3)])
        kv_ref[...] = jnp.where(lane < 64, turned, kv).astype(bf16)

    return pl.pallas_call(
        body,
        grid=(total // rows,),
        in_specs=[rows_of(rows, width)]
        + [vector(at[n], width) for n in ("ga", "ba", "gf", "bf")]
        + [full(kv_w.shape), vector(at["kv_b"], 128), full(tables.shape)],
        out_specs=[rows_of(rows, width), rows_of(rows, width), rows_of(rows, 128)],
        out_shape=[
            jax.ShapeDtypeStruct((total, width), bf16),
            jax.ShapeDtypeStruct((total, width), bf16),
            jax.ShapeDtypeStruct((total, 128), bf16),
        ],
        compiler_params=params(),
        name="norm_kv",
    )(x, *[vectors] * 4, kv_w, vectors, tables)


def query_grad_o(ha, g, q_w, vectors, at, o_w, tables, rows, times):
    total, width = ha.shape

    def body(ha_ref, g_ref, wq_ref, bq_ref, wo_ref, t_ref, q_ref, go_ref):
        q = dot(ha_ref[...], wq_ref[...], 1, 0) + bq_ref[...].astype(f32)
        turn = [stacked(t_ref[i], times) for i in range(3)]
        for c in range(0, width, 128):
            q_ref[:, c : c + 128] = rope(q[:, c : c + 128], *turn).astype(bf16)
        go_ref[...] = dot(g_ref[...], wo_ref[...], 1, 1).astype(bf16)

    return pl.pallas_call(
        body,
        grid=(total // rows,),
        in_specs=[
            rows_of(rows, width), rows_of(rows, width), full(q_w.shape), vector(at["q_b"], width),
            full(o_w.shape), full(tables.shape),
        ],
        out_specs=[rows_of(rows, width), rows_of(rows, width)],
        out_shape=[jax.ShapeDtypeStruct((total, width), bf16)] * 2,
        compiler_params=params(),
        name="query_grad_o",
    )(ha, g, q_w, vectors, o_w, tables)


def gelu_and_slope(u):
    cdf = 0.5 + 0.5 * lax.erf(u * 0.7071067811865476)
    pdf = jnp.exp(u * u * -0.5) * 0.3989422804014327
    return u * cdf, cdf + u * pdf


def feed_forward(h, g, up_w, vectors, down_w, chunk, rows, owners, merged):
    total, width = h.shape
    hidden = up_w.shape[1]
    chunks = hidden // chunk
    up_rows, down_rows = width // owners, hidden // owners
    tiles = down_rows // up_rows
    here = chunk // down_rows

    def body(h_ref, g_ref, wu_ref, bu_ref, wd_ref, act_ref, gh_ref, dbu_ref, *refs):
        gup_s = refs[-1]
        step = pl.program_id(0)

        @pl.when(step == 0)
        def _():
            gh_ref[...] = jnp.zeros_like(gh_ref)

        wu = wu_ref[...]
        wd = wd_ref[...]
        bu = bu_ref[...]

        def block(i, acc):
            sl = pl.ds(pl.multiple_of(i * rows, rows), rows)
            hb = h_ref[sl, :]
            gb = g_ref[sl, :]
            act, slope = gelu_and_slope(dot(hb, wu, 1, 0) + bu)
            act = act.astype(bf16)
            gup = (dot(gb, wd, 1, 1) * slope).astype(bf16)
            act_ref[sl, :] = act
            gup_s[sl, :] = gup
            gh_ref[sl, :] += dot(gup, wu, 1, 1)
            return acc + jnp.sum(gup.astype(f32), axis=0, keepdims=True)

        dbu_ref[...] = lax.fori_loop(0, total // rows, block, jnp.zeros((1, chunk), f32))
        dwu = dot(h_ref[...], gup_s[...], 0, 0)
        dwd = dot(act_ref[...], g_ref[...], 0, 0)
        if not merged:
            refs[0][...] = dwu.astype(bf16)
            refs[1][...] = dwd.astype(bf16)
            return
        both_ref, up_s, down_s, sems = refs[:4]

        def copies(c):
            return (
                pltpu.make_async_copy(up_s, both_ref.at[:, c], sems.at[0]),
                pltpu.make_async_copy(down_s, both_ref.at[pl.ds(here * c, here), pl.ds(chunks, tiles)], sems.at[1]),
            )

        @pl.when(step > 0)
        def _():
            for copy in copies(step - 1):
                copy.wait()

        up_s[...] = dwu.reshape(owners, up_rows, width).astype(bf16)
        down_s[...] = dwd.reshape(here, tiles, up_rows, width).astype(bf16)
        for copy in copies(step):
            copy.start()

        @pl.when(step == chunks - 1)
        def _():
            for copy in copies(step):
                copy.wait()

    whole = full((total, width))
    cols = pl.BlockSpec((width, chunk), lambda c: (0, c))
    vec = pl.BlockSpec((1, chunk), lambda c: (0, c))
    tall = pl.BlockSpec((chunk, width), lambda c: (c, 0))
    if merged:
        weight_specs = [pl.BlockSpec(memory_space=pl.ANY)]
        weight_shapes = [jax.ShapeDtypeStruct((owners, chunks + tiles, up_rows, width), bf16)]
        scratch = [
            pltpu.VMEM((owners, up_rows, width), bf16),
            pltpu.VMEM((here, tiles, up_rows, width), bf16),
            pltpu.SemaphoreType.DMA((2,)),
        ]
    else:
        weight_specs = [cols, tall]
        weight_shapes = [jax.ShapeDtypeStruct((width, hidden), bf16), jax.ShapeDtypeStruct((hidden, width), bf16)]
        scratch = []
    return pl.pallas_call(
        body,
        grid=(chunks,),
        in_specs=[whole, whole, cols, vec, tall],
        out_specs=[pl.BlockSpec((total, chunk), lambda c: (0, c)), whole, vec] + weight_specs,
        out_shape=[
            jax.ShapeDtypeStruct((total, hidden), bf16),
            jax.ShapeDtypeStruct((total, width), f32),
            jax.ShapeDtypeStruct((1, hidden), f32),
        ]
        + weight_shapes,
        scratch_shapes=scratch + [pltpu.VMEM((total, chunk), bf16)],
        compiler_params=params(),
        name="feed_forward",
    )(h, g, up_w, vectors, down_w)


def part_out(source, own, other, bit):
    def one(i, _):
        own[i] = source[i, bit].astype(bf16)
        other[i] = source[i, 1 - bit].astype(bf16)
        return 0

    lax.fori_loop(0, source.shape[0], one, 0)


def attention(lengths, place, q, go, kv, tables, first, count, keep, key_block):
    seqs, block, width = q.shape
    span = kv.shape[1]
    pairs = width // 128

    def body(len_ref, place_ref, q_ref, go_ref, kv_ref, t_ref, *refs):
        o_ref, dq_ref, dkv_ref, dk_acc, dv_acc = refs[-5:]
        live = len_ref[pl.program_id(0) + first]
        start = place_ref[0] * block
        limit = jnp.minimum(live, start + block)
        blocks = (limit + key_block - 1) // key_block
        lane = lax.broadcasted_iota(jnp.int32, (1, 128), 1)
        low = lane < 64
        scale = 0.125

        def branch(number):
            keys = number * key_block
            pair = kv_ref[0, :keys, :].astype(f32)
            swapped = pltpu.roll(pair, 64, 1)
            key_pos = (keys - key_block) + lax.broadcasted_iota(jnp.int32, (block, key_block), 1)
            own_pos = start + lax.broadcasted_iota(jnp.int32, (block, key_block), 0)
            bias = jnp.where((key_pos <= own_pos) & (key_pos < live), 0.0, -1e9).astype(f32)
            bias = stacked(bias, pairs)
            qs = jnp.concatenate([q_ref[0, :, 128 * p : 128 * (p + 1)] for p in range(pairs)], axis=0)
            gs = jnp.concatenate([go_ref[0, :, 128 * p : 128 * (p + 1)] for p in range(pairs)], axis=0)
            gf = gs.astype(f32)

            ke = jnp.where(low, pair, 0.0).astype(bf16)
            ve = jnp.where(low, swapped, 0.0).astype(bf16)
            ko = jnp.where(low, 0.0, swapped).astype(bf16)
            vo = jnp.where(low, 0.0, pair).astype(bf16)

            def scores(k_side):
                s = dot(qs, k_side, 1, 1)
                last = s[:, keys - key_block :] + bias
                return jnp.concatenate([s[:, : keys - key_block], last], axis=1) if number > 1 else last

            def softmax(s):
                top = jnp.max(s, axis=1, keepdims=True)
                expo = jnp.exp2((s - top) * (scale * LOG2E))
                prob = expo * (1.0 / jnp.sum(expo, axis=1, keepdims=True))
                return prob, prob.astype(bf16)

            def slope(prob, o, dp):
                delta = jnp.sum(o * gf, axis=1, keepdims=True)
                return (prob * (dp - delta)).astype(bf16)

            s0, s1 = scores(ke), scores(ko)
            p0, l0 = softmax(s0)
            o0 = dot(l0, ve, 1, 0)
            dp0 = dot(gs, ve, 1, 1)
            p1, l1 = softmax(s1)
            o1 = dot(l1, vo, 1, 0)
            dp1 = dot(gs, vo, 1, 1)
            ds0 = slope(p0, o0, dp0)
            dv_acc[:keys, :] = dot(l0, gs, 0, 0)
            dq0 = dot(ds0, ke, 1, 0)
            dk_acc[:keys, :] = dot(ds0, qs, 0, 0)
            ds1 = slope(p1, o1, dp1)
            dv1 = dot(l1, gs, 0, 0)
            dq1 = dot(ds1, ko, 1, 0)
            dk1 = dot(ds1, qs, 0, 0)
            o = (o0 + o1).astype(bf16)
            dq = (dq0 + dq1) * scale
            turn = [t_ref[0], -t_ref[1], -t_ref[2]]
            for p in range(pairs):
                o_ref[0, :, 128 * p : 128 * (p + 1)] = o[p * block : (p + 1) * block]
                dq_ref[0, :, 128 * p : 128 * (p + 1)] = rope(dq[p * block : (p + 1) * block], *turn).astype(bf16)
            dk = (dk_acc[:keys, :] + pltpu.roll(dk1, 64, 1)) * scale
            dv = dv1 + pltpu.roll(dv_acc[:keys, :], 64, 1)
            dkv_ref[: keys // block, 0] = jnp.where(low, dk, dv).astype(bf16).reshape(keys // block, block, 128)
            if keys < span:
                dkv_ref[keys // block :, 0] = jnp.zeros(((span - keys) // block, block, 128), bf16)

        for number in range(1, span // key_block + 1):
            pl.when(blocks == number)(functools.partial(branch, number))

    row = pl.BlockSpec((1, block, width), lambda s, *_: (s + first, 0, 0))
    kv_in = pl.BlockSpec((1, span, 128), lambda s, *_: (s + first, 0, 0))
    kv_out = pl.BlockSpec((span // block, 1, block, 128), lambda s, *_: (0, s, 0, 0))
    anywhere = pl.BlockSpec(memory_space=pl.ANY)
    return pl.pallas_call(
        body,
        grid_spec=pltpu.PrefetchScalarGridSpec(
            num_scalar_prefetch=2,
            grid=(count,),
            in_specs=[row, row, kv_in, full(tables.shape)] + [anywhere] * len(keep),
            out_specs=[row, row, kv_out],
            scratch_shapes=[pltpu.VMEM((span, 128), f32), pltpu.VMEM((span, 128), f32)],
        ),
        out_shape=[
            jax.ShapeDtypeStruct((seqs, block, width), bf16),
            jax.ShapeDtypeStruct((seqs, block, width), bf16),
            jax.ShapeDtypeStruct((span // block, count, block, 128), bf16),
        ],
        input_output_aliases={6: 0, 7: 1} if keep else {},
        compiler_params=params(),
        name="attention",
    )(lengths, place, q, go, kv, tables, *keep)


def weight_grads(o, g, ha, dq, rows, bit, owners):
    total, width = o.shape
    part = width // owners
    split = part % 8 == 0
    shape = (owners // 2, 2, part, width) if split else (width, width)

    def body(bit_ref, o_ref, g_ref, ha_ref, dq_ref, sum_ref, *refs):
        acc_o, acc_q = refs[-2:]
        step = pl.program_id(0)
        gb = g_ref[...]
        dqb = dq_ref[...]
        dwo = dot(o_ref[...], gb, 0, 0).reshape(shape)
        dwq = dot(ha_ref[...], dqb, 0, 0).reshape(shape)
        sums = jnp.concatenate(
            [jnp.sum(gb.astype(f32), axis=0, keepdims=True), jnp.sum(dqb.astype(f32), axis=0, keepdims=True)], axis=0
        )

        @pl.when(step == 0)
        def _():
            acc_o[...] = dwo
            acc_q[...] = dwq
            sum_ref[...] = sums

        @pl.when(step > 0)
        def _():
            acc_o[...] += dwo
            acc_q[...] += dwq
            sum_ref[...] += sums

        @pl.when(step == total // rows - 1)
        def _():
            if split:
                part_out(acc_o, refs[0], refs[1], bit_ref[0])
                part_out(acc_q, refs[2], refs[3], bit_ref[0])
            else:
                refs[0][...] = acc_o[...].astype(bf16)
                refs[1][...] = acc_q[...].astype(bf16)

    r = rows_of(rows, width)
    out = (owners // 2, part, width) if split else (width, width)
    number = 4 if split else 2
    return pl.pallas_call(
        body,
        grid_spec=pltpu.PrefetchScalarGridSpec(
            num_scalar_prefetch=1,
            grid=(total // rows,),
            in_specs=[r, r, r, r],
            out_specs=[full((2, width))] + [full(out)] * number,
            scratch_shapes=[pltpu.VMEM(shape, f32), pltpu.VMEM(shape, f32)],
        ),
        out_shape=[jax.ShapeDtypeStruct((2, width), f32)] + [jax.ShapeDtypeStruct(out, bf16)] * number,
        compiler_params=params(),
        name="weight_grads",
    )(bit, o, g, ha, dq)


def layer_output(o, act, x, o_w, down_w, vectors, at, rows, first, chunk, keep):
    total, width = o.shape
    hidden = act.shape[1]

    def body(o_ref, a_ref, x_ref, wo_ref, wd_ref, bo_ref, bd_ref, *refs):
        out_ref, acc = refs[-2:]
        step = pl.program_id(0)

        @pl.when(step == 0)
        def _():
            bias = bo_ref[...].astype(f32) + bd_ref[...].astype(f32)
            acc[...] = x_ref[...].astype(f32) + dot(o_ref[...], wo_ref[...], 1, 0) + bias

        acc[...] += dot(a_ref[...], wd_ref[...], 1, 0)

        @pl.when(step == hidden // chunk - 1)
        def _():
            out_ref[...] = acc[...].astype(bf16)

    part = pl.BlockSpec((rows, width), lambda k: (first, 0))
    return pl.pallas_call(
        body,
        grid=(hidden // chunk,),
        in_specs=[
            part,
            pl.BlockSpec((rows, chunk), lambda k: (first, k)),
            part,
            full((width, width)),
            pl.BlockSpec((chunk, width), lambda k: (k, 0)),
            vector(at["o_b"], width),
            vector(at["down_b"], width),
        ]
        + [pl.BlockSpec(memory_space=pl.ANY)] * len(keep),
        out_specs=part,
        out_shape=jax.ShapeDtypeStruct((total, width), bf16),
        scratch_shapes=[pltpu.VMEM((rows, width), f32)],
        input_output_aliases={7: 0} if keep else {},
        compiler_params=params(),
        name="layer_output",
    )(o, act, x, o_w, down_w, vectors, vectors, *keep)


def input_gradient(x, g, dq, q_w, ghf, gkv, later, ha, kv_w, vectors, at, tables, rows, times, first, keep):
    total, width = x.shape

    def body(*refs):
        x_ref, g_ref, dq_ref, wq_ref, ghf_ref, gkv_ref, later_ref, ha_ref, w_ref, ga_ref, gf_ref, t_ref = refs[:12]
        dx_ref, dw_ref, sum_ref, sumkv_ref = refs[-4:]
        step = pl.program_id(0)
        lane = lax.broadcasted_iota(jnp.int32, (1, 128), 1)
        pair = gkv_ref[...] + later_ref[...]
        turn = [stacked(t_ref[i], times) for i in range(3)]
        pair = jnp.where(lane < 64, rope(pair, turn[0], -turn[1], -turn[2]), pair).astype(bf16)
        gha = dot(dq_ref[...], wq_ref[...], 1, 1) + dot(pair, w_ref[...], 1, 1)
        ghf = ghf_ref[...]
        xhat, inv = standardize(x_ref[...].astype(f32))
        gn = gha * ga_ref[...].astype(f32) + ghf * gf_ref[...].astype(f32)
        mean = jnp.mean(gn, axis=1, keepdims=True)
        second = jnp.mean(gn * xhat, axis=1, keepdims=True)
        dx_ref[...] = g_ref[...].astype(f32) + inv * (gn - mean - xhat * second)
        dw = dot(ha_ref[...], pair, 0, 0)
        sums = jnp.concatenate(
            [jnp.sum(v, axis=0, keepdims=True) for v in (gha * xhat, gha, ghf * xhat, ghf)], axis=0
        )
        sumkv = jnp.sum(pair.astype(f32), axis=0, keepdims=True)

        @pl.when(step == 0)
        def _():
            if keep:
                dw_ref[...] = dw + refs[13][...]
                sum_ref[...] = sums + refs[14][...]
                sumkv_ref[...] = sumkv + refs[15][...]
            else:
                dw_ref[...] = dw
                sum_ref[...] = sums
                sumkv_ref[...] = sumkv

        @pl.when(step > 0)
        def _():
            dw_ref[...] += dw
            sum_ref[...] += sums
            sumkv_ref[...] += sumkv

    r = pl.BlockSpec((rows, width), lambda i: (i + first, 0))
    n = pl.BlockSpec((rows, 128), lambda i: (i + first, 0))
    own = pl.BlockSpec((rows, 128), lambda i: (i, 0))
    small = [full((width, 128)), full((4, width)), full((1, 128))]
    return pl.pallas_call(
        body,
        grid=(gkv.shape[0] // rows,),
        in_specs=[r, r, r, full((width, width)), r, own, n, r, full(kv_w.shape)]
        + [vector(at["ga"], width), vector(at["gf"], width), full(tables.shape)]
        + ([pl.BlockSpec(memory_space=pl.ANY)] + small if keep else []),
        out_specs=[r] + small,
        out_shape=[
            jax.ShapeDtypeStruct((total, width), f32),
            jax.ShapeDtypeStruct((width, 128), f32),
            jax.ShapeDtypeStruct((4, width), f32),
            jax.ShapeDtypeStruct((1, 128), f32),
        ],
        input_output_aliases={12: 0} if keep else {},
        compiler_params=params(),
        name="input_gradient",
    )(x, g, dq, q_w, ghf, gkv, later, ha, kv_w, vectors, vectors, tables, *keep)


def bits(size):
    return size.bit_length() - 1


def combine(items):
    digits = jnp.stack([jnp.zeros((), jnp.int32) if d is None else d.astype(jnp.int32) for _, d in items])
    flat = [p for ops, _ in items for p in ops]
    shapes, counts = [], []
    for ops, digit in items:
        shape = ops[0].shape
        if digit is None:
            shapes.append(jax.ShapeDtypeStruct(shape, f32))
            counts.append(1)
        else:
            counts.append(shape[1])
            shapes += [jax.ShapeDtypeStruct((shape[0], shape[2]) + shape[3:], bf16)] * shape[1]

    def body(digit_ref, *refs):
        ins, outs = list(refs[: len(flat)]), list(refs[len(flat) :])
        for n, (ops, digit) in enumerate(items):
            mine, ins = ins[: len(ops)], ins[len(ops) :]
            made, outs = outs[: counts[n]], outs[counts[n] :]
            shape = ops[0].shape

            def one(i, _, mine=mine, made=made, shape=shape, n=n, digit=digit):
                if digit is None:
                    made[0][i] = sum(r[i].astype(f32) for r in mine)
                else:
                    first, last = i // shape[2], i % shape[2]
                    for mask, out in enumerate(made):
                        place = digit_ref[n] ^ mask
                        if len(mine) == 1:
                            out[first, last] = mine[0][first, place, last]
                        else:
                            out[first, last] = sum(r[first, place, last].astype(f32) for r in mine).astype(bf16)
                return 0

            lax.fori_loop(0, shape[0] if digit is None else shape[0] * shape[2], one, 0)

    vmem = pl.BlockSpec(memory_space=pltpu.VMEM)
    out = pl.pallas_call(
        body,
        in_specs=[pl.BlockSpec(memory_space=pltpu.SMEM)] + [vmem] * len(flat),
        out_specs=[vmem] * len(shapes),
        out_shape=shapes,
        compiler_params=pltpu.CompilerParams(vmem_limit_bytes=VMEM_LIMIT),
        name="combine",
    )(digits, *flat)
    out = list(out)
    return [[out.pop(0) for _ in range(c)] for c in counts]


class Reduction:
    def __init__(self, parts, dims, stages, sizes, whole=None):
        self.parts = list(parts)
        self.dims = [list(d) for d in dims]
        self.stages = [list(s) for s in stages]
        self.sizes = sizes
        self.whole = whole
        self.inbox = None
        self.held = None

    def left(self):
        return max(len(s) for s in self.stages)

    def launch(self):
        self.inbox = []
        for part, dims, stages in zip(self.parts, self.dims, self.stages):
            axis, which = stages[0]
            size = self.sizes[axis]
            index = lax.axis_index(axis)
            pieces = []
            for code in range(1 << len(which)):
                mask = sum(1 << b for n, b in enumerate(which) if code >> n & 1)
                piece = part
                for place, b in sorted(((dims.index((axis, b)), b) for b in which), reverse=True):
                    bit = ((index ^ mask) >> b) & 1
                    piece = lax.dynamic_index_in_dim(piece, bit, place, keepdims=False)
                if self.whole is not None:
                    self.shape = piece.shape
                    piece = jnp.concatenate([piece.reshape(-1, 128), self.whole], axis=0)
                if mask:
                    piece = lax.ppermute(piece, axis, [(i, i ^ mask) for i in range(size)])
                pieces.append(piece)
            self.inbox.append(pieces)

    def collect(self):
        out = []
        for n, pieces in enumerate(self.inbox):
            axis, which = self.stages[n].pop(0)
            total = sum(p.astype(f32) for p in pieces[1:]) + pieces[0].astype(f32)
            for b in which:
                self.dims[n].remove((axis, b))
            if self.whole is not None:
                count = total.shape[0] - self.whole.shape[0]
                self.whole = total[count:]
                total = total[:count].reshape(self.shape)
                out.append(total)
            else:
                out.append(total.astype(bf16) if self.stages[n] else total)
        self.parts = out
        self.inbox = None

    def digit(self, n):
        axis, which = self.stages[n][0]
        return axis, which, (lax.axis_index(axis) >> which[0]) & ((1 << len(which)) - 1)

    def send(self, n, pieces):
        axis, which = self.stages[n][0]
        size = self.sizes[axis]
        masks = [m << which[0] for m in range(len(pieces))]
        return [lax.ppermute(p, axis, [(i, i ^ m) for i in range(size)]) if m else p for p, m in zip(pieces, masks)]

    def begin(self, halves):
        self.inbox = [self.send(n, list(p)) for n, p in enumerate(halves)]

    def take(self):
        held = []
        for n, pieces in enumerate(self.inbox):
            axis, which = self.stages[n].pop(0)
            for b in which:
                self.dims[n].remove((axis, b))
            held.append(pieces)
        self.held = held
        self.inbox = None

    def run(self):
        if self.inbox:
            self.collect()
        while self.left():
            self.launch()
            self.collect()
        return self.parts


def make(mesh):
    seq = mesh.shape["seq"]
    batch = mesh.shape["batch"]

    def shards(
        inputs, lengths, ga, ba, gf, bf, q_w, q_b, kv_w, kv_b, o_w, o_b, up_w, up_b, down_w, down_b, out_grad, later
    ):
        seqs, block, width = inputs.shape
        total = seqs * block
        span = block * seq
        hidden = up_w.shape[1]
        place = lax.axis_index("seq").astype(jnp.int32).reshape(1)
        tables = rope_tables(place[0] * block, block)
        x = inputs.reshape(total, width)
        g = out_grad.reshape(total, width)
        named = {"up_b": up_b, "ga": ga, "ba": ba, "gf": gf, "bf": bf, "q_b": q_b, "o_b": o_b, "down_b": down_b, "kv_b": kv_b}
        at, end = {}, 0
        for name, value in named.items():
            at[name] = end
            end += value.shape[0]
        vectors = sum(
            jnp.pad(v.astype(f32), (at[name], end - at[name] - v.shape[0])) for name, v in named.items()
        )[None]
        rows = 2 * block
        sizes = {"seq": seq, "batch": batch}
        seq_dims = [("seq", b) for b in reversed(range(bits(seq)))]
        all_dims = seq_dims + [("batch", b) for b in reversed(range(bits(batch)))]
        b_bits = [("batch", [b]) for b in range(bits(batch))]
        s_bits = [("seq", [b]) for b in range(bits(seq))]
        order_a = b_bits + s_bits
        order_b = b_bits[:1] + s_bits[:1] + b_bits[1:] + s_bits[1:]
        s_rest = [("seq", list(range(b, min(b + 2, bits(seq))))) for b in range(1, bits(seq), 2)]
        direct = [("batch", list(range(bits(batch))))] + s_bits[:1] + s_rest

        def split_rows(p):
            return p.reshape((2,) * len(all_dims) + (p.shape[0] // (seq * batch),) + p.shape[1:])

        def weights(parts, orders):
            return Reduction([split_rows(p) for p in parts], [all_dims] * len(parts), orders, sizes)

        owners = seq * batch
        fused = (width // owners) % 8 == 0 and (hidden // owners) % 8 == 0

        def fence(first, work):
            flat = [p for r in work for p in r.parts]
            first, flat = lax.optimization_barrier((first, flat))
            for r in work:
                r.parts, flat = flat[: len(r.parts)], flat[len(r.parts) :]
            return first

        def settle(value, work):
            work = [r for r in work if r.inbox]
            flat = [p for r in work for pieces in r.inbox for p in pieces]
            value, flat = lax.optimization_barrier((value, flat))
            flat = iter(flat)
            for r in work:
                r.inbox = [[next(flat) for _ in pieces] for pieces in r.inbox]
                if fused and r.whole is None:
                    r.take()
                else:
                    r.collect()
            return value

        def advance(first, work):
            work = [r for r in work if r.left() or r.held]
            plain = [r for r in work if not fused or r.whole is not None]
            work = [r for r in work if r not in plain]
            items, kinds = [], []
            for r in work:
                for n in range(len(r.parts)):
                    ops = r.held[n] if r.held else [r.parts[n]]
                    shape = ops[0].shape
                    tail = shape[-2:]
                    if r.stages[n]:
                        axis, which, digit = r.digit(n)
                        at = min(r.dims[n].index((axis, b)) for b in which)
                        lead = (2,) * len(r.dims[n])
                        rest = math.prod(shape[:-2]) // math.prod(lead)
                        before = math.prod(lead[:at])
                        middle = 1 << len(which)
                        after = math.prod(lead[at + len(which) :]) * rest
                        items.append(([p.reshape((before, middle, after) + tail) for p in ops], digit))
                    else:
                        items.append(([p.reshape((-1,) + tail) for p in ops], None))
            if items:
                made = combine(items)
                for r in work:
                    mine, made = made[: len(r.parts)], made[len(r.parts) :]
                    r.held = None
                    if r.left():
                        r.inbox = [r.send(n, p) for n, p in enumerate(mine)]
                    r.parts = [p[0] for p in mine]
            first = fence(first, work + plain)
            for r in plain:
                if r.left():
                    r.launch()
            return first

        def active(work):
            return [r for r in work if r.left() or r.held]

        ha, hf, kv = norm_kv(x, vectors, at, kv_w, tables, rows, 2)
        kv = kv.reshape(seqs, block, 128)
        kv_all = lax.all_gather(kv, "seq", axis=1, tiled=True)
        q, go = query_grad_o(ha, g, q_w, vectors, at, o_w, tables, rows, 2)
        hf, q, go = lax.optimization_barrier((hf, q, go))
        bit = (lax.axis_index("batch") & 1).astype(jnp.int32).reshape(1)
        merged = fused and hidden // 4 == width
        act, ghf, dbu, *dff = feed_forward(hf, g, up_w, vectors, down_w, hidden // 4, total // 2, owners, merged)
        dff, kv_all = lax.optimization_barrier((dff, kv_all))
        q = q.reshape(seqs, block, width)
        go = go.reshape(seqs, block, width)

        def from_kernel(made, orders):
            if len(made) == len(orders):
                r = weights(made, orders)
                r.launch()
            else:
                r = Reduction(made[::2], [all_dims] * len(orders), orders, sizes)
                r.begin(list(zip(made[::2], made[1::2])))
            return r

        live = lengths[0]
        ffn_sum = []
        if merged:
            both = lax.psum_scatter(dff[0], ("seq", "batch"), scatter_dimension=0, tiled=True)
        else:
            ffn_sum = [weights(dff, [order_a, order_b])]
        groups = [4, 4, 4, seqs - 12]
        keep = ()
        first = 0
        kv_sums = []
        for count in groups:
            work = active(ffn_sum + kv_sums)
            live = advance(live, work)
            o, dq, dkv = attention(live, place, q, go, kv_all, tables, first, count, keep, 256)
            o = settle(o, work)
            keep = (o, dq)
            first += count
            dkv = dkv.reshape((2,) * bits(seq) + (count, block, 128))
            kv_sums.append(Reduction([dkv], [seq_dims], [s_bits], sizes))
        o = o.reshape(total, width)
        dq = dq.reshape(total, width)
        later = later.reshape(total, 128)

        def gradient_of(part, begin, keep):
            part = jnp.concatenate([p.reshape(-1, 128) for p in part], axis=0)
            return input_gradient(
                x, g, dq, q_w, ghf, part, later, ha, kv_w, vectors, at, tables, rows, 2, begin * block // rows, keep
            )

        def sums_of(items):
            if fused:
                return [r.parts[0] for r in items]
            return [r.run()[0] for r in items]

        work = active(ffn_sum + kv_sums)
        o = advance(o, work)
        early, *dproj = weight_grads(o, g, ha, dq, total // 2, bit, owners)
        early = settle(early, work)
        dproj = advance(dproj, active(ffn_sum + kv_sums))
        proj_sum = from_kernel(dproj, [order_a, order_b])
        grads = gradient_of(sums_of(kv_sums[:1]), 0, ())
        grads = settle(grads, kv_sums + [proj_sum])
        work = active(kv_sums + [proj_sum])
        grads = advance(grads, work)
        grads = gradient_of(sums_of(kv_sums[1:3]), groups[0], tuple(grads))
        grads = settle(grads, work)
        grads = advance(grads, active(kv_sums + [proj_sum]))
        dx, dwkv, late, sumkv = gradient_of(sums_of(kv_sums[3:]), seqs - groups[3], tuple(grads))
        vec = jnp.concatenate([early.reshape(-1), dbu.reshape(-1), late.reshape(-1), sumkv.reshape(-1)])
        vec = jnp.pad(vec, (0, -vec.shape[0] % 1024)).reshape(-1, 128)
        kvw_sum = Reduction([split_rows(dwkv)], [all_dims], [direct], sizes, whole=vec)
        vectors = advance(vectors, [kvw_sum])
        out = ()
        for part, begin in ((2, 0), (4, 2), (4, 3)):
            out = (layer_output(o, act, x, o_w, down_w, vectors, at, total // part, begin, width, out),)
            work = active([proj_sum, kvw_sum])
            out = (settle(out[0], work),)
            vectors = advance(vectors, work)
        (out,) = out
        if not fused:
            proj_sum.run()
            kvw_sum.run()
        if merged:
            both = both[0].astype(f32)
            sum_up = both[:4].swapaxes(0, 1).reshape(-1, hidden)
            sum_down = both[4:].reshape(-1, width)
        else:
            sum_up, sum_down = [p.reshape(p.shape[-2:]) for p in ffn_sum[0].run()]
        sum_o, sum_q = [p.reshape(p.shape[-2:]) for p in proj_sum.parts]
        sum_kv = kvw_sum.parts[0].reshape(-1, 128)
        vec = kvw_sum.whole.reshape(-1)
        ends = [width, 2 * width, 2 * width + hidden]
        ends += [ends[-1] + width * (i + 1) for i in range(4)]
        sg, sq, su, s0, s1, s2, s3 = [vec[i:j] for i, j in zip([0] + ends[:-1], ends)]
        sk = vec[ends[-1] : ends[-1] + 128]
        return (
            out.reshape(seqs, block, width), kv, dx.reshape(seqs, block, width), s0, s1, s2, s3,
            sum_q, sq, sum_kv, sk, sum_o, sg, sum_up, su, sum_down, sg,
        )

    return shards


def solution(mesh):
    rows = P("batch", "seq", None)
    split = P(("seq", "batch"), None)
    return jax.shard_map(
        make(mesh),
        mesh=mesh,
        in_specs=(rows, P("batch", None)) + (P(),) * 14 + (rows, rows),
        out_specs=(rows, rows, rows, P(), P(), P(), P(), split, P(), split, P(), split, P(), split, P(), split, P()),
        check_vma=False,
    )
```

```python
import functools
import math

import jax
import jax.numpy as jnp
from jax import lax
from jax.experimental import pallas as pl
from jax.experimental.pallas import tpu as pltpu
from jax.sharding import PartitionSpec as P

ROT = 16
EPS = 1e-05
LOG2E = 1.4426950408889634
f32 = jnp.float32
bf16 = jnp.bfloat16
VMEM_LIMIT = 58 << 20


def dot(left, right, left_dim, right_dim):
    return lax.dot_general(
        left, right, (((left_dim,), (right_dim,)), ((), ())), preferred_element_type=f32
    )


def params():
    return pltpu.CompilerParams(
        dimension_semantics=("arbitrary",), vmem_limit_bytes=VMEM_LIMIT
    )


def rope_tables(first, count):
    half = ROT // 2
    lane = jnp.arange(128, dtype=jnp.int32)[None, :] % 64
    frequency = jnp.exp((lane % half).astype(f32) * (-2.0 * math.log(10000.0) / ROT))
    angles = (first + jnp.arange(count, dtype=jnp.int32)).astype(f32)[:, None] * frequency
    main = jnp.where(lane < ROT, jnp.cos(angles), 1.0)
    sin = jnp.sin(angles)
    front = jnp.where(lane < half, -sin, 0.0)
    back = jnp.where((lane >= half) & (lane < ROT), sin, 0.0)
    return jnp.stack([main, front, back])


def rope(x, main, front, back):
    return x * main + pltpu.roll(x, 120, 1) * front + pltpu.roll(x, 8, 1) * back


def stacked(table, times):
    return jnp.concatenate([table] * times, axis=0)


def standardize(x):
    mean = jnp.mean(x, axis=1, keepdims=True)
    centered = x - mean
    inv = lax.rsqrt(jnp.mean(centered * centered, axis=1, keepdims=True) + EPS)
    return centered * inv, inv


def full(shape):
    return pl.BlockSpec(shape, lambda *_: (0,) * len(shape))


def rows_of(rows, width):
    return pl.BlockSpec((rows, width), lambda i, *_: (i, 0))


def vector(start, width):
    return pl.BlockSpec((1, width), lambda *_: (0, start // width))


def norm_kv(x, vectors, at, kv_w, tables, rows, times):
    total, width = x.shape

    def body(x_ref, ga_ref, ba_ref, gf_ref, bf_ref, w_ref, b_ref, t_ref, ha_ref, hf_ref, kv_ref):
        xhat, _ = standardize(x_ref[...].astype(f32))
        ha = (xhat * ga_ref[...].astype(f32) + ba_ref[...].astype(f32)).astype(bf16)
        hf_ref[...] = (xhat * gf_ref[...].astype(f32) + bf_ref[...].astype(f32)).astype(bf16)
        ha_ref[...] = ha
        kv = dot(ha, w_ref[...], 1, 0) + b_ref[...].astype(f32)
        lane = lax.broadcasted_iota(jnp.int32, (1, 128), 1)
        turned = rope(kv, *[stacked(t_ref[i], times) for i in range(3)])
        kv_ref[...] = jnp.where(lane < 64, turned, kv).astype(bf16)

    return pl.pallas_call(
        body,
        grid=(total // rows,),
        in_specs=[rows_of(rows, width)]
        + [vector(at[n], width) for n in ("ga", "ba", "gf", "bf")]
        + [full(kv_w.shape), vector(at["kv_b"], 128), full(tables.shape)],
        out_specs=[rows_of(rows, width), rows_of(rows, width), rows_of(rows, 128)],
        out_shape=[
            jax.ShapeDtypeStruct((total, width), bf16),
            jax.ShapeDtypeStruct((total, width), bf16),
            jax.ShapeDtypeStruct((total, 128), bf16),
        ],
        compiler_params=params(),
        name="norm_kv",
    )(x, *[vectors] * 4, kv_w, vectors, tables)


def query_grad_o(ha, g, q_w, vectors, at, o_w, tables, rows, times):
    total, width = ha.shape

    def body(ha_ref, g_ref, wq_ref, bq_ref, wo_ref, t_ref, q_ref, go_ref):
        q = dot(ha_ref[...], wq_ref[...], 1, 0) + bq_ref[...].astype(f32)
        turn = [stacked(t_ref[i], times) for i in range(3)]
        for c in range(0, width, 128):
            q_ref[:, c : c + 128] = rope(q[:, c : c + 128], *turn).astype(bf16)
        go_ref[...] = dot(g_ref[...], wo_ref[...], 1, 1).astype(bf16)

    return pl.pallas_call(
        body,
        grid=(total // rows,),
        in_specs=[
            rows_of(rows, width), rows_of(rows, width), full(q_w.shape), vector(at["q_b"], width),
            full(o_w.shape), full(tables.shape),
        ],
        out_specs=[rows_of(rows, width), rows_of(rows, width)],
        out_shape=[jax.ShapeDtypeStruct((total, width), bf16)] * 2,
        compiler_params=params(),
        name="query_grad_o",
    )(ha, g, q_w, vectors, o_w, tables)


def gelu_and_slope(u):
    cdf = 0.5 + 0.5 * lax.erf(u * 0.7071067811865476)
    pdf = jnp.exp(u * u * -0.5) * 0.3989422804014327
    return u * cdf, cdf + u * pdf


def feed_forward(h, g, up_w, vectors, down_w, chunk, rows, owners, merged):
    total, width = h.shape
    hidden = up_w.shape[1]
    chunks = hidden // chunk
    up_rows, down_rows = width // owners, hidden // owners
    tiles = down_rows // up_rows
    here = chunk // down_rows

    def body(h_ref, g_ref, wu_ref, bu_ref, wd_ref, act_ref, gh_ref, dbu_ref, *refs):
        gup_s = refs[-1]
        step = pl.program_id(0)

        @pl.when(step == 0)
        def _():
            gh_ref[...] = jnp.zeros_like(gh_ref)

        wu = wu_ref[...]
        wd = wd_ref[...]
        bu = bu_ref[...]

        def block(i, acc):
            sl = pl.ds(pl.multiple_of(i * rows, rows), rows)
            hb = h_ref[sl, :]
            gb = g_ref[sl, :]
            act, slope = gelu_and_slope(dot(hb, wu, 1, 0) + bu)
            act = act.astype(bf16)
            gup = (dot(gb, wd, 1, 1) * slope).astype(bf16)
            act_ref[sl, :] = act
            gup_s[sl, :] = gup
            gh_ref[sl, :] += dot(gup, wu, 1, 1)
            return acc + jnp.sum(gup.astype(f32), axis=0, keepdims=True)

        dbu_ref[...] = lax.fori_loop(0, total // rows, block, jnp.zeros((1, chunk), f32))
        dwu = dot(h_ref[...], gup_s[...], 0, 0)
        dwd = dot(act_ref[...], g_ref[...], 0, 0)
        if not merged:
            refs[0][...] = dwu.astype(bf16)
            refs[1][...] = dwd.astype(bf16)
            return
        both_ref, up_s, down_s, sems = refs[:4]

        def copies(c):
            return (
                pltpu.make_async_copy(up_s, both_ref.at[:, c], sems.at[0]),
                pltpu.make_async_copy(down_s, both_ref.at[pl.ds(here * c, here), pl.ds(chunks, tiles)], sems.at[1]),
            )

        @pl.when(step > 0)
        def _():
            for copy in copies(step - 1):
                copy.wait()

        up_s[...] = dwu.reshape(owners, up_rows, width).astype(bf16)
        down_s[...] = dwd.reshape(here, tiles, up_rows, width).astype(bf16)
        for copy in copies(step):
            copy.start()

        @pl.when(step == chunks - 1)
        def _():
            for copy in copies(step):
                copy.wait()

    whole = full((total, width))
    cols = pl.BlockSpec((width, chunk), lambda c: (0, c))
    vec = pl.BlockSpec((1, chunk), lambda c: (0, c))
    tall = pl.BlockSpec((chunk, width), lambda c: (c, 0))
    if merged:
        weight_specs = [pl.BlockSpec(memory_space=pl.ANY)]
        weight_shapes = [jax.ShapeDtypeStruct((owners, chunks + tiles, up_rows, width), bf16)]
        scratch = [
            pltpu.VMEM((owners, up_rows, width), bf16),
            pltpu.VMEM((here, tiles, up_rows, width), bf16),
            pltpu.SemaphoreType.DMA((2,)),
        ]
    else:
        weight_specs = [cols, tall]
        weight_shapes = [jax.ShapeDtypeStruct((width, hidden), bf16), jax.ShapeDtypeStruct((hidden, width), bf16)]
        scratch = []
    return pl.pallas_call(
        body,
        grid=(chunks,),
        in_specs=[whole, whole, cols, vec, tall],
        out_specs=[pl.BlockSpec((total, chunk), lambda c: (0, c)), whole, vec] + weight_specs,
        out_shape=[
            jax.ShapeDtypeStruct((total, hidden), bf16),
            jax.ShapeDtypeStruct((total, width), f32),
            jax.ShapeDtypeStruct((1, hidden), f32),
        ]
        + weight_shapes,
        scratch_shapes=scratch + [pltpu.VMEM((total, chunk), bf16)],
        compiler_params=params(),
        name="feed_forward",
    )(h, g, up_w, vectors, down_w)


def part_out(source, own, other, bit):
    def one(i, _):
        own[i] = source[i, bit].astype(bf16)
        other[i] = source[i, 1 - bit].astype(bf16)
        return 0

    lax.fori_loop(0, source.shape[0], one, 0)


def attention(lengths, place, q, go, kv, tables, first, count, keep, key_block):
    seqs, block, width = q.shape
    span = kv.shape[1]
    pairs = width // 128

    def body(len_ref, place_ref, q_ref, go_ref, kv_ref, t_ref, *refs):
        o_ref, dq_ref, dkv_ref, dk_acc, dv_acc = refs[-5:]
        live = len_ref[pl.program_id(0) + first]
        start = place_ref[0] * block
        limit = jnp.minimum(live, start + block)
        blocks = (limit + key_block - 1) // key_block
        lane = lax.broadcasted_iota(jnp.int32, (1, 128), 1)
        low = lane < 64
        scale = 0.125

        def branch(number):
            keys = number * key_block
            pair = kv_ref[0, :keys, :].astype(f32)
            swapped = pltpu.roll(pair, 64, 1)
            key_pos = (keys - key_block) + lax.broadcasted_iota(jnp.int32, (block, key_block), 1)
            own_pos = start + lax.broadcasted_iota(jnp.int32, (block, key_block), 0)
            bias = jnp.where((key_pos <= own_pos) & (key_pos < live), 0.0, -1e9).astype(f32)
            bias = stacked(bias, pairs)
            qs = jnp.concatenate([q_ref[0, :, 128 * p : 128 * (p + 1)] for p in range(pairs)], axis=0)
            gs = jnp.concatenate([go_ref[0, :, 128 * p : 128 * (p + 1)] for p in range(pairs)], axis=0)
            gf = gs.astype(f32)

            ke = jnp.where(low, pair, 0.0).astype(bf16)
            ve = jnp.where(low, swapped, 0.0).astype(bf16)
            ko = jnp.where(low, 0.0, swapped).astype(bf16)
            vo = jnp.where(low, 0.0, pair).astype(bf16)

            def scores(k_side):
                s = dot(qs, k_side, 1, 1)
                last = s[:, keys - key_block :] + bias
                return jnp.concatenate([s[:, : keys - key_block], last], axis=1) if number > 1 else last

            def softmax(s):
                top = jnp.max(s, axis=1, keepdims=True)
                expo = jnp.exp2((s - top) * (scale * LOG2E))
                prob = expo * (1.0 / jnp.sum(expo, axis=1, keepdims=True))
                return prob, prob.astype(bf16)

            def slope(prob, o, dp):
                delta = jnp.sum(o * gf, axis=1, keepdims=True)
                return (prob * (dp - delta)).astype(bf16)

            s0, s1 = scores(ke), scores(ko)
            p0, l0 = softmax(s0)
            o0 = dot(l0, ve, 1, 0)
            dp0 = dot(gs, ve, 1, 1)
            p1, l1 = softmax(s1)
            o1 = dot(l1, vo, 1, 0)
            dp1 = dot(gs, vo, 1, 1)
            ds0 = slope(p0, o0, dp0)
            dv_acc[:keys, :] = dot(l0, gs, 0, 0)
            dq0 = dot(ds0, ke, 1, 0)
            dk_acc[:keys, :] = dot(ds0, qs, 0, 0)
            ds1 = slope(p1, o1, dp1)
            dv1 = dot(l1, gs, 0, 0)
            dq1 = dot(ds1, ko, 1, 0)
            dk1 = dot(ds1, qs, 0, 0)
            o = (o0 + o1).astype(bf16)
            dq = (dq0 + dq1) * scale
            turn = [t_ref[0], -t_ref[1], -t_ref[2]]
            for p in range(pairs):
                o_ref[0, :, 128 * p : 128 * (p + 1)] = o[p * block : (p + 1) * block]
                dq_ref[0, :, 128 * p : 128 * (p + 1)] = rope(dq[p * block : (p + 1) * block], *turn).astype(bf16)
            dk = (dk_acc[:keys, :] + pltpu.roll(dk1, 64, 1)) * scale
            dv = dv1 + pltpu.roll(dv_acc[:keys, :], 64, 1)
            dkv_ref[: keys // block, 0] = jnp.where(low, dk, dv).astype(bf16).reshape(keys // block, block, 128)
            if keys < span:
                dkv_ref[keys // block :, 0] = jnp.zeros(((span - keys) // block, block, 128), bf16)

        for number in range(1, span // key_block + 1):
            pl.when(blocks == number)(functools.partial(branch, number))

    row = pl.BlockSpec((1, block, width), lambda s, *_: (s + first, 0, 0))
    kv_in = pl.BlockSpec((1, span, 128), lambda s, *_: (s + first, 0, 0))
    kv_out = pl.BlockSpec((span // block, 1, block, 128), lambda s, *_: (0, s, 0, 0))
    anywhere = pl.BlockSpec(memory_space=pl.ANY)
    return pl.pallas_call(
        body,
        grid_spec=pltpu.PrefetchScalarGridSpec(
            num_scalar_prefetch=2,
            grid=(count,),
            in_specs=[row, row, kv_in, full(tables.shape)] + [anywhere] * len(keep),
            out_specs=[row, row, kv_out],
            scratch_shapes=[pltpu.VMEM((span, 128), f32), pltpu.VMEM((span, 128), f32)],
        ),
        out_shape=[
            jax.ShapeDtypeStruct((seqs, block, width), bf16),
            jax.ShapeDtypeStruct((seqs, block, width), bf16),
            jax.ShapeDtypeStruct((span // block, count, block, 128), bf16),
        ],
        input_output_aliases={6: 0, 7: 1} if keep else {},
        compiler_params=params(),
        name="attention",
    )(lengths, place, q, go, kv, tables, *keep)


def weight_grads(o, g, ha, dq, rows, bit, owners):
    total, width = o.shape
    part = width // owners
    split = part % 8 == 0
    shape = (owners // 2, 2, part, width) if split else (width, width)

    def body(bit_ref, o_ref, g_ref, ha_ref, dq_ref, sum_ref, *refs):
        acc_o, acc_q = refs[-2:]
        step = pl.program_id(0)
        gb = g_ref[...]
        dqb = dq_ref[...]
        dwo = dot(o_ref[...], gb, 0, 0).reshape(shape)
        dwq = dot(ha_ref[...], dqb, 0, 0).reshape(shape)
        sums = jnp.concatenate(
            [jnp.sum(gb.astype(f32), axis=0, keepdims=True), jnp.sum(dqb.astype(f32), axis=0, keepdims=True)], axis=0
        )

        @pl.when(step == 0)
        def _():
            acc_o[...] = dwo
            acc_q[...] = dwq
            sum_ref[...] = sums

        @pl.when(step > 0)
        def _():
            acc_o[...] += dwo
            acc_q[...] += dwq
            sum_ref[...] += sums

        @pl.when(step == total // rows - 1)
        def _():
            if split:
                part_out(acc_o, refs[0], refs[1], bit_ref[0])
                part_out(acc_q, refs[2], refs[3], bit_ref[0])
            else:
                refs[0][...] = acc_o[...].astype(bf16)
                refs[1][...] = acc_q[...].astype(bf16)

    r = rows_of(rows, width)
    out = (owners // 2, part, width) if split else (width, width)
    number = 4 if split else 2
    return pl.pallas_call(
        body,
        grid_spec=pltpu.PrefetchScalarGridSpec(
            num_scalar_prefetch=1,
            grid=(total // rows,),
            in_specs=[r, r, r, r],
            out_specs=[full((2, width))] + [full(out)] * number,
            scratch_shapes=[pltpu.VMEM(shape, f32), pltpu.VMEM(shape, f32)],
        ),
        out_shape=[jax.ShapeDtypeStruct((2, width), f32)] + [jax.ShapeDtypeStruct(out, bf16)] * number,
        compiler_params=params(),
        name="weight_grads",
    )(bit, o, g, ha, dq)


def layer_output(o, act, x, o_w, down_w, vectors, at, rows, first, chunk, keep):
    total, width = o.shape
    hidden = act.shape[1]

    def body(o_ref, a_ref, x_ref, wo_ref, wd_ref, bo_ref, bd_ref, *refs):
        out_ref, acc = refs[-2:]
        step = pl.program_id(0)

        @pl.when(step == 0)
        def _():
            bias = bo_ref[...].astype(f32) + bd_ref[...].astype(f32)
            acc[...] = x_ref[...].astype(f32) + dot(o_ref[...], wo_ref[...], 1, 0) + bias

        acc[...] += dot(a_ref[...], wd_ref[...], 1, 0)

        @pl.when(step == hidden // chunk - 1)
        def _():
            out_ref[...] = acc[...].astype(bf16)

    part = pl.BlockSpec((rows, width), lambda k: (first, 0))
    return pl.pallas_call(
        body,
        grid=(hidden // chunk,),
        in_specs=[
            part,
            pl.BlockSpec((rows, chunk), lambda k: (first, k)),
            part,
            full((width, width)),
            pl.BlockSpec((chunk, width), lambda k: (k, 0)),
            vector(at["o_b"], width),
            vector(at["down_b"], width),
        ]
        + [pl.BlockSpec(memory_space=pl.ANY)] * len(keep),
        out_specs=part,
        out_shape=jax.ShapeDtypeStruct((total, width), bf16),
        scratch_shapes=[pltpu.VMEM((rows, width), f32)],
        input_output_aliases={7: 0} if keep else {},
        compiler_params=params(),
        name="layer_output",
    )(o, act, x, o_w, down_w, vectors, vectors, *keep)


def input_gradient(x, g, dq, q_w, ghf, gkv, later, ha, kv_w, vectors, at, tables, rows, times, first, keep):
    total, width = x.shape

    def body(*refs):
        x_ref, g_ref, dq_ref, wq_ref, ghf_ref, gkv_ref, later_ref, ha_ref, w_ref, ga_ref, gf_ref, t_ref = refs[:12]
        dx_ref, dw_ref, sum_ref, sumkv_ref = refs[-4:]
        step = pl.program_id(0)
        lane = lax.broadcasted_iota(jnp.int32, (1, 128), 1)
        pair = gkv_ref[...] + later_ref[...]
        turn = [stacked(t_ref[i], times) for i in range(3)]
        pair = jnp.where(lane < 64, rope(pair, turn[0], -turn[1], -turn[2]), pair).astype(bf16)
        gha = dot(dq_ref[...], wq_ref[...], 1, 1) + dot(pair, w_ref[...], 1, 1)
        ghf = ghf_ref[...]
        xhat, inv = standardize(x_ref[...].astype(f32))
        gn = gha * ga_ref[...].astype(f32) + ghf * gf_ref[...].astype(f32)
        mean = jnp.mean(gn, axis=1, keepdims=True)
        second = jnp.mean(gn * xhat, axis=1, keepdims=True)
        dx_ref[...] = g_ref[...].astype(f32) + inv * (gn - mean - xhat * second)
        dw = dot(ha_ref[...], pair, 0, 0)
        sums = jnp.concatenate(
            [jnp.sum(v, axis=0, keepdims=True) for v in (gha * xhat, gha, ghf * xhat, ghf)], axis=0
        )
        sumkv = jnp.sum(pair.astype(f32), axis=0, keepdims=True)

        @pl.when(step == 0)
        def _():
            if keep:
                dw_ref[...] = dw + refs[13][...]
                sum_ref[...] = sums + refs[14][...]
                sumkv_ref[...] = sumkv + refs[15][...]
            else:
                dw_ref[...] = dw
                sum_ref[...] = sums
                sumkv_ref[...] = sumkv

        @pl.when(step > 0)
        def _():
            dw_ref[...] += dw
            sum_ref[...] += sums
            sumkv_ref[...] += sumkv

    r = pl.BlockSpec((rows, width), lambda i: (i + first, 0))
    n = pl.BlockSpec((rows, 128), lambda i: (i + first, 0))
    own = pl.BlockSpec((rows, 128), lambda i: (i, 0))
    small = [full((width, 128)), full((4, width)), full((1, 128))]
    return pl.pallas_call(
        body,
        grid=(gkv.shape[0] // rows,),
        in_specs=[r, r, r, full((width, width)), r, own, n, r, full(kv_w.shape)]
        + [vector(at["ga"], width), vector(at["gf"], width), full(tables.shape)]
        + ([pl.BlockSpec(memory_space=pl.ANY)] + small if keep else []),
        out_specs=[r] + small,
        out_shape=[
            jax.ShapeDtypeStruct((total, width), f32),
            jax.ShapeDtypeStruct((width, 128), f32),
            jax.ShapeDtypeStruct((4, width), f32),
            jax.ShapeDtypeStruct((1, 128), f32),
        ],
        input_output_aliases={12: 0} if keep else {},
        compiler_params=params(),
        name="input_gradient",
    )(x, g, dq, q_w, ghf, gkv, later, ha, kv_w, vectors, vectors, tables, *keep)


def bits(size):
    return size.bit_length() - 1


def combine(items):
    digits = jnp.stack([jnp.zeros((), jnp.int32) if d is None else d.astype(jnp.int32) for _, d in items])
    flat = [p for ops, _ in items for p in ops]
    shapes, counts = [], []
    for ops, digit in items:
        shape = ops[0].shape
        if digit is None:
            shapes.append(jax.ShapeDtypeStruct(shape, f32))
            counts.append(1)
        else:
            counts.append(shape[1])
            shapes += [jax.ShapeDtypeStruct((shape[0], shape[2]) + shape[3:], bf16)] * shape[1]

    def body(digit_ref, *refs):
        ins, outs = list(refs[: len(flat)]), list(refs[len(flat) :])
        for n, (ops, digit) in enumerate(items):
            mine, ins = ins[: len(ops)], ins[len(ops) :]
            made, outs = outs[: counts[n]], outs[counts[n] :]
            shape = ops[0].shape

            def one(i, _, mine=mine, made=made, shape=shape, n=n, digit=digit):
                if digit is None:
                    made[0][i] = sum(r[i].astype(f32) for r in mine)
                else:
                    first, last = i // shape[2], i % shape[2]
                    for mask, out in enumerate(made):
                        place = digit_ref[n] ^ mask
                        if len(mine) == 1:
                            out[first, last] = mine[0][first, place, last]
                        else:
                            out[first, last] = sum(r[first, place, last].astype(f32) for r in mine).astype(bf16)
                return 0

            lax.fori_loop(0, shape[0] if digit is None else shape[0] * shape[2], one, 0)

    vmem = pl.BlockSpec(memory_space=pltpu.VMEM)
    out = pl.pallas_call(
        body,
        in_specs=[pl.BlockSpec(memory_space=pltpu.SMEM)] + [vmem] * len(flat),
        out_specs=[vmem] * len(shapes),
        out_shape=shapes,
        compiler_params=pltpu.CompilerParams(vmem_limit_bytes=VMEM_LIMIT),
        name="combine",
    )(digits, *flat)
    out = list(out)
    return [[out.pop(0) for _ in range(c)] for c in counts]


class Reduction:
    def __init__(self, parts, dims, stages, sizes, whole=None):
        self.parts = list(parts)
        self.dims = [list(d) for d in dims]
        self.stages = [list(s) for s in stages]
        self.sizes = sizes
        self.whole = whole
        self.inbox = None
        self.held = None

    def left(self):
        return max(len(s) for s in self.stages)

    def launch(self):
        self.inbox = []
        for part, dims, stages in zip(self.parts, self.dims, self.stages):
            axis, which = stages[0]
            size = self.sizes[axis]
            index = lax.axis_index(axis)
            pieces = []
            for code in range(1 << len(which)):
                mask = sum(1 << b for n, b in enumerate(which) if code >> n & 1)
                piece = part
                for place, b in sorted(((dims.index((axis, b)), b) for b in which), reverse=True):
                    bit = ((index ^ mask) >> b) & 1
                    piece = lax.dynamic_index_in_dim(piece, bit, place, keepdims=False)
                if self.whole is not None:
                    self.shape = piece.shape
                    piece = jnp.concatenate([piece.reshape(-1, 128), self.whole], axis=0)
                if mask:
                    piece = lax.ppermute(piece, axis, [(i, i ^ mask) for i in range(size)])
                pieces.append(piece)
            self.inbox.append(pieces)

    def collect(self):
        out = []
        for n, pieces in enumerate(self.inbox):
            axis, which = self.stages[n].pop(0)
            total = sum(p.astype(f32) for p in pieces[1:]) + pieces[0].astype(f32)
            for b in which:
                self.dims[n].remove((axis, b))
            if self.whole is not None:
                count = total.shape[0] - self.whole.shape[0]
                self.whole = total[count:]
                total = total[:count].reshape(self.shape)
                out.append(total)
            else:
                out.append(total.astype(bf16) if self.stages[n] else total)
        self.parts = out
        self.inbox = None

    def digit(self, n):
        axis, which = self.stages[n][0]
        return axis, which, (lax.axis_index(axis) >> which[0]) & ((1 << len(which)) - 1)

    def send(self, n, pieces):
        axis, which = self.stages[n][0]
        size = self.sizes[axis]
        masks = [m << which[0] for m in range(len(pieces))]
        return [lax.ppermute(p, axis, [(i, i ^ m) for i in range(size)]) if m else p for p, m in zip(pieces, masks)]

    def begin(self, halves):
        self.inbox = [self.send(n, list(p)) for n, p in enumerate(halves)]

    def take(self):
        held = []
        for n, pieces in enumerate(self.inbox):
            axis, which = self.stages[n].pop(0)
            for b in which:
                self.dims[n].remove((axis, b))
            held.append(pieces)
        self.held = held
        self.inbox = None

    def run(self):
        if self.inbox:
            self.collect()
        while self.left():
            self.launch()
            self.collect()
        return self.parts


def make(mesh):
    seq = mesh.shape["seq"]
    batch = mesh.shape["batch"]

    def shards(
        inputs, lengths, ga, ba, gf, bf, q_w, q_b, kv_w, kv_b, o_w, o_b, up_w, up_b, down_w, down_b, out_grad, later
    ):
        seqs, block, width = inputs.shape
        total = seqs * block
        span = block * seq
        hidden = up_w.shape[1]
        place = lax.axis_index("seq").astype(jnp.int32).reshape(1)
        tables = rope_tables(place[0] * block, block)
        x = inputs.reshape(total, width)
        g = out_grad.reshape(total, width)
        named = {"up_b": up_b, "ga": ga, "ba": ba, "gf": gf, "bf": bf, "q_b": q_b, "o_b": o_b, "down_b": down_b, "kv_b": kv_b}
        at, end = {}, 0
        for name, value in named.items():
            at[name] = end
            end += value.shape[0]
        vectors = sum(
            jnp.pad(v.astype(f32), (at[name], end - at[name] - v.shape[0])) for name, v in named.items()
        )[None]
        rows = 2 * block
        sizes = {"seq": seq, "batch": batch}
        seq_dims = [("seq", b) for b in reversed(range(bits(seq)))]
        all_dims = seq_dims + [("batch", b) for b in reversed(range(bits(batch)))]
        b_bits = [("batch", [b]) for b in range(bits(batch))]
        s_bits = [("seq", [b]) for b in range(bits(seq))]
        order_a = b_bits + s_bits
        order_b = b_bits[:1] + s_bits[:1] + b_bits[1:] + s_bits[1:]
        s_rest = [("seq", list(range(b, min(b + 2, bits(seq))))) for b in range(1, bits(seq), 2)]
        direct = [("batch", list(range(bits(batch))))] + s_bits[:1] + s_rest

        def split_rows(p):
            return p.reshape((2,) * len(all_dims) + (p.shape[0] // (seq * batch),) + p.shape[1:])

        def weights(parts, orders):
            return Reduction([split_rows(p) for p in parts], [all_dims] * len(parts), orders, sizes)

        owners = seq * batch
        fused = (width // owners) % 8 == 0 and (hidden // owners) % 8 == 0

        def fence(first, work):
            flat = [p for r in work for p in r.parts]
            first, flat = lax.optimization_barrier((first, flat))
            for r in work:
                r.parts, flat = flat[: len(r.parts)], flat[len(r.parts) :]
            return first

        def settle(value, work):
            work = [r for r in work if r.inbox]
            flat = [p for r in work for pieces in r.inbox for p in pieces]
            value, flat = lax.optimization_barrier((value, flat))
            flat = iter(flat)
            for r in work:
                r.inbox = [[next(flat) for _ in pieces] for pieces in r.inbox]
                if fused and r.whole is None:
                    r.take()
                else:
                    r.collect()
            return value

        def advance(first, work):
            work = [r for r in work if r.left() or r.held]
            plain = [r for r in work if not fused or r.whole is not None]
            work = [r for r in work if r not in plain]
            items, kinds = [], []
            for r in work:
                for n in range(len(r.parts)):
                    ops = r.held[n] if r.held else [r.parts[n]]
                    shape = ops[0].shape
                    tail = shape[-2:]
                    if r.stages[n]:
                        axis, which, digit = r.digit(n)
                        at = min(r.dims[n].index((axis, b)) for b in which)
                        lead = (2,) * len(r.dims[n])
                        rest = math.prod(shape[:-2]) // math.prod(lead)
                        before = math.prod(lead[:at])
                        middle = 1 << len(which)
                        after = math.prod(lead[at + len(which) :]) * rest
                        items.append(([p.reshape((before, middle, after) + tail) for p in ops], digit))
                    else:
                        items.append(([p.reshape((-1,) + tail) for p in ops], None))
            if items:
                made = combine(items)
                for r in work:
                    mine, made = made[: len(r.parts)], made[len(r.parts) :]
                    r.held = None
                    if r.left():
                        r.inbox = [r.send(n, p) for n, p in enumerate(mine)]
                    r.parts = [p[0] for p in mine]
            first = fence(first, work + plain)
            for r in plain:
                if r.left():
                    r.launch()
            return first

        def active(work):
            return [r for r in work if r.left() or r.held]

        ha, hf, kv = norm_kv(x, vectors, at, kv_w, tables, rows, 2)
        kv = kv.reshape(seqs, block, 128)
        kv_all = lax.all_gather(kv, "seq", axis=1, tiled=True)
        q, go = query_grad_o(ha, g, q_w, vectors, at, o_w, tables, rows, 2)
        hf, q, go = lax.optimization_barrier((hf, q, go))
        bit = (lax.axis_index("batch") & 1).astype(jnp.int32).reshape(1)
        merged = fused and hidden // 4 == width
        act, ghf, dbu, *dff = feed_forward(hf, g, up_w, vectors, down_w, hidden // 4, total // 2, owners, merged)
        dff, kv_all = lax.optimization_barrier((dff, kv_all))
        q = q.reshape(seqs, block, width)
        go = go.reshape(seqs, block, width)

        def from_kernel(made, orders):
            if len(made) == len(orders):
                r = weights(made, orders)
                r.launch()
            else:
                r = Reduction(made[::2], [all_dims] * len(orders), orders, sizes)
                r.begin(list(zip(made[::2], made[1::2])))
            return r

        live = lengths[0]
        ffn_sum = []
        if merged:
            both = lax.psum_scatter(dff[0], ("seq", "batch"), scatter_dimension=0, tiled=True)
        else:
            ffn_sum = [weights(dff, [order_a, order_b])]
        groups = [8, seqs - 8]
        keep = ()
        first = 0
        kv_sums = []
        for count in groups:
            work = active(ffn_sum + kv_sums)
            live = advance(live, work)
            o, dq, dkv = attention(live, place, q, go, kv_all, tables, first, count, keep, 256)
            o = settle(o, work)
            keep = (o, dq)
            first += count
            dkv = dkv.reshape((2,) * bits(seq) + (count, block, 128))
            kv_sums.append(Reduction([dkv], [seq_dims], [s_bits], sizes))
        o = o.reshape(total, width)
        dq = dq.reshape(total, width)
        later = later.reshape(total, 128)

        def gradient_of(part, begin, keep):
            part = jnp.concatenate([p.reshape(-1, 128) for p in part], axis=0)
            return input_gradient(
                x, g, dq, q_w, ghf, part, later, ha, kv_w, vectors, at, tables, rows, 2, begin * block // rows, keep
            )

        def sums_of(items):
            if fused:
                return [r.parts[0] for r in items]
            return [r.run()[0] for r in items]

        def output_half(part, keep):
            return (layer_output(o, act, x, o_w, down_w, vectors, at, total // 2, part, width, keep),)

        work = active(ffn_sum + kv_sums)
        o, vectors = advance((o, vectors), work)
        early, *dproj = weight_grads(o, g, ha, dq, total // 2, bit, owners)
        early, vectors = lax.optimization_barrier((early, vectors))
        out = output_half(0, ())
        out = settle(out, work)
        dproj, vectors = advance((dproj, vectors), active(ffn_sum + kv_sums))
        proj_sum = from_kernel(dproj, [order_a, order_b])
        out = output_half(1, tuple(out))
        (out,) = settle(out, kv_sums + [proj_sum])
        work = active(kv_sums + [proj_sum])
        vectors = advance(vectors, work)
        grads = gradient_of(sums_of(kv_sums[:1]), 0, ())
        grads = settle(grads, work)
        grads = advance(grads, active(kv_sums + [proj_sum]))
        dx, dwkv, late, sumkv = gradient_of(sums_of(kv_sums[1:]), groups[0], tuple(grads))
        vec = jnp.concatenate([early.reshape(-1), dbu.reshape(-1), late.reshape(-1), sumkv.reshape(-1)])
        vec = jnp.pad(vec, (0, -vec.shape[0] % 1024)).reshape(-1, 128)
        kvw_sum = Reduction([split_rows(dwkv)], [all_dims], [direct], sizes, whole=vec)
        late = advance(late, [kvw_sum])
        for _ in range(3):
            work = active([proj_sum, kvw_sum])
            late = settle(late, work)
            late = advance(late, work)
        if not fused:
            proj_sum.run()
            kvw_sum.run()
        if merged:
            both = both[0].astype(f32)
            sum_up = both[:4].swapaxes(0, 1).reshape(-1, hidden)
            sum_down = both[4:].reshape(-1, width)
        else:
            sum_up, sum_down = [p.reshape(p.shape[-2:]) for p in ffn_sum[0].run()]
        sum_o, sum_q = [p.reshape(p.shape[-2:]) for p in proj_sum.parts]
        sum_kv = kvw_sum.parts[0].reshape(-1, 128)
        vec = kvw_sum.whole.reshape(-1)
        ends = [width, 2 * width, 2 * width + hidden]
        ends += [ends[-1] + width * (i + 1) for i in range(4)]
        sg, sq, su, s0, s1, s2, s3 = [vec[i:j] for i, j in zip([0] + ends[:-1], ends)]
        sk = vec[ends[-1] : ends[-1] + 128]
        return (
            out.reshape(seqs, block, width), kv, dx.reshape(seqs, block, width), s0, s1, s2, s3,
            sum_q, sq, sum_kv, sk, sum_o, sg, sum_up, su, sum_down, sg,
        )

    return shards


def solution(mesh):
    rows = P("batch", "seq", None)
    split = P(("seq", "batch"), None)
    return jax.shard_map(
        make(mesh),
        mesh=mesh,
        in_specs=(rows, P("batch", None)) + (P(),) * 14 + (rows, rows),
        out_specs=(rows, rows, rows, P(), P(), P(), P(), split, P(), split, P(), split, P(), split, P(), split, P()),
        check_vma=False,
    )
```

```python
import functools
import math

import jax
import jax.numpy as jnp
from jax import lax
from jax.experimental import pallas as pl
from jax.experimental.pallas import tpu as pltpu
from jax.sharding import PartitionSpec as P

ROT = 16
EPS = 1e-05
LOG2E = 1.4426950408889634
f32 = jnp.float32
bf16 = jnp.bfloat16
VMEM_LIMIT = 58 << 20


def dot(left, right, left_dim, right_dim):
    return lax.dot_general(
        left, right, (((left_dim,), (right_dim,)), ((), ())), preferred_element_type=f32
    )


def params():
    return pltpu.CompilerParams(
        dimension_semantics=("arbitrary",), vmem_limit_bytes=VMEM_LIMIT
    )


def rope_tables(first, count):
    half = ROT // 2
    lane = jnp.arange(128, dtype=jnp.int32)[None, :] % 64
    frequency = jnp.exp((lane % half).astype(f32) * (-2.0 * math.log(10000.0) / ROT))
    angles = (first + jnp.arange(count, dtype=jnp.int32)).astype(f32)[:, None] * frequency
    main = jnp.where(lane < ROT, jnp.cos(angles), 1.0)
    sin = jnp.sin(angles)
    front = jnp.where(lane < half, -sin, 0.0)
    back = jnp.where((lane >= half) & (lane < ROT), sin, 0.0)
    return jnp.stack([main, front, back])


def rope(x, main, front, back):
    return x * main + pltpu.roll(x, 120, 1) * front + pltpu.roll(x, 8, 1) * back


def stacked(table, times):
    return jnp.concatenate([table] * times, axis=0)


def standardize(x):
    mean = jnp.mean(x, axis=1, keepdims=True)
    centered = x - mean
    inv = lax.rsqrt(jnp.mean(centered * centered, axis=1, keepdims=True) + EPS)
    return centered * inv, inv


def full(shape):
    return pl.BlockSpec(shape, lambda *_: (0,) * len(shape))


def rows_of(rows, width):
    return pl.BlockSpec((rows, width), lambda i, *_: (i, 0))


def vector(start, width):
    return pl.BlockSpec((1, width), lambda *_: (0, start // width))


def norm_kv(x, vectors, at, kv_w, tables, rows, times):
    total, width = x.shape

    def body(x_ref, ga_ref, ba_ref, gf_ref, bf_ref, w_ref, b_ref, t_ref, ha_ref, hf_ref, kv_ref):
        xhat, _ = standardize(x_ref[...].astype(f32))
        ha = (xhat * ga_ref[...].astype(f32) + ba_ref[...].astype(f32)).astype(bf16)
        hf_ref[...] = (xhat * gf_ref[...].astype(f32) + bf_ref[...].astype(f32)).astype(bf16)
        ha_ref[...] = ha
        kv = dot(ha, w_ref[...], 1, 0) + b_ref[...].astype(f32)
        lane = lax.broadcasted_iota(jnp.int32, (1, 128), 1)
        turned = rope(kv, *[stacked(t_ref[i], times) for i in range(3)])
        kv_ref[...] = jnp.where(lane < 64, turned, kv).astype(bf16)

    return pl.pallas_call(
        body,
        grid=(total // rows,),
        in_specs=[rows_of(rows, width)]
        + [vector(at[n], width) for n in ("ga", "ba", "gf", "bf")]
        + [full(kv_w.shape), vector(at["kv_b"], 128), full(tables.shape)],
        out_specs=[rows_of(rows, width), rows_of(rows, width), rows_of(rows, 128)],
        out_shape=[
            jax.ShapeDtypeStruct((total, width), bf16),
            jax.ShapeDtypeStruct((total, width), bf16),
            jax.ShapeDtypeStruct((total, 128), bf16),
        ],
        compiler_params=params(),
        name="norm_kv",
    )(x, *[vectors] * 4, kv_w, vectors, tables)


def query_grad_o(ha, g, q_w, vectors, at, o_w, tables, rows, times):
    total, width = ha.shape

    def body(ha_ref, g_ref, wq_ref, bq_ref, wo_ref, t_ref, q_ref, go_ref):
        q = dot(ha_ref[...], wq_ref[...], 1, 0) + bq_ref[...].astype(f32)
        turn = [stacked(t_ref[i], times) for i in range(3)]
        for c in range(0, width, 128):
            q_ref[:, c : c + 128] = rope(q[:, c : c + 128], *turn).astype(bf16)
        go_ref[...] = dot(g_ref[...], wo_ref[...], 1, 1).astype(bf16)

    return pl.pallas_call(
        body,
        grid=(total // rows,),
        in_specs=[
            rows_of(rows, width), rows_of(rows, width), full(q_w.shape), vector(at["q_b"], width),
            full(o_w.shape), full(tables.shape),
        ],
        out_specs=[rows_of(rows, width), rows_of(rows, width)],
        out_shape=[jax.ShapeDtypeStruct((total, width), bf16)] * 2,
        compiler_params=params(),
        name="query_grad_o",
    )(ha, g, q_w, vectors, o_w, tables)


def gelu_and_slope(u):
    cdf = 0.5 + 0.5 * lax.erf(u * 0.7071067811865476)
    pdf = jnp.exp(u * u * -0.5) * 0.3989422804014327
    return u * cdf, cdf + u * pdf


def feed_forward(h, g, up_w, vectors, down_w, chunk, rows, owners, merged):
    total, width = h.shape
    hidden = up_w.shape[1]
    chunks = hidden // chunk
    up_rows, down_rows = width // owners, hidden // owners
    tiles = down_rows // up_rows
    here = chunk // down_rows

    def body(h_ref, g_ref, wu_ref, bu_ref, wd_ref, act_ref, gh_ref, dbu_ref, *refs):
        gup_s = refs[-1]
        step = pl.program_id(0)

        @pl.when(step == 0)
        def _():
            gh_ref[...] = jnp.zeros_like(gh_ref)

        wu = wu_ref[...]
        wd = wd_ref[...]
        bu = bu_ref[...]

        def block(i, acc):
            sl = pl.ds(pl.multiple_of(i * rows, rows), rows)
            hb = h_ref[sl, :]
            gb = g_ref[sl, :]
            act, slope = gelu_and_slope(dot(hb, wu, 1, 0) + bu)
            act = act.astype(bf16)
            gup = (dot(gb, wd, 1, 1) * slope).astype(bf16)
            act_ref[sl, :] = act
            gup_s[sl, :] = gup
            gh_ref[sl, :] += dot(gup, wu, 1, 1)
            return acc + jnp.sum(gup.astype(f32), axis=0, keepdims=True)

        dbu_ref[...] = lax.fori_loop(0, total // rows, block, jnp.zeros((1, chunk), f32))
        dwu = dot(h_ref[...], gup_s[...], 0, 0)
        dwd = dot(act_ref[...], g_ref[...], 0, 0)
        if not merged:
            refs[0][...] = dwu.astype(bf16)
            refs[1][...] = dwd.astype(bf16)
            return
        both_ref, up_s, down_s, sems = refs[:4]

        def copies(c):
            return (
                pltpu.make_async_copy(up_s, both_ref.at[:, c], sems.at[0]),
                pltpu.make_async_copy(down_s, both_ref.at[pl.ds(here * c, here), pl.ds(chunks, tiles)], sems.at[1]),
            )

        @pl.when(step > 0)
        def _():
            for copy in copies(step - 1):
                copy.wait()

        up_s[...] = dwu.reshape(owners, up_rows, width).astype(bf16)
        down_s[...] = dwd.reshape(here, tiles, up_rows, width).astype(bf16)
        for copy in copies(step):
            copy.start()

        @pl.when(step == chunks - 1)
        def _():
            for copy in copies(step):
                copy.wait()

    whole = full((total, width))
    cols = pl.BlockSpec((width, chunk), lambda c: (0, c))
    vec = pl.BlockSpec((1, chunk), lambda c: (0, c))
    tall = pl.BlockSpec((chunk, width), lambda c: (c, 0))
    if merged:
        weight_specs = [pl.BlockSpec(memory_space=pl.ANY)]
        weight_shapes = [jax.ShapeDtypeStruct((owners, chunks + tiles, up_rows, width), bf16)]
        scratch = [
            pltpu.VMEM((owners, up_rows, width), bf16),
            pltpu.VMEM((here, tiles, up_rows, width), bf16),
            pltpu.SemaphoreType.DMA((2,)),
        ]
    else:
        weight_specs = [cols, tall]
        weight_shapes = [jax.ShapeDtypeStruct((width, hidden), bf16), jax.ShapeDtypeStruct((hidden, width), bf16)]
        scratch = []
    return pl.pallas_call(
        body,
        grid=(chunks,),
        in_specs=[whole, whole, cols, vec, tall],
        out_specs=[pl.BlockSpec((total, chunk), lambda c: (0, c)), whole, vec] + weight_specs,
        out_shape=[
            jax.ShapeDtypeStruct((total, hidden), bf16),
            jax.ShapeDtypeStruct((total, width), f32),
            jax.ShapeDtypeStruct((1, hidden), f32),
        ]
        + weight_shapes,
        scratch_shapes=scratch + [pltpu.VMEM((total, chunk), bf16)],
        compiler_params=params(),
        name="feed_forward",
    )(h, g, up_w, vectors, down_w)


def part_out(source, own, other, bit):
    def one(i, _):
        own[i] = source[i, bit].astype(bf16)
        other[i] = source[i, 1 - bit].astype(bf16)
        return 0

    lax.fori_loop(0, source.shape[0], one, 0)


def attention(lengths, place, q, go, kv, tables, first, count, keep, key_block):
    seqs, block, width = q.shape
    span = kv.shape[1]
    pairs = width // 128

    def body(len_ref, place_ref, q_ref, go_ref, kv_ref, t_ref, *refs):
        o_ref, dq_ref, kept_ref, sent_ref, dk_acc, dv_acc = refs[-6:]
        live = len_ref[pl.program_id(0) + first]
        start = place_ref[0] * block
        limit = jnp.minimum(live, start + block)
        blocks = (limit + key_block - 1) // key_block
        lane = lax.broadcasted_iota(jnp.int32, (1, 128), 1)
        low = lane < 64
        scale = 0.125

        def branch(number):
            keys = number * key_block
            pair = kv_ref[0, :keys, :].astype(f32)
            swapped = pltpu.roll(pair, 64, 1)
            key_pos = (keys - key_block) + lax.broadcasted_iota(jnp.int32, (block, key_block), 1)
            own_pos = start + lax.broadcasted_iota(jnp.int32, (block, key_block), 0)
            bias = jnp.where((key_pos <= own_pos) & (key_pos < live), 0.0, -1e9).astype(f32)
            bias = stacked(bias, pairs)
            qs = jnp.concatenate([q_ref[0, :, 128 * p : 128 * (p + 1)] for p in range(pairs)], axis=0)
            gs = jnp.concatenate([go_ref[0, :, 128 * p : 128 * (p + 1)] for p in range(pairs)], axis=0)
            gf = gs.astype(f32)

            ke = jnp.where(low, pair, 0.0).astype(bf16)
            ve = jnp.where(low, swapped, 0.0).astype(bf16)
            ko = jnp.where(low, 0.0, swapped).astype(bf16)
            vo = jnp.where(low, 0.0, pair).astype(bf16)

            def scores(k_side):
                s = dot(qs, k_side, 1, 1)
                last = s[:, keys - key_block :] + bias
                return jnp.concatenate([s[:, : keys - key_block], last], axis=1) if number > 1 else last

            def softmax(s):
                top = jnp.max(s, axis=1, keepdims=True)
                expo = jnp.exp2((s - top) * (scale * LOG2E))
                prob = expo * (1.0 / jnp.sum(expo, axis=1, keepdims=True))
                return prob, prob.astype(bf16)

            def slope(prob, o, dp):
                delta = jnp.sum(o * gf, axis=1, keepdims=True)
                return (prob * (dp - delta)).astype(bf16)

            s0, s1 = scores(ke), scores(ko)
            p0, l0 = softmax(s0)
            o0 = dot(l0, ve, 1, 0)
            dp0 = dot(gs, ve, 1, 1)
            p1, l1 = softmax(s1)
            o1 = dot(l1, vo, 1, 0)
            dp1 = dot(gs, vo, 1, 1)
            ds0 = slope(p0, o0, dp0)
            dv_acc[:keys, :] = dot(l0, gs, 0, 0)
            dq0 = dot(ds0, ke, 1, 0)
            dk_acc[:keys, :] = dot(ds0, qs, 0, 0)
            ds1 = slope(p1, o1, dp1)
            dv1 = dot(l1, gs, 0, 0)
            dq1 = dot(ds1, ko, 1, 0)
            dk1 = dot(ds1, qs, 0, 0)
            o = (o0 + o1).astype(bf16)
            dq = (dq0 + dq1) * scale
            turn = [t_ref[0], -t_ref[1], -t_ref[2]]
            for p in range(pairs):
                o_ref[0, :, 128 * p : 128 * (p + 1)] = o[p * block : (p + 1) * block]
                dq_ref[0, :, 128 * p : 128 * (p + 1)] = rope(dq[p * block : (p + 1) * block], *turn).astype(bf16)
            dk = (dk_acc[:keys, :] + pltpu.roll(dk1, 64, 1)) * scale
            dv = dv1 + pltpu.roll(dv_acc[:keys, :], 64, 1)
            both = jnp.where(low, dk, dv).astype(bf16).reshape(keys // block // 2, 2, block, 128)
            odd = place_ref[0] % 2 == 1
            half = keys // block // 2
            kept_ref[:half, 0] = jnp.where(odd, both[:, 1], both[:, 0])
            sent_ref[:half, 0] = jnp.where(odd, both[:, 0], both[:, 1])
            if keys < span:
                rest = jnp.zeros((span // block // 2 - half, block, 128), bf16)
                kept_ref[half:, 0] = rest
                sent_ref[half:, 0] = rest

        for number in range(1, span // key_block + 1):
            pl.when(blocks == number)(functools.partial(branch, number))

    row = pl.BlockSpec((1, block, width), lambda s, *_: (s + first, 0, 0))
    kv_in = pl.BlockSpec((1, span, 128), lambda s, *_: (s + first, 0, 0))
    kv_out = pl.BlockSpec((span // block // 2, 1, block, 128), lambda s, *_: (0, s, 0, 0))
    anywhere = pl.BlockSpec(memory_space=pl.ANY)
    return pl.pallas_call(
        body,
        grid_spec=pltpu.PrefetchScalarGridSpec(
            num_scalar_prefetch=2,
            grid=(count,),
            in_specs=[row, row, kv_in, full(tables.shape)] + [anywhere] * len(keep),
            out_specs=[row, row, kv_out, kv_out],
            scratch_shapes=[pltpu.VMEM((span, 128), f32), pltpu.VMEM((span, 128), f32)],
        ),
        out_shape=[
            jax.ShapeDtypeStruct((seqs, block, width), bf16),
            jax.ShapeDtypeStruct((seqs, block, width), bf16),
        ]
        + [jax.ShapeDtypeStruct((span // block // 2, count, block, 128), bf16)] * 2,
        input_output_aliases={6: 0, 7: 1} if keep else {},
        compiler_params=params(),
        name="attention",
    )(lengths, place, q, go, kv, tables, *keep)


def weight_grads(o, g, ha, dq, rows, bit, owners):
    total, width = o.shape
    part = width // owners
    split = part % 8 == 0
    shape = (owners // 2, 2, part, width) if split else (width, width)

    def body(bit_ref, o_ref, g_ref, ha_ref, dq_ref, sum_ref, *refs):
        acc_o, acc_q = refs[-2:]
        step = pl.program_id(0)
        gb = g_ref[...]
        dqb = dq_ref[...]
        dwo = dot(o_ref[...], gb, 0, 0).reshape(shape)
        dwq = dot(ha_ref[...], dqb, 0, 0).reshape(shape)
        sums = jnp.concatenate(
            [jnp.sum(gb.astype(f32), axis=0, keepdims=True), jnp.sum(dqb.astype(f32), axis=0, keepdims=True)], axis=0
        )

        @pl.when(step == 0)
        def _():
            acc_o[...] = dwo
            acc_q[...] = dwq
            sum_ref[...] = sums

        @pl.when(step > 0)
        def _():
            acc_o[...] += dwo
            acc_q[...] += dwq
            sum_ref[...] += sums

        @pl.when(step == total // rows - 1)
        def _():
            if split:
                part_out(acc_o, refs[0], refs[1], bit_ref[0])
                part_out(acc_q, refs[2], refs[3], bit_ref[0])
            else:
                refs[0][...] = acc_o[...].astype(bf16)
                refs[1][...] = acc_q[...].astype(bf16)

    r = rows_of(rows, width)
    out = (owners // 2, part, width) if split else (width, width)
    number = 4 if split else 2
    return pl.pallas_call(
        body,
        grid_spec=pltpu.PrefetchScalarGridSpec(
            num_scalar_prefetch=1,
            grid=(total // rows,),
            in_specs=[r, r, r, r],
            out_specs=[full((2, width))] + [full(out)] * number,
            scratch_shapes=[pltpu.VMEM(shape, f32), pltpu.VMEM(shape, f32)],
        ),
        out_shape=[jax.ShapeDtypeStruct((2, width), f32)] + [jax.ShapeDtypeStruct(out, bf16)] * number,
        compiler_params=params(),
        name="weight_grads",
    )(bit, o, g, ha, dq)


def layer_output(o, act, x, o_w, down_w, vectors, at, rows, first, chunk, keep):
    total, width = o.shape
    hidden = act.shape[1]

    def body(o_ref, a_ref, x_ref, wo_ref, wd_ref, bo_ref, bd_ref, *refs):
        out_ref, acc = refs[-2:]
        step = pl.program_id(0)

        @pl.when(step == 0)
        def _():
            bias = bo_ref[...].astype(f32) + bd_ref[...].astype(f32)
            acc[...] = x_ref[...].astype(f32) + dot(o_ref[...], wo_ref[...], 1, 0) + bias

        acc[...] += dot(a_ref[...], wd_ref[...], 1, 0)

        @pl.when(step == hidden // chunk - 1)
        def _():
            out_ref[...] = acc[...].astype(bf16)

    part = pl.BlockSpec((rows, width), lambda k: (first, 0))
    return pl.pallas_call(
        body,
        grid=(hidden // chunk,),
        in_specs=[
            part,
            pl.BlockSpec((rows, chunk), lambda k: (first, k)),
            part,
            full((width, width)),
            pl.BlockSpec((chunk, width), lambda k: (k, 0)),
            vector(at["o_b"], width),
            vector(at["down_b"], width),
        ]
        + [pl.BlockSpec(memory_space=pl.ANY)] * len(keep),
        out_specs=part,
        out_shape=jax.ShapeDtypeStruct((total, width), bf16),
        scratch_shapes=[pltpu.VMEM((rows, width), f32)],
        input_output_aliases={7: 0} if keep else {},
        compiler_params=params(),
        name="layer_output",
    )(o, act, x, o_w, down_w, vectors, vectors, *keep)


def input_gradient(x, g, dq, q_w, ghf, gkv, later, ha, kv_w, vectors, at, tables, rows, times, first, keep):
    total, width = x.shape

    def body(*refs):
        x_ref, g_ref, dq_ref, wq_ref, ghf_ref, gkv_ref, later_ref, ha_ref, w_ref, ga_ref, gf_ref, t_ref = refs[:12]
        dx_ref, dw_ref, sum_ref, sumkv_ref = refs[-4:]
        step = pl.program_id(0)
        lane = lax.broadcasted_iota(jnp.int32, (1, 128), 1)
        pair = gkv_ref[...] + later_ref[...]
        turn = [stacked(t_ref[i], times) for i in range(3)]
        pair = jnp.where(lane < 64, rope(pair, turn[0], -turn[1], -turn[2]), pair).astype(bf16)
        gha = dot(dq_ref[...], wq_ref[...], 1, 1) + dot(pair, w_ref[...], 1, 1)
        ghf = ghf_ref[...]
        xhat, inv = standardize(x_ref[...].astype(f32))
        gn = gha * ga_ref[...].astype(f32) + ghf * gf_ref[...].astype(f32)
        mean = jnp.mean(gn, axis=1, keepdims=True)
        second = jnp.mean(gn * xhat, axis=1, keepdims=True)
        dx_ref[...] = g_ref[...].astype(f32) + inv * (gn - mean - xhat * second)
        dw = dot(ha_ref[...], pair, 0, 0)
        sums = jnp.concatenate(
            [jnp.sum(v, axis=0, keepdims=True) for v in (gha * xhat, gha, ghf * xhat, ghf)], axis=0
        )
        sumkv = jnp.sum(pair.astype(f32), axis=0, keepdims=True)

        @pl.when(step == 0)
        def _():
            if keep:
                dw_ref[...] = dw + refs[13][...]
                sum_ref[...] = sums + refs[14][...]
                sumkv_ref[...] = sumkv + refs[15][...]
            else:
                dw_ref[...] = dw
                sum_ref[...] = sums
                sumkv_ref[...] = sumkv

        @pl.when(step > 0)
        def _():
            dw_ref[...] += dw
            sum_ref[...] += sums
            sumkv_ref[...] += sumkv

    r = pl.BlockSpec((rows, width), lambda i: (i + first, 0))
    n = pl.BlockSpec((rows, 128), lambda i: (i + first, 0))
    own = pl.BlockSpec((rows, 128), lambda i: (i, 0))
    small = [full((width, 128)), full((4, width)), full((1, 128))]
    return pl.pallas_call(
        body,
        grid=(gkv.shape[0] // rows,),
        in_specs=[r, r, r, full((width, width)), r, own, n, r, full(kv_w.shape)]
        + [vector(at["ga"], width), vector(at["gf"], width), full(tables.shape)]
        + ([pl.BlockSpec(memory_space=pl.ANY)] + small if keep else []),
        out_specs=[r] + small,
        out_shape=[
            jax.ShapeDtypeStruct((total, width), f32),
            jax.ShapeDtypeStruct((width, 128), f32),
            jax.ShapeDtypeStruct((4, width), f32),
            jax.ShapeDtypeStruct((1, 128), f32),
        ],
        input_output_aliases={12: 0} if keep else {},
        compiler_params=params(),
        name="input_gradient",
    )(x, g, dq, q_w, ghf, gkv, later, ha, kv_w, vectors, vectors, tables, *keep)


def bits(size):
    return size.bit_length() - 1


def combine(items):
    digits = jnp.stack([jnp.zeros((), jnp.int32) if d is None else d.astype(jnp.int32) for _, d in items])
    flat = [p for ops, _ in items for p in ops]
    shapes, counts = [], []
    for ops, digit in items:
        shape = ops[0].shape
        if digit is None:
            shapes.append(jax.ShapeDtypeStruct(shape, f32))
            counts.append(1)
        else:
            counts.append(shape[1])
            shapes += [jax.ShapeDtypeStruct((shape[0], shape[2]) + shape[3:], bf16)] * shape[1]

    def body(digit_ref, *refs):
        ins, outs = list(refs[: len(flat)]), list(refs[len(flat) :])
        for n, (ops, digit) in enumerate(items):
            mine, ins = ins[: len(ops)], ins[len(ops) :]
            made, outs = outs[: counts[n]], outs[counts[n] :]
            shape = ops[0].shape

            def one(i, _, mine=mine, made=made, shape=shape, n=n, digit=digit):
                if digit is None:
                    made[0][i] = sum(r[i].astype(f32) for r in mine)
                else:
                    first, last = i // shape[2], i % shape[2]
                    for mask, out in enumerate(made):
                        place = digit_ref[n] ^ mask
                        if len(mine) == 1:
                            out[first, last] = mine[0][first, place, last]
                        else:
                            out[first, last] = sum(r[first, place, last].astype(f32) for r in mine).astype(bf16)
                return 0

            lax.fori_loop(0, shape[0] if digit is None else shape[0] * shape[2], one, 0)

    vmem = pl.BlockSpec(memory_space=pltpu.VMEM)
    out = pl.pallas_call(
        body,
        in_specs=[pl.BlockSpec(memory_space=pltpu.SMEM)] + [vmem] * len(flat),
        out_specs=[vmem] * len(shapes),
        out_shape=shapes,
        compiler_params=pltpu.CompilerParams(vmem_limit_bytes=VMEM_LIMIT),
        name="combine",
    )(digits, *flat)
    out = list(out)
    return [[out.pop(0) for _ in range(c)] for c in counts]


class Reduction:
    def __init__(self, parts, dims, stages, sizes, whole=None):
        self.parts = list(parts)
        self.dims = [list(d) for d in dims]
        self.stages = [list(s) for s in stages]
        self.sizes = sizes
        self.whole = whole
        self.inbox = None
        self.held = None

    def left(self):
        return max(len(s) for s in self.stages)

    def launch(self):
        self.inbox = []
        for part, dims, stages in zip(self.parts, self.dims, self.stages):
            axis, which = stages[0]
            size = self.sizes[axis]
            index = lax.axis_index(axis)
            pieces = []
            for code in range(1 << len(which)):
                mask = sum(1 << b for n, b in enumerate(which) if code >> n & 1)
                piece = part
                for place, b in sorted(((dims.index((axis, b)), b) for b in which), reverse=True):
                    bit = ((index ^ mask) >> b) & 1
                    piece = lax.dynamic_index_in_dim(piece, bit, place, keepdims=False)
                if self.whole is not None:
                    self.shape = piece.shape
                    piece = jnp.concatenate([piece.reshape(-1, 128), self.whole], axis=0)
                if mask:
                    piece = lax.ppermute(piece, axis, [(i, i ^ mask) for i in range(size)])
                pieces.append(piece)
            self.inbox.append(pieces)

    def collect(self):
        out = []
        for n, pieces in enumerate(self.inbox):
            axis, which = self.stages[n].pop(0)
            total = sum(p.astype(f32) for p in pieces[1:]) + pieces[0].astype(f32)
            for b in which:
                self.dims[n].remove((axis, b))
            if self.whole is not None:
                count = total.shape[0] - self.whole.shape[0]
                self.whole = total[count:]
                total = total[:count].reshape(self.shape)
                out.append(total)
            else:
                out.append(total.astype(bf16) if self.stages[n] else total)
        self.parts = out
        self.inbox = None

    def digit(self, n):
        axis, which = self.stages[n][0]
        return axis, which, (lax.axis_index(axis) >> which[0]) & ((1 << len(which)) - 1)

    def send(self, n, pieces):
        axis, which = self.stages[n][0]
        size = self.sizes[axis]
        masks = [m << which[0] for m in range(len(pieces))]
        return [lax.ppermute(p, axis, [(i, i ^ m) for i in range(size)]) if m else p for p, m in zip(pieces, masks)]

    def begin(self, halves):
        self.inbox = [self.send(n, list(p)) for n, p in enumerate(halves)]

    def take(self):
        held = []
        for n, pieces in enumerate(self.inbox):
            axis, which = self.stages[n].pop(0)
            for b in which:
                self.dims[n].remove((axis, b))
            held.append(pieces)
        self.held = held
        self.inbox = None

    def run(self):
        if self.inbox:
            self.collect()
        while self.left():
            self.launch()
            self.collect()
        return self.parts


def make(mesh):
    seq = mesh.shape["seq"]
    batch = mesh.shape["batch"]

    def shards(
        inputs, lengths, ga, ba, gf, bf, q_w, q_b, kv_w, kv_b, o_w, o_b, up_w, up_b, down_w, down_b, out_grad, later
    ):
        seqs, block, width = inputs.shape
        total = seqs * block
        span = block * seq
        hidden = up_w.shape[1]
        place = lax.axis_index("seq").astype(jnp.int32).reshape(1)
        tables = rope_tables(place[0] * block, block)
        x = inputs.reshape(total, width)
        g = out_grad.reshape(total, width)
        named = {"up_b": up_b, "ga": ga, "ba": ba, "gf": gf, "bf": bf, "q_b": q_b, "o_b": o_b, "down_b": down_b, "kv_b": kv_b}
        at, end = {}, 0
        for name, value in named.items():
            at[name] = end
            end += value.shape[0]
        vectors = sum(
            jnp.pad(v.astype(f32), (at[name], end - at[name] - v.shape[0])) for name, v in named.items()
        )[None]
        rows = 2 * block
        sizes = {"seq": seq, "batch": batch}
        seq_dims = [("seq", b) for b in reversed(range(bits(seq)))]
        all_dims = seq_dims + [("batch", b) for b in reversed(range(bits(batch)))]
        b_bits = [("batch", [b]) for b in range(bits(batch))]
        s_bits = [("seq", [b]) for b in range(bits(seq))]
        order_a = b_bits + s_bits
        order_b = b_bits[:1] + s_bits[:1] + b_bits[1:] + s_bits[1:]
        s_rest = [("seq", list(range(b, min(b + 2, bits(seq))))) for b in range(1, bits(seq), 2)]
        direct = [("batch", list(range(bits(batch))))] + s_bits[:1] + s_rest

        def split_rows(p):
            return p.reshape((2,) * len(all_dims) + (p.shape[0] // (seq * batch),) + p.shape[1:])

        def weights(parts, orders):
            return Reduction([split_rows(p) for p in parts], [all_dims] * len(parts), orders, sizes)

        owners = seq * batch
        fused = (width // owners) % 8 == 0 and (hidden // owners) % 8 == 0

        def fence(first, work):
            flat = [p for r in work for p in r.parts]
            first, flat = lax.optimization_barrier((first, flat))
            for r in work:
                r.parts, flat = flat[: len(r.parts)], flat[len(r.parts) :]
            return first

        def settle(value, work):
            work = [r for r in work if r.inbox]
            flat = [p for r in work for pieces in r.inbox for p in pieces]
            value, flat = lax.optimization_barrier((value, flat))
            flat = iter(flat)
            for r in work:
                r.inbox = [[next(flat) for _ in pieces] for pieces in r.inbox]
                if fused and r.whole is None:
                    r.take()
                else:
                    r.collect()
            return value

        def advance(first, work):
            work = [r for r in work if (r.left() or r.held) and not r.inbox]
            plain = [r for r in work if not fused or r.whole is not None]
            work = [r for r in work if r not in plain]
            items, kinds = [], []
            for r in work:
                for n in range(len(r.parts)):
                    ops = r.held[n] if r.held else [r.parts[n]]
                    shape = ops[0].shape
                    tail = shape[-2:]
                    if r.stages[n]:
                        axis, which, digit = r.digit(n)
                        at = min(r.dims[n].index((axis, b)) for b in which)
                        lead = (2,) * len(r.dims[n])
                        rest = math.prod(shape[:-2]) // math.prod(lead)
                        before = math.prod(lead[:at])
                        middle = 1 << len(which)
                        after = math.prod(lead[at + len(which) :]) * rest
                        items.append(([p.reshape((before, middle, after) + tail) for p in ops], digit))
                    else:
                        items.append(([p.reshape((-1,) + tail) for p in ops], None))
            if items:
                made = combine(items)
                for r in work:
                    mine, made = made[: len(r.parts)], made[len(r.parts) :]
                    r.held = None
                    if r.left():
                        r.inbox = [r.send(n, p) for n, p in enumerate(mine)]
                    r.parts = [p[0] for p in mine]
            first = fence(first, work + plain)
            for r in plain:
                if r.left():
                    r.launch()
            return first

        ha, hf, kv = norm_kv(x, vectors, at, kv_w, tables, rows, 2)
        kv = kv.reshape(seqs, block, 128)
        kv_all = lax.all_gather(kv, "seq", axis=1, tiled=True)
        q, go = query_grad_o(ha, g, q_w, vectors, at, o_w, tables, total // 2, seqs // 2)
        hf, q, go = lax.optimization_barrier((hf, q, go))
        bit = (lax.axis_index("batch") & 1).astype(jnp.int32).reshape(1)
        merged = fused and hidden // 4 == width
        act, ghf, dbu, *dff = feed_forward(hf, g, up_w, vectors, down_w, hidden // 4, total // 2, owners, merged)
        dff, kv_all = lax.optimization_barrier((dff, kv_all))
        q = q.reshape(seqs, block, width)
        go = go.reshape(seqs, block, width)

        def from_kernel(made, orders):
            if len(made) == len(orders):
                r = weights(made, orders)
                r.launch()
            else:
                r = Reduction(made[::2], [all_dims] * len(orders), orders, sizes)
                r.begin(list(zip(made[::2], made[1::2])))
            return r

        live = lengths[0]
        ffn_sum = []
        if merged:
            both = lax.psum_scatter(dff[0], ("seq", "batch"), scatter_dimension=0, tiled=True)
        else:
            ffn_sum = [weights(dff, [order_a, order_b])]
        groups = [8, seqs - 8]
        keep = ()
        first = 0
        kv_sums = []
        for count in groups:
            live = advance(live, ffn_sum + kv_sums)
            o, dq, kept, sent = attention(live, place, q, go, kv_all, tables, first, count, keep, 256)
            o = settle(o, ffn_sum + kv_sums)
            keep = (o, dq)
            first += count
            kept, sent = [p.reshape((2,) * (bits(seq) - 1) + (count, block, 128)) for p in (kept, sent)]
            kv_sums.append(Reduction([kept], [seq_dims], [s_bits], sizes))
            kv_sums[-1].begin([(kept, sent)])
        o = o.reshape(total, width)
        dq = dq.reshape(total, width)
        later = later.reshape(total, 128)

        def gradient_of(part, begin, keep):
            part = jnp.concatenate([p.reshape(-1, 128) for p in part], axis=0)
            return input_gradient(
                x, g, dq, q_w, ghf, part, later, ha, kv_w, vectors, at, tables, rows, 2, begin * block // rows, keep
            )

        def sums_of(items):
            if fused:
                return [r.parts[0] for r in items]
            return [r.run()[0] for r in items]

        def output_half(part, keep):
            return (layer_output(o, act, x, o_w, down_w, vectors, at, total // 2, part, width, keep),)

        o, vectors = advance((o, vectors), ffn_sum + kv_sums)
        early, *dproj = weight_grads(o, g, ha, dq, total // 2, bit, owners)
        early, vectors = lax.optimization_barrier((early, vectors))
        out = output_half(0, ())
        out = settle(out, ffn_sum + kv_sums)
        dproj, vectors = advance((dproj, vectors), ffn_sum + kv_sums)
        proj_sum = from_kernel(dproj, [order_a, order_b])
        out = output_half(1, tuple(out))
        (out,) = settle(out, kv_sums + [proj_sum])
        work = kv_sums + [proj_sum]
        vectors = advance(vectors, work)
        grads = gradient_of(sums_of(kv_sums[:1]), 0, ())
        grads = settle(grads, work)
        grads = advance(grads, work)
        dx, dwkv, late, sumkv = gradient_of(sums_of(kv_sums[1:]), groups[0], tuple(grads))
        vec = jnp.concatenate([early.reshape(-1), dbu.reshape(-1), late.reshape(-1), sumkv.reshape(-1)])
        vec = jnp.pad(vec, (0, -vec.shape[0] % 1024)).reshape(-1, 128)
        kvw_sum = Reduction([split_rows(dwkv)], [all_dims], [direct], sizes, whole=vec)
        late = advance(late, [kvw_sum])
        if merged:
            both = both[0].astype(f32)
            sum_up = both[:4].swapaxes(0, 1).reshape(-1, hidden)
            sum_down = both[4:].reshape(-1, width)
            late = (sum_up, sum_down)
        for _ in range(3):
            work = [proj_sum, kvw_sum]
            late = settle(late, work)
            late = advance(late, work)
        if merged:
            sum_up, sum_down = late
        if not fused:
            proj_sum.run()
            kvw_sum.run()
        if not merged:
            sum_up, sum_down = [p.reshape(p.shape[-2:]) for p in ffn_sum[0].run()]
        sum_o, sum_q = [p.reshape(p.shape[-2:]) for p in proj_sum.parts]
        sum_kv = kvw_sum.parts[0].reshape(-1, 128)
        vec = kvw_sum.whole.reshape(-1)
        ends = [width, 2 * width, 2 * width + hidden]
        ends += [ends[-1] + width * (i + 1) for i in range(4)]
        sg, sq, su, s0, s1, s2, s3 = [vec[i:j] for i, j in zip([0] + ends[:-1], ends)]
        sk = vec[ends[-1] : ends[-1] + 128]
        return (
            out.reshape(seqs, block, width), kv, dx.reshape(seqs, block, width), s0, s1, s2, s3,
            sum_q, sq, sum_kv, sk, sum_o, sg, sum_up, su, sum_down, sg,
        )

    return shards


def solution(mesh):
    rows = P("batch", "seq", None)
    split = P(("seq", "batch"), None)
    return jax.shard_map(
        make(mesh),
        mesh=mesh,
        in_specs=(rows, P("batch", None)) + (P(),) * 14 + (rows, rows),
        out_specs=(rows, rows, rows, P(), P(), P(), P(), split, P(), split, P(), split, P(), split, P(), split, P()),
        check_vma=False,
    )
```
